32 devices in a mesh: seq: 8 (over z, core), fsdp: 4 (over y, x).
Axes of the slice: x: 2, y: 2, z: 4, core: 2. Of those that a mesh axis runs over, the one named last changes fastest.
Arguments:
- tokens: bfloat16 [4, 1024, 1024], P('fsdp', 'seq'), may hold values from -6 to 6
- ln1_gain: float32 [1024], replicated, may hold values from 0.25 to 1.75
- ln1_bias: float32 [1024], replicated, may hold values from -3 to 3
- qkv_weight: bfloat16 [1024, 3072], P(('seq', 'fsdp')), may hold values from -0.1875 to 0.1875
- qkv_bias: float32 [3072], replicated, may hold values from -2.5 to 2.5
- out_weight: bfloat16 [1024, 1024], P(('seq', 'fsdp')), may hold values from -3 to 3
- ln2_gain: float32 [1024], replicated, may hold values from 0.25 to 1.75
- ln2_bias: float32 [1024], replicated, may hold values from -3 to 3
- gate_up_weight: bfloat16 [1024, 5632], P(('seq', 'fsdp')), may hold values from -0.1875 to 0.1875
- down_weight: bfloat16 [2816, 1024], P(('seq', 'fsdp')), may hold values from -0.109375 to 0.109375
- out_grad: bfloat16 [4, 1024, 1024], P('fsdp', 'seq'), may hold values from -6 to 6
Outputs:
- block_out: bfloat16 [4, 1024, 1024], P('fsdp', 'seq')
- input_grad: float32 [4, 1024, 1024], P('fsdp', 'seq')
- ln1_gain_grad: float32 [1024], replicated
- ln1_bias_grad: float32 [1024], replicated
- qkv_weight_grad: float32 [1024, 3072], P(('seq', 'fsdp'))
- qkv_bias_grad: float32 [3072], replicated
- out_weight_grad: float32 [1024, 1024], P(('seq', 'fsdp'))
- ln2_gain_grad: float32 [1024], replicated
- ln2_bias_grad: float32 [1024], replicated
- gate_up_weight_grad: float32 [1024, 5632], P(('seq', 'fsdp'))
- down_weight_grad: float32 [2816, 1024], P(('seq', 'fsdp'))
The draws below stay inside these ranges and needn't reach their ends.
All inputs are finite; a program needn't handle non-finite values.
Results may differ from the reference program's by a relative error of at most 0.011.
Values may be sent and summed in bfloat16 or wider, within the bound.
No kernel may reach another device: no remote copies, remote signals or barrier semaphores. Data moves between devices by JAX's collectives and lax.ppermute only.
A program may use at most 192 MiB of HBM per device.

```python
import jax
import jax.numpy as jnp
from jax import lax

D = 1024
H = 16
HD = 64
FF = 2816
ROT = 16
LENGTH = 1024
SEQS = 4


def block_scale(rng, dims, pieces, least, largest):
    gain, own = 1.0, jax.random.fold_in(rng, 6)
    for dim, shards_of in pieces:
        heights = jnp.exp(jax.random.uniform(jax.random.fold_in(own, dim), (shards_of,), jnp.float32, least / len(pieces), largest / len(pieces)))
        gain = gain * jnp.repeat(heights, dims[dim] // shards_of).reshape([-1 if axis == dim else 1 for axis in range(len(dims))])
    return gain


def normal_values(stream_key, shape, width, most, pieces=(), held_as=jnp.bfloat16):
    values = jax.random.normal(stream_key, shape, jnp.float32) * width
    if len(pieces) > 0:
        values = block_scale(stream_key, shape, pieces, -0.22, 0.18) * values
    return jnp.clip(values, min=-most, max=most).astype(held_as)


def setup_inputs(seed: int = 0) -> dict:
    keys = jax.random.split(jax.random.key(seed), 12)
    return {
        "tokens": normal_values(keys[0], (SEQS, LENGTH, D), 1.0, 6.0, ((0, 4), (1, 8))),
        "ln1_gain": jnp.clip(1.0 + 0.15 * jax.random.normal(keys[1], (D,), jnp.float32), 0.25, 1.75),
        "ln1_bias": normal_values(keys[2], (D,), 0.5, 3.0, (), jnp.float32),
        "qkv_weight": normal_values(keys[3], (D, 3 * D), D ** -0.5, 0.1875, ((0, 32),)),
        "qkv_bias": normal_values(keys[4], (3 * D,), 0.5, 2.5, (), jnp.float32),
        "out_weight": normal_values(keys[5], (D, D), (D // 256) ** -0.5, 3.0, ((0, 32),)),
        "ln2_gain": jnp.clip(1.0 + 0.15 * jax.random.normal(keys[6], (D,), jnp.float32), 0.25, 1.75),
        "ln2_bias": normal_values(keys[7], (D,), 0.5, 3.0, (), jnp.float32),
        "gate_up_weight": normal_values(keys[8], (D, 2 * FF), D ** -0.5, 0.1875, ((0, 32),)),
        "down_weight": normal_values(keys[9], (FF, D), FF ** -0.5, 0.109375, ((0, 32),)),
        "out_grad": normal_values(keys[10], (SEQS, LENGTH, D), 1.0, 6.0, ((0, 4), (1, 8))),
    }


EPS = 1e-05
PRECISE = lax.Precision.HIGHEST

@jax.custom_vjp
def low(v):
    return lax.optimization_barrier(v.astype(jnp.bfloat16)).astype(jnp.float32)

@jax.custom_vjp
def low_back(v):
    return v

def low_keep(v):
    return (low(v), None)

def low_pass(kept, grad):
    return (grad,)

def back_keep(v):
    return (v, None)

def back_low(kept, grad):
    return (low(grad),)
low.defvjp(low_keep, low_pass)
low_back.defvjp(back_keep, back_low)

def layer_norm(values, gain_vec, shift_vec):
    average = lax.optimization_barrier(jnp.mean(values, axis=-1, keepdims=True))
    centred = values - average
    variance = lax.optimization_barrier(jnp.mean(centred * centred, axis=-1, keepdims=True))
    return centred * lax.rsqrt(variance + EPS) * gain_vec + shift_vec

def rotate(heads_in, positions):
    half_rot = ROT // 2
    frequency = 10000.0 ** (-2.0 * jnp.arange(half_rot).astype(jnp.float32) / ROT)
    angles = positions.astype(jnp.float32)[:, None] * frequency[None, :]
    cosines = jnp.cos(angles)[:, None, :]
    sines = jnp.sin(angles)[:, None, :]
    lower_half = heads_in[..., :half_rot]
    upper_half = heads_in[..., half_rot:ROT]
    return jnp.concatenate([lower_half * cosines - upper_half * sines, upper_half * cosines + lower_half * sines, heads_in[..., ROT:]], axis=-1)

def swiglu(gate_up):
    half_width = gate_up.shape[-1] // 2
    return jax.nn.silu(gate_up[:, :half_width]) * gate_up[:, half_width:]

def attention(queries, keys_in, values_in):
    length = queries.shape[0]
    block_rows = min(512, length)
    scaling = HD ** (-0.5)
    key_index = jnp.arange(length).astype(jnp.int32)

    def one_block(args):
        query_block, first_row = args
        scores = jnp.einsum('qhd,khd->hqk', query_block, keys_in, precision=PRECISE) * scaling
        scores = low_back(scores)
        row_index = first_row + jnp.arange(block_rows).astype(jnp.int32)
        causal = row_index[:, None] >= key_index[None, :]
        scores = jnp.where(causal[None], scores, -jnp.inf)
        weights = low(jax.nn.softmax(scores, axis=-1))
        return jnp.einsum('hqk,khd->qhd', weights, values_in, precision=PRECISE)
    blocks = queries.reshape(length // block_rows, block_rows, queries.shape[1], queries.shape[2])
    starts = (jnp.arange(length // block_rows) * block_rows).astype(jnp.int32)
    result = lax.map(jax.checkpoint(one_block), (blocks, starts))
    return result.reshape(queries.shape)

def sequence_layer(seq_rows, params):
    ln1_gain, ln1_bias, qkv_weight, qkv_bias, out_weight, ln2_gain, ln2_bias, gate_up_weight, down_weight = params
    length = seq_rows.shape[0]
    hidden1 = low(layer_norm(seq_rows, ln1_gain, ln1_bias))
    projected = low_back(jnp.dot(hidden1, qkv_weight, precision=PRECISE) + qkv_bias)
    projected = projected.reshape(length, 3, H, HD)
    positions = jnp.arange(length).astype(jnp.int32)
    queries = low(rotate(projected[:, 0], positions))
    keys_in = low(rotate(projected[:, 1], positions))
    values_in = low(projected[:, 2])
    attended = attention(queries, keys_in, values_in)
    attended = low_back(low(attended)).reshape(length, D)
    middle = seq_rows + low_back(jnp.dot(attended, out_weight, precision=PRECISE))
    hidden2 = low(layer_norm(middle, ln2_gain, ln2_bias))
    gate_up = low_back(jnp.dot(hidden2, gate_up_weight, precision=PRECISE))
    activation = low(swiglu(gate_up))
    return middle + jnp.dot(activation, down_weight, precision=PRECISE)

def reference(tokens, ln1_gain, ln1_bias, qkv_weight, qkv_bias, out_weight, ln2_gain, ln2_bias, gate_up_weight, down_weight, out_grad):
    params = tuple((array.astype(jnp.float32) for array in (ln1_gain, ln1_bias, qkv_weight, qkv_bias, out_weight, ln2_gain, ln2_bias, gate_up_weight, down_weight)))
    inputs = tokens.astype(jnp.float32)

    def forward(inputs_f, params_f):
        layer = jax.checkpoint(sequence_layer)

        def step(carry, seq_rows):
            return (carry, layer(seq_rows, params_f))
        unused, outputs = lax.scan(step, jnp.zeros((), jnp.float32), inputs_f)
        return outputs
    outputs, pull = jax.vjp(forward, inputs, params)
    input_grad, grads = pull(out_grad.astype(jnp.float32))
    return (outputs.astype(jnp.bfloat16), input_grad, grads[0], grads[1], grads[2], grads[3], grads[4], grads[5], grads[6], grads[7], grads[8])
```

```python
import jax
import jax.numpy as jnp
from jax import lax
from jax.experimental import pallas as pl
from jax.experimental.pallas import tpu as pltpu
from jax.sharding import PartitionSpec as P

H = 16
HD = 64
ROT = 16
EPS = 1e-05
BF = jnp.bfloat16
F32 = jnp.float32
CORES = 2
VMEM_BYTES = 56 * 1024 * 1024


def swap_cores(value, seq):
    return lax.ppermute(value, "seq", [(i, i ^ 1) for i in range(seq)])


def line_groups(seq):
    return [[CORES * z + c for z in range(seq // CORES)] for c in range(CORES)]


def spread(value, axis, size, groups=None):
    copies = jnp.broadcast_to(value[None], (size,) + value.shape)
    return lax.all_to_all(
        copies, axis, split_axis=0, concat_axis=0, tiled=True, axis_index_groups=groups
    )


def exchange(value, axis, groups=None):
    return lax.all_to_all(
        value, axis, split_axis=0, concat_axis=0, tiled=True, axis_index_groups=groups
    )


def by_core(mine, other, core):
    first = core == 0
    return jnp.stack([jnp.where(first, mine, other), jnp.where(first, other, mine)], axis=1)


def gather_seq(value, seq, core):
    lines = seq // CORES
    mine = spread(value, "seq", lines, line_groups(seq))
    other = swap_cores(mine, seq)
    return by_core(mine, other, core).reshape((seq,) + value.shape)


def reduce_seq(parts, seq, core):
    lines = seq // CORES
    parts = parts.reshape((lines, CORES) + parts.shape[1:])
    first = core == 0
    keep = jnp.where(first, parts[:, 0], parts[:, 1])
    give = jnp.where(first, parts[:, 1], parts[:, 0]).astype(BF)
    both = (keep + swap_cores(give, seq).astype(F32)).astype(BF)
    return jnp.sum(exchange(both, "seq", line_groups(seq)).astype(F32), axis=0)


def reduce_fsdp(parts):
    return jnp.sum(exchange(parts.astype(BF), "fsdp").astype(F32), axis=0)


def sum_all(value, seq, fsdp):
    step = 1
    while step < fsdp:
        value = value + lax.ppermute(value, "fsdp", [(i, i ^ step) for i in range(fsdp)])
        step *= 2
    step = 1
    while step < seq:
        value = value + lax.ppermute(value, "seq", [(i, i ^ step) for i in range(seq)])
        step *= 2
    return value


def rotary_tables(length, width):
    half = ROT // 2
    lane = jnp.arange(width, dtype=jnp.int32) % HD
    frequency = 10000.0 ** (-2.0 * (lane % half).astype(F32) / ROT)
    angles = jnp.arange(length, dtype=jnp.int32).astype(F32)[:, None] * frequency[None, :]
    rotated = (lane < ROT)[None, :]
    sines = jnp.where((lane < half)[None, :], -jnp.sin(angles), jnp.sin(angles))
    return (jnp.where(rotated, jnp.cos(angles), 1.0), jnp.where(rotated, sines, 0.0))


def lane_roll(value, shift):
    width = value.shape[1]
    if width % 128 == 0:
        return pltpu.roll(value, shift % width, 1)
    return jnp.roll(value, shift, axis=1)


def rotate(value, cosines, sines):
    half = ROT // 2
    lane = lax.broadcasted_iota(jnp.int32, value.shape, 1) % HD
    partner = jnp.where(lane < half, lane_roll(value, -half), lane_roll(value, half))
    return value * cosines + partner * sines


def dot(left, right, left_dim, right_dim):
    return lax.dot_general(
        left, right, (((left_dim,), (right_dim,)), ((), ())), preferred_element_type=F32
    )


def head_lanes(value, head):
    lane = lax.broadcasted_iota(jnp.int32, value.shape, 1)
    return jnp.where(lane // HD == head, value, jnp.zeros_like(value))


def causal(scores, first_row):
    rows = first_row + lax.broadcasted_iota(jnp.int32, scores.shape, 0)
    cols = lax.broadcasted_iota(jnp.int32, scores.shape, 1)
    return jnp.where(rows >= cols, scores, -jnp.inf)


def forward_kernel(
    tok_ref, gain_ref, bias_ref, w_ref, qb_ref, cos_ref, sin_ref, h1_ref, q_ref, k_ref, v_ref, att_ref, lse_ref
):
    length, width = q_ref.shape
    heads = width // HD
    block = min(256, length)
    for at in range(0, length, block):
        rows = pl.ds(at, block)
        x = tok_ref[rows, :].astype(F32)
        mean = jnp.mean(x, axis=-1, keepdims=True)
        centred = x - mean
        var = jnp.mean(centred * centred, axis=-1, keepdims=True)
        h1 = (centred * lax.rsqrt(var + EPS) * gain_ref[...] + bias_ref[...]).astype(BF)
        h1_ref[rows, :] = h1
        p = dot(h1, w_ref[...], 1, 0) + qb_ref[...]
        cosines, sines = cos_ref[rows, :], sin_ref[rows, :]
        q_ref[rows, :] = rotate(p[:, :width], cosines, sines).astype(BF)
        k_ref[rows, :] = rotate(p[:, width : 2 * width], cosines, sines).astype(BF)
        v_ref[rows, :] = p[:, 2 * width :].astype(BF)
    scaling = HD ** (-0.5)
    for at in range(0, length, block):
        rows, upto = pl.ds(at, block), pl.ds(0, at + block)
        q = q_ref[rows, :]
        k = k_ref[upto, :]
        v = v_ref[upto, :]
        att = jnp.zeros((block, width), F32)
        totals = []
        for head in range(heads):
            scores = causal(dot(head_lanes(q, head), k, 1, 1) * scaling, at)
            top = jnp.max(scores, axis=-1, keepdims=True)
            exponent = jnp.exp(scores - top)
            total = jnp.sum(exponent, axis=-1, keepdims=True)
            weights = (exponent * (1.0 / total)).astype(BF)
            att = att + head_lanes(dot(weights, v, 1, 0), head)
            totals.append(jnp.broadcast_to(top + jnp.log(total), (block, HD)))
        att_ref[rows, :] = att.astype(BF)
        lse_ref[rows, :] = jnp.concatenate(totals, axis=1)


def backward_kernel(
    q_ref, k_ref, v_ref, lse_ref, do_ref, cos_ref, sin_ref, w_ref, dp_ref, dh_ref, dk_acc, dv_acc
):
    length, width = q_ref.shape
    heads = width // HD
    block = min(256, length)
    scaling = HD ** (-0.5)
    dk_acc[...] = jnp.zeros_like(dk_acc)
    dv_acc[...] = jnp.zeros_like(dv_acc)
    for at in range(0, length, block):
        rows, upto = pl.ds(at, block), pl.ds(0, at + block)
        q = q_ref[rows, :]
        do = do_ref[rows, :]
        k = k_ref[upto, :]
        v = v_ref[upto, :]
        dq = jnp.zeros((block, width), F32)
        for head in range(heads):
            qh, doh = head_lanes(q, head), head_lanes(do, head)
            lse = lse_ref[rows, head * HD : head * HD + 1]
            scores = causal(dot(qh, k, 1, 1) * scaling, at)
            probs = jnp.exp(scores - lse)
            dprobs = dot(doh, v, 1, 1)
            delta = jnp.sum(probs * dprobs, axis=-1, keepdims=True)
            dscores = (probs * (dprobs - delta)).astype(BF)
            dq = dq + head_lanes(dot(dscores, k, 1, 0), head)
            dk_acc[upto, :] += dot(dscores, qh, 0, 0)
            dv_acc[upto, :] += dot(probs.astype(BF), doh, 0, 0)
        dq = rotate(dq * scaling, cos_ref[rows, :], -sin_ref[rows, :])
        dp_ref[rows, :width] = dq.astype(BF)
    for at in range(0, length, block):
        rows = pl.ds(at, block)
        dk = rotate(dk_acc[rows, :] * scaling, cos_ref[rows, :], -sin_ref[rows, :])
        dp_ref[rows, width : 2 * width] = dk.astype(BF)
        dp_ref[rows, 2 * width :] = dv_acc[rows, :].astype(BF)
        dh_ref[rows, :] = dot(dp_ref[rows, :], w_ref[...], 1, 1)


def forward_call(tok_all, gain, bias, w, qb, cosines, sines):
    length, depth = tok_all.shape
    width = cosines.shape[1]
    shape = jax.ShapeDtypeStruct
    return pl.pallas_call(
        forward_kernel,
        out_shape=(
            shape((length, depth), BF),
            shape((length, width), BF),
            shape((length, width), BF),
            shape((length, width), BF),
            shape((length, width), BF),
            shape((length, width), F32),
        ),
        compiler_params=pltpu.CompilerParams(vmem_limit_bytes=VMEM_BYTES),
        name="attention_forward",
    )(tok_all, gain.reshape(1, -1), bias.reshape(1, -1), w, qb.reshape(1, -1), cosines, sines)


def backward_call(q, k, v, lse, do, cosines, sines, w):
    length, width = q.shape
    depth = w.shape[0]
    shape = jax.ShapeDtypeStruct
    return pl.pallas_call(
        backward_kernel,
        out_shape=(shape((length, 3 * width), BF), shape((length, depth), F32)),
        scratch_shapes=[pltpu.VMEM((length, width), F32), pltpu.VMEM((length, width), F32)],
        compiler_params=pltpu.CompilerParams(vmem_limit_bytes=VMEM_BYTES),
        name="attention_backward",
    )(q, k, v, lse, do, cosines, sines, w)


def norm_parts(values):
    mean = jnp.mean(values, axis=-1, keepdims=True)
    centred = values - mean
    inv = lax.rsqrt(jnp.mean(centred * centred, axis=-1, keepdims=True) + EPS)
    return (centred * inv, inv)


def norm_back(grad, gain, unit, inv):
    scaled = grad * gain
    return inv * (
        scaled
        - jnp.mean(scaled, axis=-1, keepdims=True)
        - unit * jnp.mean(scaled * unit, axis=-1, keepdims=True)
    )


def on_device(
    seq,
    fsdp,
    tokens,
    ln1_gain,
    ln1_bias,
    qkv_weight,
    qkv_bias,
    out_weight,
    ln2_gain,
    ln2_bias,
    gate_up_weight,
    down_weight,
    out_grad,
):
    rows, depth = tokens.shape[1], tokens.shape[2]
    length = rows * seq
    width = depth // seq
    piece = qkv_weight.shape[0]
    unit_piece = down_weight.shape[0]
    hidden = seq * unit_piece
    place = lax.axis_index("seq")
    core = place % CORES
    x_b = tokens.reshape(rows, depth)
    g_b = out_grad.reshape(rows, depth)
    x = x_b.astype(F32)

    tok_all = gather_seq(x_b, seq, core).reshape(length, depth)
    w = qkv_weight.reshape(piece, 3, seq, width).transpose(2, 0, 1, 3)
    w = exchange(w.reshape(seq, piece, 3 * width), "seq")
    w = spread(w, "fsdp", fsdp).transpose(1, 0, 2, 3).reshape(depth, 3 * width)
    qb = lax.dynamic_slice_in_dim(qkv_bias.reshape(3, seq, width), place, 1, axis=1)
    cosines, sines = rotary_tables(length, width)

    gu = gate_up_weight.reshape(piece, 2, seq, fsdp, unit_piece).transpose(3, 0, 1, 2, 4)
    gu = exchange(gu.reshape(fsdp, piece, 2 * hidden), "fsdp")
    w_out = gather_seq(out_weight, seq, core)
    w_out = spread(w_out, "fsdp", fsdp).transpose(1, 0, 2, 3).reshape(depth, depth)

    h1_all, q, k, v, att, lse = forward_call(
        tok_all, ln1_gain, ln1_bias, w, qb.reshape(3 * width), cosines, sines
    )
    att = exchange(att.reshape(seq, rows, width), "seq")
    att = att.transpose(1, 0, 2).reshape(rows, depth)

    w_gu = gather_seq(gu.reshape(fsdp * piece, 2 * hidden), seq, core).reshape(depth, 2 * hidden)
    w_down = gather_seq(down_weight, seq, core).reshape(hidden, depth)
    g_all = spread(g_b, "fsdp", fsdp).reshape(fsdp * rows, depth)

    z = x + jnp.dot(att, w_out, preferred_element_type=F32)
    u2, r2 = norm_parts(z)
    h2 = (u2 * ln2_gain + ln2_bias).astype(BF)
    h2_all = spread(h2, "fsdp", fsdp).reshape(fsdp * rows, depth)

    gate_up = jnp.dot(h2_all, w_gu, preferred_element_type=F32)
    gate, up = gate_up[:, :hidden], gate_up[:, hidden:]
    sig = jax.nn.sigmoid(gate)
    silu = gate * sig
    m = (silu * up).astype(BF)
    dm = dot(g_all, w_down, 1, 1)
    dgate = dm * up * sig * (1.0 + gate * (1.0 - sig))
    dup = dm * silu
    dgu = jnp.concatenate([dgate, dup], axis=1).astype(BF)
    dh2 = reduce_fsdp(dot(dgu, w_gu, 1, 1).reshape(fsdp, rows, depth))
    ffn = reduce_fsdp(jnp.dot(m, w_down, preferred_element_type=F32).reshape(fsdp, rows, depth))
    block_out = (z + ffn).astype(BF)

    down_grad = reduce_seq(dot(m, g_all, 0, 0).reshape(seq, unit_piece, depth), seq, core)
    gu_grad = dot(h2_all, dgu, 0, 0).reshape(seq, fsdp * piece, 2 * hidden)
    gu_grad = reduce_seq(gu_grad, seq, core).astype(BF)
    gu_grad = exchange(gu_grad.reshape(fsdp, piece, 2 * hidden), "fsdp")
    gu_grad = gu_grad.reshape(fsdp, piece, 2, seq, unit_piece).transpose(1, 2, 3, 0, 4)
    gu_grad = gu_grad.reshape(piece, 2 * seq * fsdp * unit_piece).astype(F32)

    g = g_b.astype(F32)
    dz = g + norm_back(dh2, ln2_gain, u2, r2)
    dz_b = dz.astype(BF)
    do = dot(dz_b, w_out, 1, 1).astype(BF)
    do = exchange(do.reshape(rows, seq, width).transpose(1, 0, 2), "seq").reshape(length, width)

    out_grad_w = dot(att, dz_b, 0, 0).reshape(seq, fsdp, piece, depth).transpose(1, 0, 2, 3)
    out_grad_w = reduce_seq(reduce_fsdp(out_grad_w), seq, core)

    dp, dh1 = backward_call(q, k, v, lse, do, cosines, sines, w)
    dh1 = reduce_seq(dh1.reshape(seq, rows, depth), seq, core)
    qkv_grad = dot(h1_all, dp, 0, 0).reshape(seq, fsdp, piece, 3 * width).transpose(1, 0, 2, 3)
    qkv_grad = exchange(reduce_fsdp(qkv_grad).astype(BF), "seq")
    qkv_grad = qkv_grad.reshape(seq, piece, 3, width).transpose(1, 2, 0, 3)
    qkv_grad = qkv_grad.reshape(piece, 3 * depth).astype(F32)

    u1, r1 = norm_parts(x)
    input_grad = dz + norm_back(dh1, ln1_gain, u1, r1)
    own_bias = jnp.sum(dp.astype(F32), axis=0).reshape(3, 1, width)
    bias_part = lax.dynamic_update_slice_in_dim(
        jnp.zeros((3, seq, width), F32), own_bias, place, axis=1
    )
    small = jnp.concatenate(
        [
            jnp.sum(dh1 * u1, axis=0),
            jnp.sum(dh1, axis=0),
            jnp.sum(dh2 * u2, axis=0),
            jnp.sum(dh2, axis=0),
            bias_part.reshape(3 * depth),
        ]
    )
    small = sum_all(small.reshape(-1, 128), seq, fsdp).reshape(-1)
    return (
        block_out.reshape(1, rows, depth),
        input_grad.reshape(1, rows, depth),
        small[:depth],
        small[depth : 2 * depth],
        qkv_grad,
        small[4 * depth :],
        out_grad_w,
        small[2 * depth : 3 * depth],
        small[3 * depth : 4 * depth],
        gu_grad,
        down_grad,
    )


def solution(mesh):
    seq, fsdp = mesh.shape["seq"], mesh.shape["fsdp"]
    split = P(("seq", "fsdp"), None)
    toks = P("fsdp", "seq", None)

    def step(*args):
        return on_device(seq, fsdp, *args)

    return jax.shard_map(
        step,
        mesh=mesh,
        in_specs=(toks, P(), P(), split, P(), split, P(), P(), split, split, toks),
        out_specs=(toks, toks, P(), P(), split, P(), split, P(), P(), split, split),
        check_vma=False,
    )
```

```python
import functools

import jax
import jax.numpy as jnp
from jax import lax
from jax.experimental import pallas as pl
from jax.experimental.pallas import tpu as pltpu
from jax.sharding import PartitionSpec as P

H = 16
HD = 64
ROT = 16
EPS = 1e-05
BF = jnp.bfloat16
F32 = jnp.float32
CORES = 2
LANES = 128
VMEM_BYTES = 56 * 1024 * 1024


def to_core(value, seq):
    return lax.ppermute(value, "seq", [(i, i ^ 1) for i in range(seq)])


def to_line(value, seq, step):
    chips = seq // CORES
    return lax.ppermute(
        value,
        "seq",
        [
            (CORES * z + c, CORES * ((z + step) % chips) + c)
            for z in range(chips)
            for c in range(CORES)
        ],
    )


def to_fsdp(value, fsdp, flip):
    return lax.ppermute(value, "fsdp", [(i, i ^ flip) for i in range(fsdp)])


def sum_all(value, seq, fsdp):
    step = 1
    while step < fsdp:
        value = value + to_fsdp(value, fsdp, step)
        step *= 2
    step = 1
    while step < seq:
        value = value + lax.ppermute(value, "seq", [(i, i ^ step) for i in range(seq)])
        step *= 2
    return value


def call(body, out_shape, scratch, name, *args, smem=True):
    specs = [pl.BlockSpec(memory_space=pltpu.VMEM) for _ in args]
    if smem:
        specs[0] = pl.BlockSpec(memory_space=pltpu.SMEM)
    return pl.pallas_call(
        body,
        out_shape=out_shape,
        in_specs=specs,
        scratch_shapes=scratch,
        compiler_params=pltpu.CompilerParams(vmem_limit_bytes=VMEM_BYTES),
        name=name,
    )(*args)


def shape(dims, dtype):
    return jax.ShapeDtypeStruct(dims, dtype)


def row_type(step):
    return BF if step % 16 == 0 else F32


def at_rows(start, count, step):
    return pl.ds(pl.multiple_of(start, step), count)


def dot(left, right, left_dim, right_dim):
    return lax.dot_general(
        left, right, (((left_dim,), (right_dim,)), ((), ())), preferred_element_type=F32
    )


def rotary_tables(length, width):
    half = ROT // 2
    lane = jnp.arange(width, dtype=jnp.int32) % HD
    frequency = 10000.0 ** (-2.0 * (lane % half).astype(F32) / ROT)
    angles = jnp.arange(length, dtype=jnp.int32).astype(F32)[:, None] * frequency[None, :]
    rotated = (lane < ROT)[None, :]
    sines = jnp.where((lane < half)[None, :], -jnp.sin(angles), jnp.sin(angles))
    return (jnp.where(rotated, jnp.cos(angles), 1.0), jnp.where(rotated, sines, 0.0))


def lane_roll(value, shift):
    width = value.shape[1]
    if width % LANES == 0:
        return pltpu.roll(value, shift % width, 1)
    return jnp.roll(value, shift, axis=1)


def rotate(value, cosines, sines):
    half = ROT // 2
    lane = lax.broadcasted_iota(jnp.int32, value.shape, 1) % HD
    partner = jnp.where(lane < half, lane_roll(value, -half), lane_roll(value, half))
    return value * cosines + partner * sines


def head_lanes(value, head):
    lane = lax.broadcasted_iota(jnp.int32, value.shape, 1)
    return jnp.where(lane // HD == head, value, jnp.zeros_like(value))


def causal(scores, first_row):
    rows = first_row + lax.broadcasted_iota(jnp.int32, scores.shape, 0)
    cols = lax.broadcasted_iota(jnp.int32, scores.shape, 1)
    return jnp.where(rows >= cols, scores, -jnp.inf)


def norm_parts(values):
    mean = jnp.mean(values, axis=-1, keepdims=True)
    centred = values - mean
    inv = lax.rsqrt(jnp.mean(centred * centred, axis=-1, keepdims=True) + EPS)
    return (centred * inv, inv)


def norm_back(grad, gain, unit, inv):
    scaled = grad * gain
    return inv * (
        scaled
        - jnp.mean(scaled, axis=-1, keepdims=True)
        - unit * jnp.mean(scaled * unit, axis=-1, keepdims=True)
    )


def forward_kernel(chips, fsdp, place, *refs):
    refs = list(refs)
    mine, refs = refs[:chips], refs[chips:]
    other, refs = refs[:chips], refs[chips:]
    parts, refs = refs[:fsdp], refs[fsdp:]
    gain, bias, qb, cos_ref, sin_ref, h1_ref, u1_ref, q_ref, k_ref, v_ref, lse_ref, w_ref = refs[:12]
    att_out, refs = refs[12 : 12 + chips], refs[12 + chips :]
    w_rows, att_ref = refs
    z, core, f = place[0], place[1], place[2]
    length, width = q_ref.shape
    rows = mine[0].shape[0]
    piece = parts[0].shape[2]
    seq = chips * CORES
    for j in range(fsdp):
        for k in range(chips):
            for c in range(CORES):
                src = lax.rem(z + chips - k, chips) * CORES + (core ^ c)
                at = (src * fsdp + (f ^ j)) * piece
                w_rows[at_rows(at, piece, piece), :] = parts[j][k, c].astype(w_rows.dtype)
    w_ref[...] = w_rows[...].astype(BF)
    for k in range(chips):
        for c, ref in ((0, mine[k]), (1, other[k])):
            src = lax.rem(z + chips - k, chips) * CORES + (core ^ c)
            u1, _ = norm_parts(ref[...].astype(F32))
            at = at_rows(src * rows, rows, rows)
            u1_ref[at, :] = u1.astype(BF)
            h1_ref[at, :] = (u1 * gain[...] + bias[...]).astype(BF)
    me = z * CORES + core
    biases = [qb[pl.ds(part * seq + me, 1), :] for part in range(3)]
    block = min(256, length)
    for at in range(0, length, block):
        here = pl.ds(at, block)
        p = dot(h1_ref[here, :], w_ref[...], 1, 0)
        cosines, sines = cos_ref[here, :], sin_ref[here, :]
        q_ref[here, :] = rotate(p[:, :width] + biases[0], cosines, sines).astype(BF)
        k_ref[here, :] = rotate(p[:, width : 2 * width] + biases[1], cosines, sines).astype(BF)
        v_ref[here, :] = (p[:, 2 * width :] + biases[2]).astype(BF)
    scaling = HD ** (-0.5)
    for at in range(0, length, block):
        here, upto = pl.ds(at, block), pl.ds(0, at + block)
        q, k, v = q_ref[here, :], k_ref[upto, :], v_ref[upto, :]
        att = jnp.zeros((block, width), F32)
        totals = []
        for head in range(width // HD):
            scores = causal(dot(head_lanes(q, head), k, 1, 1) * scaling, at)
            top = jnp.max(scores, axis=-1, keepdims=True)
            exponent = jnp.exp(scores - top)
            total = jnp.sum(exponent, axis=-1, keepdims=True)
            weights = (exponent * (1.0 / total)).astype(BF)
            att = att + head_lanes(dot(weights, v, 1, 0), head)
            totals.append(jnp.broadcast_to(top + jnp.log(total), (block, HD)))
        att_ref[here, :] = att.astype(BF)
        lse_ref[here, :] = jnp.concatenate(totals, axis=1)
    for k in range(chips):
        at = lax.rem(z + k, chips) * (CORES * rows)
        att_out[k][...] = att_ref[at_rows(at, CORES * rows, CORES * rows), :]


def project_kernel(chips, fsdp, place, *refs):
    refs = list(refs)
    att, refs = refs[:chips], refs[chips:]
    parts, refs = refs[:fsdp], refs[fsdp:]
    keep_ref, give_ref, w_ref, w_rows, res = refs
    core, f = place[1], place[2]
    rows = keep_ref.shape[0]
    width = att[0].shape[1]
    piece = parts[0].shape[1]
    for j in range(fsdp):
        for k in range(chips):
            at = k * width + (f ^ j) * piece
            w_rows[at_rows(at, piece, piece), :] = parts[j][k].astype(w_rows.dtype)
    w_ref[...] = w_rows[...].astype(BF)
    res[...] = dot(jnp.concatenate([a[...] for a in att], axis=1), w_ref[...], 1, 0)
    keep_ref[...] = res[at_rows(core * rows, rows, rows), :]
    give_ref[...] = res[at_rows((1 - core) * rows, rows, rows), :]


def norm2_kernel(x_ref, keep_ref, got_ref, gain, bias, z_ref, h2_ref):
    z = x_ref[...].astype(F32) + (keep_ref[...] + got_ref[...])
    z_ref[...] = z
    u2, _ = norm_parts(z)
    h2_ref[...] = (u2 * gain[...] + bias[...]).astype(BF)


def feed_kernel(chips, fsdp, hidden, unit_piece, place, *refs):
    refs = list(refs)
    h2, refs = refs[:fsdp], refs[fsdp:]
    g, refs = refs[:fsdp], refs[fsdp:]
    mine, refs = refs[:chips], refs[chips:]
    other, refs = refs[:chips], refs[chips:]
    keep_ref, refs = refs[0], refs[1:]
    sends, refs = refs[: fsdp - 1], refs[fsdp - 1 :]
    m_ref, dgu_ref, wd_ref, gu_rows, down_rows = refs
    z, core, f = place[0], place[1], place[2]
    rows, depth = keep_ref.shape
    tiles = gu_rows.shape[1] // LANES
    piece = depth // (chips * CORES * fsdp)
    unit_pad = down_pad(unit_piece)
    first = fsdp * tiles * piece
    for k in range(chips):
        for c, ref in ((0, mine[k]), (1, other[k])):
            src = lax.rem(z + chips - k, chips) * CORES + (core ^ c)
            for j in range(fsdp):
                at = at_rows((src * fsdp + (f ^ j)) * piece, piece, piece)
                for t in range(tiles):
                    tile = ref[pl.ds((j * tiles + t) * piece, piece), :]
                    gu_rows[at, t * LANES : (t + 1) * LANES] = tile.astype(gu_rows.dtype)
            for t in range(depth // LANES):
                tile = ref[pl.ds(first + t * unit_pad, unit_pad), :].astype(F32)
                at = at_rows(src * unit_pad, unit_pad, unit_pad)
                down_rows[at, t * LANES : (t + 1) * LANES] = tile
    for s in range(chips * CORES):
        wd_ref[s * unit_piece : (s + 1) * unit_piece, :] = down_rows[
            s * unit_pad : s * unit_pad + unit_piece, :
        ].astype(BF)
    w_gu = gu_rows[...].astype(BF)
    w_down = wd_ref[...]
    gu = dot(jnp.concatenate([ref[...] for ref in h2], axis=0), w_gu, 1, 0)
    gate, up = gu[:, :hidden], gu[:, hidden : 2 * hidden]
    dm = dot(jnp.concatenate([ref[...] for ref in g], axis=0), w_down, 1, 1)
    sig = 1.0 / (1.0 + jnp.exp(-gate))
    silu = gate * sig
    m_ref[...] = (silu * up).astype(BF)
    if dgu_ref.shape[1] > 2 * hidden:
        dgu_ref[...] = jnp.zeros_like(dgu_ref)
    dgu_ref[:, :hidden] = (dm * up * sig * (1.0 + gate * (1.0 - sig))).astype(BF)
    dgu_ref[:, hidden : 2 * hidden] = (dm * silu).astype(BF)
    for j in range(fsdp):
        dh2 = dot(dgu_ref[j * rows : (j + 1) * rows, :], w_gu, 1, 1)
        if j == 0:
            keep_ref[...] = dh2
        else:
            sends[j - 1][...] = dh2.astype(BF)


def down_kernel(fsdp, m_ref, wd_ref, keep_ref, *sends):
    rows = keep_ref.shape[0]
    for j in range(fsdp):
        part = dot(m_ref[j * rows : (j + 1) * rows, :], wd_ref[...], 1, 0)
        if j == 0:
            keep_ref[...] = part
        else:
            sends[j - 1][...] = part.astype(BF)


def down_pad(unit_piece):
    return -(-unit_piece // 16) * 16


def feed_grad_kernel(chips, fsdp, hidden, unit_piece, place, *refs):
    refs = list(refs)
    m_ref, dgu_ref = refs[:2]
    h2, refs = refs[2 : 2 + fsdp], refs[2 + fsdp :]
    g, refs = refs[:fsdp], refs[fsdp:]
    keep_ref, give_ref, gu_acc, down_acc = refs
    z, core = place[0], place[1]
    depth = h2[0].shape[1]
    tiles = dgu_ref.shape[1] // LANES
    block = depth // (chips * CORES)
    unit_pad = down_pad(unit_piece)
    down = dot(m_ref[...], jnp.concatenate([r[...] for r in g], axis=0), 0, 0)
    for s in range(chips * CORES):
        down_acc[s * unit_pad : s * unit_pad + unit_piece, :] = down[
            s * unit_piece : (s + 1) * unit_piece, :
        ]
        if unit_pad > unit_piece:
            down_acc[s * unit_pad + unit_piece : (s + 1) * unit_pad, :] = jnp.zeros(
                (unit_pad - unit_piece, depth), F32
            )
    gu_acc[...] = dot(jnp.concatenate([r[...] for r in h2], axis=0), dgu_ref[...], 0, 0)
    for k in range(chips):
        for c, ref in ((0, keep_ref), (1, give_ref)):
            dst = lax.rem(z + k, chips) * CORES + (core ^ c)
            rows = at_rows(dst * block, block, block)
            for t in range(tiles):
                ref[k, t * block : (t + 1) * block, :] = gu_acc[
                    rows, t * LANES : (t + 1) * LANES
                ].astype(BF)
            rows = at_rows(dst * unit_pad, unit_pad, unit_pad)
            for t in range(depth // LANES):
                at = tiles * block + t * unit_pad
                ref[k, at : at + unit_pad, :] = down_acc[
                    rows, t * LANES : (t + 1) * LANES
                ].astype(BF)


def norm2_back_kernel(count, *refs):
    keep_ref, got, refs = refs[0], refs[1 : 1 + count], refs[1 + count :]
    z_ref, g_ref, gain, dz_ref, dzb_ref, sums_ref = refs
    dh2 = keep_ref[...]
    for ref in got:
        dh2 = dh2 + ref[...].astype(F32)
    u2, r2 = norm_parts(z_ref[...])
    dz = g_ref[...].astype(F32) + norm_back(dh2, gain[...], u2, r2)
    dz_ref[...] = dz
    dzb_ref[...] = dz.astype(BF)
    sums_ref[0:1, :] = jnp.sum(dh2 * u2, axis=0, keepdims=True)
    sums_ref[1:2, :] = jnp.sum(dh2, axis=0, keepdims=True)


def project_back_kernel(chips, place, mine_ref, other_ref, w_ref, dz2_ref, *outs):
    core = place[1]
    rows = mine_ref.shape[0]
    width = outs[0].shape[1]
    dz2_ref[at_rows(core * rows, rows, rows), :] = mine_ref[...]
    dz2_ref[at_rows((1 - core) * rows, rows, rows), :] = other_ref[...]
    do = dot(dz2_ref[...], w_ref[...], 1, 1)
    for k in range(chips):
        outs[k][...] = do[:, k * width : (k + 1) * width].astype(BF)


def project_grad_kernel(chips, fsdp, place, *refs):
    att, refs = refs[:chips], refs[chips:]
    dz2_ref, refs = refs[0], refs[1:]
    outs, acc = refs[:fsdp], refs[fsdp]
    f = place[2]
    width = att[0].shape[1]
    piece = width // fsdp
    acc[...] = dot(jnp.concatenate([a[...] for a in att], axis=1), dz2_ref[...], 0, 0)
    for j in range(fsdp):
        for k in range(chips):
            at = k * width + (f ^ j) * piece
            outs[j][k] = acc[at_rows(at, piece, piece), :].astype(BF)


def backward_kernel(chips, place, *refs):
    q_ref, k_ref, v_ref, lse_ref = refs[:4]
    do_in, refs = refs[4 : 4 + chips], refs[4 + chips :]
    cos_ref, sin_ref, w_ref, dp_ref, keep_ref, give_ref, do_ref, dk_acc, dv_acc, dh_ref = refs
    z, core = place[0], place[1]
    length, width = q_ref.shape
    rows = keep_ref.shape[1]
    for k in range(chips):
        at = lax.rem(z + k, chips) * (CORES * rows)
        do_ref[at_rows(at, CORES * rows, CORES * rows), :] = do_in[k][...]
    heads = width // HD
    block = min(256, length)
    scaling = HD ** (-0.5)
    dk_acc[...] = jnp.zeros_like(dk_acc)
    dv_acc[...] = jnp.zeros_like(dv_acc)
    for at in range(0, length, block):
        here, upto = pl.ds(at, block), pl.ds(0, at + block)
        q, do, k, v = q_ref[here, :], do_ref[here, :], k_ref[upto, :], v_ref[upto, :]
        dq = jnp.zeros((block, width), F32)
        for head in range(heads):
            qh, doh = head_lanes(q, head), head_lanes(do, head)
            lse = lse_ref[here, head * HD : head * HD + 1]
            scores = causal(dot(qh, k, 1, 1) * scaling, at)
            probs = jnp.exp(scores - lse)
            dprobs = dot(doh, v, 1, 1)
            delta = jnp.sum(probs * dprobs, axis=-1, keepdims=True)
            dscores = (probs * (dprobs - delta)).astype(BF)
            dq = dq + head_lanes(dot(dscores, k, 1, 0), head)
            dk_acc[upto, :] += dot(dscores, qh, 0, 0)
            dv_acc[upto, :] += dot(probs.astype(BF), doh, 0, 0)
        dq = rotate(dq * scaling, cos_ref[here, :], -sin_ref[here, :])
        dp_ref[here, :width] = dq.astype(BF)
    for at in range(0, length, block):
        here = pl.ds(at, block)
        dk = rotate(dk_acc[here, :] * scaling, cos_ref[here, :], -sin_ref[here, :])
        dp_ref[here, width : 2 * width] = dk.astype(BF)
        dp_ref[here, 2 * width :] = dv_acc[here, :].astype(BF)
        dh_ref[here, :] = dot(dp_ref[here, :], w_ref[...], 1, 1).astype(BF)
    for k in range(chips):
        at = lax.rem(z + k, chips) * CORES
        keep_ref[k] = dh_ref[at_rows((at + core) * rows, rows, rows), :]
        give_ref[k] = dh_ref[at_rows((at + 1 - core) * rows, rows, rows), :]


def qkv_grad_kernel(chips, fsdp, place, h1_ref, u1_ref, dp_ref, w_ref, sums_ref, bias_ref, *refs):
    outs, acc = refs[:fsdp], refs[fsdp]
    f = place[2]
    piece = outs[0].shape[1]
    length = dp_ref.shape[0]
    acc[...] = dot(h1_ref[...], dp_ref[...], 0, 0)
    for j in range(fsdp):
        for s in range(chips * CORES):
            at = (s * fsdp + (f ^ j)) * piece
            outs[j][s] = acc[at_rows(at, piece, piece), :].astype(BF)
    block = min(256, length)
    gains = jnp.zeros((1, u1_ref.shape[1]), F32)
    shifts = jnp.zeros((1, u1_ref.shape[1]), F32)
    biases = jnp.zeros((1, dp_ref.shape[1]), F32)
    for at in range(0, length, block):
        here = pl.ds(at, block)
        dh1 = dot(dp_ref[here, :], w_ref[...], 1, 1)
        gains = gains + jnp.sum(dh1 * u1_ref[here, :].astype(F32), axis=0, keepdims=True)
        shifts = shifts + jnp.sum(dh1, axis=0, keepdims=True)
        biases = biases + jnp.sum(dp_ref[here, :].astype(F32), axis=0, keepdims=True)
    sums_ref[0:1, :] = gains
    sums_ref[1:2, :] = shifts
    bias_ref[...] = biases


def norm1_back_kernel(count, *refs):
    got, refs = refs[:count], refs[count:]
    x_ref, gain, dz_ref, out_ref = refs
    dh1 = got[0][...].astype(F32)
    for ref in got[1:]:
        dh1 = dh1 + ref[...].astype(F32)
    u1, r1 = norm_parts(x_ref[...].astype(F32))
    out_ref[...] = dz_ref[...] + norm_back(dh1, gain[...], u1, r1)


def on_device(
    seq,
    fsdp,
    tokens,
    ln1_gain,
    ln1_bias,
    qkv_weight,
    qkv_bias,
    out_weight,
    ln2_gain,
    ln2_bias,
    gate_up_weight,
    down_weight,
    out_grad,
):
    rows, depth = tokens.shape[1], tokens.shape[2]
    length = rows * seq
    chips = seq // CORES
    width = depth // seq
    piece = qkv_weight.shape[0]
    unit_piece = down_weight.shape[0]
    hidden = seq * unit_piece
    tiles = -(-2 * hidden // LANES)
    unit_pad = down_pad(unit_piece)
    me = lax.axis_index("seq")
    z, core, f = me // CORES, me % CORES, lax.axis_index("fsdp")
    place = jnp.stack([z, core, f]).astype(jnp.int32)
    steps, flips = range(1, chips), range(1, fsdp)
    x_b = tokens.reshape(rows, depth)
    g_b = out_grad.reshape(rows, depth)
    row = lambda v: v.reshape(1, -1)

    mine = [x_b] + [to_line(x_b, seq, k) for k in steps]
    other = [to_core(v, seq) for v in mine]

    w = qkv_weight.reshape(piece, 3, chips, CORES, width).transpose(2, 3, 0, 1, 4)
    w = w.reshape(chips, CORES, piece, 3 * width)
    w = lax.dynamic_slice_in_dim(jnp.concatenate([w, w], axis=0), z, chips, axis=0)
    keep = lax.dynamic_index_in_dim(w, core, axis=1, keepdims=False)
    give = lax.dynamic_index_in_dim(w, 1 - core, axis=1, keepdims=False)
    w = jnp.stack([keep, to_core(give, seq)], axis=1)
    w = jnp.stack([w[0]] + [to_line(w[k], seq, k) for k in steps])
    w_parts = [w] + [to_fsdp(w, fsdp, j) for j in flips]
    cosines, sines = rotary_tables(length, width)

    o = jnp.stack([out_weight] + [to_line(out_weight, seq, k) for k in steps])
    o_parts = [o] + [to_fsdp(o, fsdp, j) for j in flips]

    gu = gate_up_weight.reshape(piece, 2, seq, fsdp, unit_piece).transpose(3, 0, 1, 2, 4)
    gu = gu.reshape(fsdp, piece, 2 * hidden)
    gu = jnp.pad(gu, ((0, 0), (0, 0), (0, tiles * LANES - 2 * hidden)))
    gu = gu.reshape(fsdp, piece, tiles, LANES).transpose(0, 2, 1, 3)
    pick = lambda v, j: lax.dynamic_index_in_dim(v, f ^ j, axis=0, keepdims=False)
    gu = [pick(gu, 0)] + [to_fsdp(pick(gu, j), fsdp, j) for j in flips]
    down = jnp.pad(down_weight, ((0, unit_pad - unit_piece), (0, 0)))
    down = down.reshape(unit_pad, depth // LANES, LANES).transpose(1, 0, 2)
    feed = jnp.concatenate(
        [v.reshape(-1, LANES) for v in gu] + [down.reshape(-1, LANES)], axis=0
    )
    feed_mine = [feed] + [to_line(feed, seq, k) for k in steps]
    feed_other = [to_core(v, seq) for v in feed_mine]
    g_parts = [g_b] + [to_fsdp(g_b, fsdp, j) for j in flips]

    outs = call(
        functools.partial(forward_kernel, chips, fsdp),
        [shape((length, depth), BF)] * 2
        + [shape((length, width), BF)] * 3
        + [shape((length, width), F32), shape((depth, 3 * width), BF)]
        + [shape((CORES * rows, width), BF)] * chips,
        [pltpu.VMEM((depth, 3 * width), row_type(piece)), pltpu.VMEM((length, width), BF)],
        "attention_forward",
        place,
        *mine,
        *other,
        *w_parts,
        row(ln1_gain),
        row(ln1_bias),
        qkv_bias.reshape(3 * seq, width),
        cosines,
        sines,
    )
    h1, u1, q, k_, v, lse, w_qkv = outs[:7]
    att = outs[7:]
    att = [att[0]] + [to_line(att[k], seq, k) for k in steps]

    keep, give, w_out = call(
        functools.partial(project_kernel, chips, fsdp),
        [shape((rows, depth), F32)] * 2 + [shape((chips * width, depth), BF)],
        [
            pltpu.VMEM((chips * width, depth), row_type(piece)),
            pltpu.VMEM((CORES * rows, depth), F32),
        ],
        "out_projection",
        place,
        *att,
        *o_parts,
    )
    z_res, h2 = call(
        norm2_kernel,
        [shape((rows, depth), F32), shape((rows, depth), BF)],
        [],
        "norm2",
        x_b,
        keep,
        to_core(give, seq),
        row(ln2_gain),
        row(ln2_bias),
        smem=False,
    )
    h2_parts = [h2] + [to_fsdp(h2, fsdp, j) for j in flips]

    tokens_here = fsdp * rows
    outs = call(
        functools.partial(feed_kernel, chips, fsdp, hidden, unit_piece),
        [shape((rows, depth), F32)]
        + [shape((rows, depth), BF)] * (fsdp - 1)
        + [
            shape((tokens_here, hidden), BF),
            shape((tokens_here, tiles * LANES), BF),
            shape((hidden, depth), BF),
        ],
        [
            pltpu.VMEM((depth, tiles * LANES), row_type(piece)),
            pltpu.VMEM((seq * unit_pad, depth), F32),
        ],
        "feed_forward",
        place,
        *h2_parts,
        *g_parts,
        *feed_mine,
        *feed_other,
    )
    dh2_keep, dh2_send = outs[0], outs[1:fsdp]
    m, dgu, w_down = outs[fsdp:]
    dh2_got = [to_fsdp(v, fsdp, j) for j, v in zip(flips, dh2_send)]

    dz, dz_b, sums2 = call(
        functools.partial(norm2_back_kernel, fsdp - 1),
        [shape((rows, depth), F32), shape((rows, depth), BF), shape((2, depth), F32)],
        [],
        "norm2_back",
        dh2_keep,
        *dh2_got,
        z_res,
        g_b,
        row(ln2_gain),
        smem=False,
    )
    outs = call(
        functools.partial(project_back_kernel, chips),
        [shape((CORES * rows, depth), BF)] + [shape((CORES * rows, width), BF)] * chips,
        [],
        "out_projection_back",
        place,
        dz_b,
        to_core(dz_b, seq),
        w_out,
    )
    dz2, do = outs[0], outs[1:]
    do = [do[0]] + [to_line(do[k], seq, chips - k) for k in steps]

    outs = call(
        functools.partial(backward_kernel, chips),
        [shape((length, 3 * width), BF)] + [shape((chips, rows, depth), BF)] * 2,
        [
            pltpu.VMEM((length, width), BF),
            pltpu.VMEM((length, width), F32),
            pltpu.VMEM((length, width), F32),
            pltpu.VMEM((length, depth), BF),
        ],
        "attention_backward",
        place,
        q,
        k_,
        v,
        lse,
        *do,
        cosines,
        sines,
        w_qkv,
    )
    dp, dh_keep, dh_give = outs
    dh_both = [
        (dh_keep[k].astype(F32) + to_core(dh_give[k], seq).astype(F32)).astype(BF)
        for k in range(chips)
    ]
    dh1 = [dh_both[0]] + [to_line(dh_both[k], seq, k) for k in steps]
    input_grad = call(
        functools.partial(norm1_back_kernel, chips),
        shape((rows, depth), F32),
        [],
        "norm1_back",
        *dh1,
        x_b,
        row(ln1_gain),
        dz,
        smem=False,
    )

    outs = call(
        functools.partial(qkv_grad_kernel, chips, fsdp),
        [shape((2, depth), F32), shape((1, 3 * width), F32)]
        + [shape((seq, piece, 3 * width), BF)] * fsdp,
        [pltpu.VMEM((depth, 3 * width), F32)],
        "qkv_gradient",
        place,
        h1,
        u1,
        dp,
        w_qkv,
    )
    sums1, own_bias, blocks = outs[0], outs[1], outs[2:]
    total = blocks[0].astype(F32)
    for j in flips:
        total = total + to_fsdp(blocks[j], fsdp, j).astype(F32)
    total = total.astype(BF).reshape(chips, CORES, piece, 3 * width)
    total = lax.dynamic_slice_in_dim(jnp.concatenate([total, total], axis=0), z, chips, axis=0)
    keep = lax.dynamic_index_in_dim(total, core, axis=1, keepdims=False)
    give = lax.dynamic_index_in_dim(total, 1 - core, axis=1, keepdims=False)
    total = jnp.stack([keep, to_core(give, seq)], axis=1)
    total = jnp.stack([total[0]] + [to_line(total[k], seq, k) for k in steps])
    total = jnp.concatenate([total[:1], total[1:][::-1]], axis=0)
    total = jnp.concatenate([total, total], axis=0)
    total = lax.dynamic_slice_in_dim(total, (chips - z) % chips, chips, axis=0)
    total = jnp.where(core == 0, total, total[:, ::-1])
    total = total.reshape(seq, piece, 3, width).transpose(1, 2, 0, 3)
    qkv_grad = total.reshape(piece, 3 * depth).astype(F32)

    bias_part = lax.dynamic_update_slice_in_dim(
        jnp.zeros((3, seq, width), F32), own_bias.reshape(3, 1, width), me, axis=1
    )
    small = jnp.concatenate([sums1.reshape(-1), sums2.reshape(-1), bias_part.reshape(-1)])
    small = sum_all(small.reshape(-1, LANES), seq, fsdp).reshape(-1)

    outs = call(
        functools.partial(down_kernel, fsdp),
        [shape((rows, depth), F32)] + [shape((rows, depth), BF)] * (fsdp - 1),
        [],
        "down_projection",
        m,
        w_down,
        smem=False,
    )
    block_out = z_res + outs[0]
    for j in flips:
        block_out = block_out + to_fsdp(outs[j], fsdp, j).astype(F32)
    block_out = block_out.astype(BF)

    outs = call(
        functools.partial(project_grad_kernel, chips, fsdp),
        [shape((chips, piece, depth), BF)] * fsdp,
        [pltpu.VMEM((chips * width, depth), F32)],
        "out_projection_gradient",
        place,
        *att,
        dz2,
    )
    total = outs[0].astype(F32)
    for j in flips:
        total = total + to_fsdp(outs[j], fsdp, j).astype(F32)
    out_w_grad = total[0]
    for k in steps:
        out_w_grad = out_w_grad + to_line(total[k].astype(BF), seq, chips - k).astype(F32)

    block = depth // seq
    lines = tiles * block + (depth // LANES) * unit_pad
    keep, give = call(
        functools.partial(feed_grad_kernel, chips, fsdp, hidden, unit_piece),
        [shape((chips, lines, LANES), BF)] * 2,
        [
            pltpu.VMEM((depth, tiles * LANES), F32),
            pltpu.VMEM((seq * unit_pad, depth), F32),
        ],
        "feed_gradient",
        place,
        m,
        dgu,
        *h2_parts,
        *g_parts,
    )
    give = to_core(give, seq)
    both = [keep[k].astype(F32) + give[k].astype(F32) for k in range(chips)]
    total = both[0]
    for k in steps:
        total = total + to_line(both[k].astype(BF), seq, k).astype(F32)
    down_grad = total[tiles * block :].reshape(depth // LANES, unit_pad, LANES)
    down_grad = down_grad[:, :unit_piece].transpose(1, 0, 2).reshape(unit_piece, depth)
    gu = total[: tiles * block].astype(BF).reshape(tiles, fsdp, piece, LANES)
    gu = gu.transpose(1, 2, 0, 3).reshape(fsdp, piece, tiles * LANES)[:, :, : 2 * hidden]
    gu = [pick(gu, 0)] + [to_fsdp(pick(gu, j), fsdp, j) for j in flips]
    gu = jnp.stack(gu)
    order = jnp.arange(fsdp, dtype=jnp.int32) ^ f
    gu = jnp.take(gu, order, axis=0)
    gu = gu.reshape(fsdp, piece, 2, seq, unit_piece).transpose(1, 2, 3, 0, 4)
    gu_grad = gu.reshape(piece, 2 * seq * fsdp * unit_piece).astype(F32)

    return (
        block_out.reshape(1, rows, depth),
        input_grad.reshape(1, rows, depth),
        small[:depth],
        small[depth : 2 * depth],
        qkv_grad,
        small[4 * depth :],
        out_w_grad,
        small[2 * depth : 3 * depth],
        small[3 * depth : 4 * depth],
        gu_grad,
        down_grad,
    )


def solution(mesh):
    seq, fsdp = mesh.shape["seq"], mesh.shape["fsdp"]
    split = P(("seq", "fsdp"), None)
    toks = P("fsdp", "seq", None)

    def step(*args):
        return on_device(seq, fsdp, *args)

    return jax.shard_map(
        step,
        mesh=mesh,
        in_specs=(toks, P(), P(), split, P(), split, P(), P(), split, split, toks),
        out_specs=(toks, toks, P(), P(), split, P(), split, P(), P(), split, split),
        check_vma=False,
    )
```

```python
import functools

import jax
import jax.numpy as jnp
from jax import lax
from jax.experimental import pallas as pl
from jax.experimental.pallas import tpu as pltpu
from jax.sharding import PartitionSpec as P

H = 16
HD = 64
ROT = 16
EPS = 1e-05
BF = jnp.bfloat16
F32 = jnp.float32
CORES = 2
LANES = 128
ATT = 10_000_000_000
FILL_SHORT = 4_000_000_000
FILL_LONG = 8_000_000_000
FILL_LAST = 10_000_000_000
LONG = 50_000_000_000
VMEM_BYTES = 56 * 1024 * 1024


def to_core(value, seq):
    return lax.ppermute(value, "seq", [(i, i ^ 1) for i in range(seq)])


def to_line(value, seq, step):
    return lax.ppermute(value, "seq", [(i, i ^ (CORES * step)) for i in range(seq)])


def to_fsdp(value, fsdp, flip):
    return lax.ppermute(value, "fsdp", [(i, i ^ flip) for i in range(fsdp)])


def after(values, *earlier):
    flat, tree = jax.tree.flatten(values)
    held = lax.optimization_barrier((flat, earlier))[0]
    return jax.tree.unflatten(tree, held)


def call(body, out_shape, scratch, name, *args, smem=True, flops=1_000_000_000):
    specs = [pl.BlockSpec(memory_space=pltpu.VMEM) for _ in args]
    if smem:
        specs[0] = pl.BlockSpec(memory_space=pltpu.SMEM)
    return pl.pallas_call(
        body,
        out_shape=out_shape,
        in_specs=specs,
        scratch_shapes=scratch,
        compiler_params=pltpu.CompilerParams(vmem_limit_bytes=VMEM_BYTES),
        cost_estimate=pl.CostEstimate(flops=flops, transcendentals=0, bytes_accessed=1000000),
        name=name,
    )(*args)


def shape(dims, dtype):
    return jax.ShapeDtypeStruct(dims, dtype)


def row_type(step):
    return BF if step % 16 == 0 else F32


def at_rows(start, count, step):
    return pl.ds(pl.multiple_of(start, step), count)


def dot(left, right, left_dim, right_dim):
    return lax.dot_general(
        left, right, (((left_dim,), (right_dim,)), ((), ())), preferred_element_type=F32
    )


def rotary_tables(length, width):
    half = ROT // 2
    lane = jnp.arange(width, dtype=jnp.int32) % HD
    frequency = 10000.0 ** (-2.0 * (lane % half).astype(F32) / ROT)
    angles = jnp.arange(length, dtype=jnp.int32).astype(F32)[:, None] * frequency[None, :]
    rotated = (lane < ROT)[None, :]
    sines = jnp.where((lane < half)[None, :], -jnp.sin(angles), jnp.sin(angles))
    return (jnp.where(rotated, jnp.cos(angles), 1.0), jnp.where(rotated, sines, 0.0))


def lane_roll(value, shift):
    width = value.shape[1]
    if width % LANES == 0:
        return pltpu.roll(value, shift % width, 1)
    return jnp.roll(value, shift, axis=1)


def rotate(value, cosines, sines):
    half = ROT // 2
    lane = lax.broadcasted_iota(jnp.int32, value.shape, 1) % HD
    partner = jnp.where(lane < half, lane_roll(value, -half), lane_roll(value, half))
    return value * cosines + partner * sines


def head_lanes(value, head):
    lane = lax.broadcasted_iota(jnp.int32, value.shape, 1)
    return jnp.where(lane // HD == head, value, jnp.zeros_like(value))


def causal(scores, first_row):
    rows = first_row + lax.broadcasted_iota(jnp.int32, scores.shape, 0)
    cols = lax.broadcasted_iota(jnp.int32, scores.shape, 1)
    return jnp.where(rows >= cols, scores, -jnp.inf)


def norm_parts(values):
    mean = jnp.mean(values, axis=-1, keepdims=True)
    centred = values - mean
    inv = lax.rsqrt(jnp.mean(centred * centred, axis=-1, keepdims=True) + EPS)
    return (centred * inv, inv)


def norm_back(grad, gain, unit, inv):
    scaled = grad * gain
    return inv * (
        scaled
        - jnp.mean(scaled, axis=-1, keepdims=True)
        - unit * jnp.mean(scaled * unit, axis=-1, keepdims=True)
    )


def inputs_kernel(chips, fsdp, place, *refs):
    refs = list(refs)
    tok_ref, parts, refs = refs[0], refs[1 : 1 + fsdp], refs[1 + fsdp :]
    gain, bias, qb, cos_ref, sin_ref, h1_ref, u1_ref, q_ref, k_ref, v_ref, w_ref, w_rows = refs
    z, core, f = place[0], place[1], place[2]
    length, width = q_ref.shape
    rows = tok_ref.shape[1]
    piece = parts[0].shape[2]
    seq = chips * CORES
    for j in range(fsdp):
        for k in range(chips):
            for c in range(CORES):
                at = (((z ^ k) * CORES + (core ^ c)) * fsdp + (f ^ j)) * piece
                w_rows[at_rows(at, piece, piece), :] = parts[j][c, k].astype(w_rows.dtype)
    w_ref[...] = w_rows[...].astype(BF)
    for s in range(seq):
        u1, _ = norm_parts(tok_ref[s].astype(F32))
        here = pl.ds(s * rows, rows)
        u1_ref[here, :] = u1.astype(BF)
        h1_ref[here, :] = (u1 * gain[...] + bias[...]).astype(BF)
    me = z * CORES + core
    biases = [qb[pl.ds(part * seq + me, 1), :] for part in range(3)]
    block = min(256, length)
    for at in range(0, length, block):
        here = pl.ds(at, block)
        p = dot(h1_ref[here, :], w_ref[...], 1, 0)
        cosines, sines = cos_ref[here, :], sin_ref[here, :]
        q_ref[here, :] = rotate(p[:, :width] + biases[0], cosines, sines).astype(BF)
        k_ref[here, :] = rotate(p[:, width : 2 * width] + biases[1], cosines, sines).astype(BF)
        v_ref[here, :] = (p[:, 2 * width :] + biases[2]).astype(BF)


def attend_kernel(chips, place, q_ref, k_ref, v_ref, lse_ref, *refs):
    att_out, att_ref = refs[:chips], refs[chips]
    z = place[0]
    length, width = q_ref.shape
    rows = length // (chips * CORES)
    block = min(256, length)
    scaling = HD ** (-0.5)
    for at in range(0, length, block):
        here, upto = pl.ds(at, block), pl.ds(0, at + block)
        q, k, v = q_ref[here, :], k_ref[upto, :], v_ref[upto, :]
        att = jnp.zeros((block, width), F32)
        totals = []
        for head in range(width // HD):
            scores = causal(dot(head_lanes(q, head), k, 1, 1) * scaling, at)
            top = jnp.max(scores, axis=-1, keepdims=True)
            exponent = jnp.exp(scores - top)
            total = jnp.sum(exponent, axis=-1, keepdims=True)
            weights = (exponent * (1.0 / total)).astype(BF)
            att = att + head_lanes(dot(weights, v, 1, 0), head)
            totals.append(jnp.broadcast_to(top + jnp.log(total), (block, HD)))
        att_ref[here, :] = att.astype(BF)
        lse_ref[here, :] = jnp.concatenate(totals, axis=1)
    for k in range(chips):
        at = (z ^ k) * (CORES * rows)
        att_out[k][...] = att_ref[at_rows(at, CORES * rows, CORES * rows), :]


def project_kernel(chips, fsdp, place, *refs):
    refs = list(refs)
    att, refs = refs[:chips], refs[chips:]
    parts, refs = refs[:fsdp], refs[fsdp:]
    keep_ref, give_ref, w_ref, w_rows, res = refs
    core, f = place[1], place[2]
    rows = keep_ref.shape[0]
    width = att[0].shape[1]
    piece = parts[0].shape[1]
    for j in range(fsdp):
        for k in range(chips):
            at = k * width + (f ^ j) * piece
            w_rows[at_rows(at, piece, piece), :] = parts[j][k].astype(w_rows.dtype)
    w_ref[...] = w_rows[...].astype(BF)
    res[...] = dot(jnp.concatenate([a[...] for a in att], axis=1), w_ref[...], 1, 0)
    keep_ref[...] = res[at_rows(core * rows, rows, rows), :]
    give_ref[...] = res[at_rows((1 - core) * rows, rows, rows), :]


def norm2_kernel(x_ref, keep_ref, got_ref, gain, bias, z_ref, h2_ref):
    z = x_ref[...].astype(F32) + (keep_ref[...] + got_ref[...])
    z_ref[...] = z
    u2, _ = norm_parts(z)
    h2_ref[...] = (u2 * gain[...] + bias[...]).astype(BF)


def feed_kernel(seq, fsdp, hidden, unit_piece, place, *refs):
    refs = list(refs)
    h2, refs = refs[:fsdp], refs[fsdp:]
    g, refs = refs[:fsdp], refs[fsdp:]
    feed_ref, keep_ref, refs = refs[0], refs[1], refs[2:]
    sends, refs = refs[: fsdp - 1], refs[fsdp - 1 :]
    m_ref, dgu_ref, wd_ref, g_all, gu_rows, down_rows = refs
    f = place[2]
    rows, depth = keep_ref.shape
    tiles = gu_rows.shape[1] // LANES
    piece = depth // (seq * fsdp)
    unit_pad = down_pad(unit_piece)
    first = fsdp * tiles * piece
    for s in range(seq):
        for j in range(fsdp):
            at = at_rows((s * fsdp + (f ^ j)) * piece, piece, piece)
            for t in range(tiles):
                tile = feed_ref[s, pl.ds((j * tiles + t) * piece, piece), :]
                gu_rows[at, t * LANES : (t + 1) * LANES] = tile.astype(gu_rows.dtype)
        for t in range(depth // LANES):
            down_rows[s * unit_pad : (s + 1) * unit_pad, t * LANES : (t + 1) * LANES] = feed_ref[
                s, pl.ds(first + t * unit_pad, unit_pad), :
            ].astype(F32)
    for j in range(fsdp):
        g_all[j * rows : (j + 1) * rows, :] = g[j][...]
    for s in range(seq):
        wd_ref[s * unit_piece : (s + 1) * unit_piece, :] = down_rows[
            s * unit_pad : s * unit_pad + unit_piece, :
        ].astype(BF)
    w_gu = gu_rows[...].astype(BF)
    w_down = wd_ref[...]
    gu = dot(jnp.concatenate([ref[...] for ref in h2], axis=0), w_gu, 1, 0)
    gate, up = gu[:, :hidden], gu[:, hidden : 2 * hidden]
    dm = dot(g_all[...], w_down, 1, 1)
    sig = 1.0 / (1.0 + jnp.exp(-gate))
    silu = gate * sig
    m_ref[...] = (silu * up).astype(BF)
    if dgu_ref.shape[1] > 2 * hidden:
        dgu_ref[...] = jnp.zeros_like(dgu_ref)
    dgu_ref[:, :hidden] = (dm * up * sig * (1.0 + gate * (1.0 - sig))).astype(BF)
    dgu_ref[:, hidden : 2 * hidden] = (dm * silu).astype(BF)
    for j in range(fsdp):
        dh2 = dot(dgu_ref[j * rows : (j + 1) * rows, :], w_gu, 1, 1)
        if j == 0:
            keep_ref[...] = dh2
        else:
            sends[j - 1][...] = dh2.astype(BF)


def down_kernel(fsdp, m_ref, wd_ref, keep_ref, *sends):
    rows = keep_ref.shape[0]
    for j in range(fsdp):
        part = dot(m_ref[j * rows : (j + 1) * rows, :], wd_ref[...], 1, 0)
        if j == 0:
            keep_ref[...] = part
        else:
            sends[j - 1][...] = part.astype(BF)


def down_pad(unit_piece):
    return -(-unit_piece // 16) * 16


def feed_grad_kernel(seq, fsdp, hidden, unit_piece, place, *refs):
    m_ref, dgu_ref, g_all = refs[:3]
    h2, refs = refs[3 : 3 + fsdp], refs[3 + fsdp :]
    out_ref, gu_acc, down_acc = refs
    depth = h2[0].shape[1]
    tiles = dgu_ref.shape[1] // LANES
    block = depth // seq
    unit_pad = down_pad(unit_piece)
    down_acc[...] = dot(m_ref[...], g_all[...], 0, 0)
    gu_acc[...] = dot(jnp.concatenate([r[...] for r in h2], axis=0), dgu_ref[...], 0, 0)
    for s in range(seq):
        for t in range(tiles):
            out_ref[s, t * block : (t + 1) * block, :] = gu_acc[
                s * block : (s + 1) * block, t * LANES : (t + 1) * LANES
            ].astype(BF)
        for t in range(depth // LANES):
            down = down_acc[
                s * unit_piece : (s + 1) * unit_piece, t * LANES : (t + 1) * LANES
            ].astype(BF)
            if unit_pad > unit_piece:
                down = jnp.concatenate(
                    [down, jnp.zeros((unit_pad - unit_piece, LANES), BF)], axis=0
                )
            at = tiles * block + t * unit_pad
            out_ref[s, at : at + unit_pad, :] = down


def norm2_back_kernel(count, *refs):
    keep_ref, got, refs = refs[0], refs[1 : 1 + count], refs[1 + count :]
    z_ref, g_ref, gain, dz_ref, dzb_ref, sums_ref = refs
    dh2 = keep_ref[...]
    for ref in got:
        dh2 = dh2 + ref[...].astype(F32)
    u2, r2 = norm_parts(z_ref[...])
    dz = g_ref[...].astype(F32) + norm_back(dh2, gain[...], u2, r2)
    dz_ref[...] = dz
    dzb_ref[...] = dz.astype(BF)
    sums_ref[0:1, :] = jnp.sum(dh2 * u2, axis=0, keepdims=True)
    sums_ref[1:2, :] = jnp.sum(dh2, axis=0, keepdims=True)


def project_back_kernel(chips, place, mine_ref, other_ref, w_ref, dz2_ref, *outs):
    core = place[1]
    rows = mine_ref.shape[0]
    width = outs[0].shape[1]
    dz2_ref[at_rows(core * rows, rows, rows), :] = mine_ref[...]
    dz2_ref[at_rows((1 - core) * rows, rows, rows), :] = other_ref[...]
    do = dot(dz2_ref[...], w_ref[...], 1, 1)
    for k in range(chips):
        outs[k][...] = do[:, k * width : (k + 1) * width].astype(BF)


def project_grad_kernel(chips, fsdp, place, *refs):
    att, refs = refs[:chips], refs[chips:]
    dz2_ref, refs = refs[0], refs[1:]
    outs, acc = refs[:fsdp], refs[fsdp]
    f = place[2]
    width = att[0].shape[1]
    piece = width // fsdp
    acc[...] = dot(jnp.concatenate([a[...] for a in att], axis=1), dz2_ref[...], 0, 0)
    for j in range(fsdp):
        for k in range(chips):
            at = k * width + (f ^ j) * piece
            outs[j][k] = acc[at_rows(at, piece, piece), :].astype(BF)


def backward_kernel(chips, place, *refs):
    q_ref, k_ref, v_ref, lse_ref = refs[:4]
    do_in, refs = refs[4 : 4 + chips], refs[4 + chips :]
    cos_ref, sin_ref, w_ref, dp_ref, give_ref, refs = *refs[:5], refs[5:]
    keep, refs = refs[:chips], refs[chips:]
    do_ref, dk_acc, dv_acc, dh_ref = refs
    z, core = place[0], place[1]
    length, width = q_ref.shape
    rows = give_ref.shape[1]
    for k in range(chips):
        at = (z ^ k) * (CORES * rows)
        do_ref[at_rows(at, CORES * rows, CORES * rows), :] = do_in[k][...]
    heads = width // HD
    block = min(256, length)
    scaling = HD ** (-0.5)
    dk_acc[...] = jnp.zeros_like(dk_acc)
    dv_acc[...] = jnp.zeros_like(dv_acc)
    for at in range(0, length, block):
        here, upto = pl.ds(at, block), pl.ds(0, at + block)
        q, do, k, v = q_ref[here, :], do_ref[here, :], k_ref[upto, :], v_ref[upto, :]
        dq = jnp.zeros((block, width), F32)
        for head in range(heads):
            qh, doh = head_lanes(q, head), head_lanes(do, head)
            lse = lse_ref[here, head * HD : head * HD + 1]
            scores = causal(dot(qh, k, 1, 1) * scaling, at)
            probs = jnp.exp(scores - lse)
            dprobs = dot(doh, v, 1, 1)
            delta = jnp.sum(probs * dprobs, axis=-1, keepdims=True)
            dscores = (probs * (dprobs - delta)).astype(BF)
            dq = dq + head_lanes(dot(dscores, k, 1, 0), head)
            dk_acc[upto, :] += dot(dscores, qh, 0, 0)
            dv_acc[upto, :] += dot(probs.astype(BF), doh, 0, 0)
        dq = rotate(dq * scaling, cos_ref[here, :], -sin_ref[here, :])
        dp_ref[here, :width] = dq.astype(BF)
    for at in range(0, length, block):
        here = pl.ds(at, block)
        dk = rotate(dk_acc[here, :] * scaling, cos_ref[here, :], -sin_ref[here, :])
        dp_ref[here, width : 2 * width] = dk.astype(BF)
        dp_ref[here, 2 * width :] = dv_acc[here, :].astype(BF)
        dh_ref[here, :] = dot(dp_ref[here, :], w_ref[...], 1, 1).astype(BF)
    for k in range(chips):
        at = (z ^ k) * CORES
        keep[k][...] = dh_ref[at_rows((at + core) * rows, rows, rows), :]
        give_ref[k] = dh_ref[at_rows((at + 1 - core) * rows, rows, rows), :]


def add_kernel(count, got_ref, *refs):
    for k in range(count):
        refs[count + k][...] = (refs[k][...].astype(F32) + got_ref[k].astype(F32)).astype(BF)


def small_rows(depth, lanes):
    return -(-depth // lanes), -(-(4 * -(-depth // lanes) + 1) // 16) * 16


def tree_sum(values):
    values = list(values)
    while len(values) > 1:
        values = [values[i] + values[i + 1] for i in range(0, len(values), 2)]
    return values[0]


def qkv_grad_kernel(chips, fsdp, place, h1_ref, u1_ref, dp_ref, w_ref, sums2_ref, *refs):
    outs, acc = refs[:fsdp], refs[fsdp]
    f = place[2]
    seq = chips * CORES
    depth, lanes = acc.shape
    piece = depth // (seq * fsdp)
    length = dp_ref.shape[0]
    acc[...] = dot(h1_ref[...], dp_ref[...], 0, 0)
    block = min(256, length)
    gains = jnp.zeros((1, depth), F32)
    shifts = jnp.zeros((1, depth), F32)
    biases = jnp.zeros((1, lanes), F32)
    for at in range(0, length, block):
        here = pl.ds(at, block)
        dh1 = dot(dp_ref[here, :], w_ref[...], 1, 1)
        gains = gains + jnp.sum(dh1 * u1_ref[here, :].astype(F32), axis=0, keepdims=True)
        shifts = shifts + jnp.sum(dh1, axis=0, keepdims=True)
        biases = biases + jnp.sum(dp_ref[here, :].astype(F32), axis=0, keepdims=True)
    per, count = small_rows(depth, lanes)
    small = []
    for v in (gains, shifts, sums2_ref[0:1, :], sums2_ref[1:2, :]):
        if per * lanes > depth:
            v = jnp.concatenate([v, jnp.zeros((1, per * lanes - depth), F32)], axis=1)
        small += [v[:, r * lanes : (r + 1) * lanes] for r in range(per)]
    small.append(biases)
    if count > len(small):
        small.append(jnp.zeros((count - len(small), lanes), F32))
    small = jnp.concatenate(small, axis=0)
    for j in range(fsdp):
        for s in range(seq):
            at = (s * fsdp + (f ^ j)) * piece
            outs[j][s * piece : (s + 1) * piece, :] = acc[at_rows(at, piece, piece), :].astype(BF)
        outs[j][seq * piece :, :] = small.astype(BF)


def qkv_line_kernel(chips, fsdp, place, *refs):
    got, refs = refs[:fsdp], refs[fsdp:]
    outs, acc = refs[:chips], refs[chips]
    z, core = place[0], place[1]
    count = outs[0].shape[0]
    total_rows = got[0].shape[0]
    small = total_rows - acc.shape[0]
    piece = acc.shape[0] // (chips * CORES)
    total = tree_sum([ref[...].astype(F32) for ref in got])
    acc[...] = total[: total_rows - small, :]
    for k in range(chips):
        for c in range(CORES):
            at = ((z ^ k) * CORES + (core ^ c)) * piece
            outs[k][c * piece : (c + 1) * piece, :] = acc[at_rows(at, piece, piece), :].astype(BF)
        outs[k][CORES * piece : count, :] = total[total_rows - small :, :].astype(BF)


def qkv_core_kernel(chips, piece, per, *refs):
    got, (keep_ref, give_ref) = refs[:chips], refs[chips:]
    lanes = keep_ref.shape[1]
    small = [ref[CORES * piece :, :].astype(F32) for ref in got]
    total = tree_sum(small)
    bias = [v[4 * per : 4 * per + 1, :] for v in small]
    rest = keep_ref.shape[0] - chips * piece - 4 * per - chips
    pad = [jnp.zeros((rest, lanes), F32)] if rest > 0 else []
    tail = jnp.concatenate([total[: 4 * per, :]] + bias + pad, axis=0)
    for c, ref in ((0, keep_ref), (1, give_ref)):
        for k in range(chips):
            ref[k * piece : (k + 1) * piece, :] = got[k][c * piece : (c + 1) * piece, :]
        ref[chips * piece :, :] = tail.astype(BF)


def qkv_final_kernel(chips, piece, per, place, keep_ref, got_ref, grad_ref, small_ref, bias_ref, acc):
    z, core = place[0], place[1]
    seq = chips * CORES
    lanes = keep_ref.shape[1]
    width = lanes // 3
    depth = small_ref.shape[1]
    at = chips * piece
    tails = [ref[at:, :].astype(F32) for ref in (keep_ref, got_ref)]
    total = tails[0] + tails[1]
    for c, ref in ((0, keep_ref), (1, got_ref)):
        for k in range(chips):
            src = (z ^ k) * CORES + (core ^ c)
            rows = ref[k * piece : (k + 1) * piece, :].astype(F32)
            bias = tails[c][4 * per + k : 4 * per + k + 1, :]
            for part in range(3):
                acc[part * seq + src] = rows[:, part * width : (part + 1) * width]
                bias_ref[pl.ds(part * seq + src, 1), :] = bias[:, part * width : (part + 1) * width]
    for i in range(3 * seq):
        grad_ref[:, i * width : (i + 1) * width] = acc[i]
    for v in range(4):
        for r in range(per):
            upto = min(lanes, depth - r * lanes)
            small_ref[v : v + 1, r * lanes : r * lanes + upto] = total[v * per + r : v * per + r + 1, :upto]


def norm1_back_kernel(count, *refs):
    got, refs = refs[:count], refs[count:]
    x_ref, gain, dz_ref, out_ref = refs
    dh1 = got[0][...].astype(F32)
    for ref in got[1:]:
        dh1 = dh1 + ref[...].astype(F32)
    u1, r1 = norm_parts(x_ref[...].astype(F32))
    out_ref[...] = dz_ref[...] + norm_back(dh1, gain[...], u1, r1)


def on_device(
    seq,
    fsdp,
    tokens,
    ln1_gain,
    ln1_bias,
    qkv_weight,
    qkv_bias,
    out_weight,
    ln2_gain,
    ln2_bias,
    gate_up_weight,
    down_weight,
    out_grad,
):
    rows, depth = tokens.shape[1], tokens.shape[2]
    length = rows * seq
    chips = seq // CORES
    width = depth // seq
    piece = qkv_weight.shape[0]
    unit_piece = down_weight.shape[0]
    hidden = seq * unit_piece
    tiles = -(-2 * hidden // LANES)
    unit_pad = down_pad(unit_piece)
    me = lax.axis_index("seq")
    z, core, f = me // CORES, me % CORES, lax.axis_index("fsdp")
    place = jnp.stack([z, core, f]).astype(jnp.int32)
    steps, flips = range(1, chips), range(1, fsdp)
    by_place = jnp.arange(seq, dtype=jnp.int32) ^ me
    x_b = tokens.reshape(rows, depth)
    g_b = out_grad.reshape(rows, depth)
    row = lambda v: v.reshape(1, -1)

    tok_all = lax.all_gather(x_b, "seq", axis=0)

    w = qkv_weight.reshape(piece, 3, seq, width).transpose(2, 0, 1, 3)
    w = jnp.take(w.reshape(seq, piece, 3 * width), by_place, axis=0)
    w = w.reshape(chips, CORES, piece, 3 * width)
    w = [w[0]] + [to_line(w[k], seq, k) for k in steps]
    w = [jnp.stack([v[c] for v in w]) for c in range(CORES)]
    cosines, sines = rotary_tables(length, width)
    w = jnp.stack([w[0], to_core(after(w[1], cosines, sines), seq)])
    w_parts = [w] + [to_fsdp(w, fsdp, j) for j in flips]

    o = jnp.stack([out_weight] + [to_line(out_weight, seq, k) for k in steps])
    o_parts = [o] + [to_fsdp(o, fsdp, j) for j in flips]

    gu = gate_up_weight.reshape(piece, 2, seq, fsdp, unit_piece).transpose(3, 0, 1, 2, 4)
    gu = gu.reshape(fsdp, piece, 2 * hidden)
    gu = jnp.pad(gu, ((0, 0), (0, 0), (0, tiles * LANES - 2 * hidden)))
    gu = gu.reshape(fsdp, piece, tiles, LANES).transpose(0, 2, 1, 3)
    pick = lambda v, j: lax.dynamic_index_in_dim(v, f ^ j, axis=0, keepdims=False)
    gu = after(gu, w)
    gu = [pick(gu, 0)] + [to_fsdp(pick(gu, j), fsdp, j) for j in flips]
    g_late = after(g_b, o)
    g_parts = [g_b] + [to_fsdp(g_late, fsdp, j) for j in flips]
    down = jnp.pad(down_weight, ((0, unit_pad - unit_piece), (0, 0)))
    down = down.reshape(unit_pad, depth // LANES, LANES).transpose(1, 0, 2)
    feed = jnp.concatenate(
        [v.reshape(-1, LANES) for v in gu] + [down.reshape(-1, LANES)], axis=0
    )
    feed = lax.all_gather(feed, "seq", axis=0)

    outs = call(
        functools.partial(inputs_kernel, chips, fsdp),
        [shape((length, depth), BF)] * 2
        + [shape((length, width), BF)] * 3
        + [shape((depth, 3 * width), BF)],
        [pltpu.VMEM((depth, 3 * width), row_type(piece))],
        "attention_inputs",
        place,
        tok_all,
        *w_parts,
        row(ln1_gain),
        row(ln1_bias),
        qkv_bias.reshape(3 * seq, width),
        cosines,
        sines,
    )
    h1, u1, q, k_, v, w_qkv = outs
    outs = call(
        functools.partial(attend_kernel, chips),
        [shape((length, width), F32)] + [shape((CORES * rows, width), BF)] * chips,
        [pltpu.VMEM((length, width), BF)],
        "attention_forward",
        place,
        q,
        k_,
        v,
        flops=ATT,
    )
    lse, att = outs[0], outs[1:]
    att = [att[0]] + [to_line(att[k], seq, k) for k in steps]

    keep, give, w_out = call(
        functools.partial(project_kernel, chips, fsdp),
        [shape((rows, depth), F32)] * 2 + [shape((chips * width, depth), BF)],
        [
            pltpu.VMEM((chips * width, depth), row_type(piece)),
            pltpu.VMEM((CORES * rows, depth), F32),
        ],
        "out_projection",
        place,
        *att,
        *o_parts,
    )
    z_res, h2 = call(
        norm2_kernel,
        [shape((rows, depth), F32), shape((rows, depth), BF)],
        [],
        "norm2",
        x_b,
        keep,
        to_core(give, seq),
        row(ln2_gain),
        row(ln2_bias),
        smem=False,
    )
    h2_parts = [h2] + [to_fsdp(h2, fsdp, j) for j in flips]

    tokens_here = fsdp * rows
    outs = call(
        functools.partial(feed_kernel, seq, fsdp, hidden, unit_piece),
        [shape((rows, depth), F32)]
        + [shape((rows, depth), BF)] * (fsdp - 1)
        + [
            shape((tokens_here, hidden), BF),
            shape((tokens_here, tiles * LANES), BF),
            shape((hidden, depth), BF),
            shape((tokens_here, depth), BF),
        ],
        [
            pltpu.VMEM((depth, tiles * LANES), row_type(piece)),
            pltpu.VMEM((seq * unit_pad, depth), F32),
        ],
        "feed_forward",
        place,
        *h2_parts,
        *g_parts,
        feed,
    )
    dh2_keep, dh2_send = outs[0], outs[1:fsdp]
    m, dgu, w_down, g_all = outs[fsdp:]
    dh2_got = [to_fsdp(v, fsdp, j) for j, v in zip(flips, dh2_send)]

    block = depth // seq
    lines = tiles * block + (depth // LANES) * unit_pad
    feed_grad = call(
        functools.partial(feed_grad_kernel, seq, fsdp, hidden, unit_piece),
        shape((seq, lines, LANES), BF),
        [
            pltpu.VMEM((depth, tiles * LANES), F32),
            pltpu.VMEM((hidden, depth), F32),
        ],
        "feed_gradient",
        place,
        m,
        dgu,
        g_all,
        *h2_parts,
        flops=FILL_LONG,
    )
    feed_total = lax.psum_scatter(feed_grad, "seq", scatter_dimension=0).astype(F32)

    ffn = call(
        functools.partial(down_kernel, fsdp),
        [shape((rows, depth), F32)] + [shape((rows, depth), BF)] * (fsdp - 1),
        [],
        "down_projection",
        m,
        w_down,
        smem=False,
        flops=FILL_SHORT,
    )
    dh2_got = after(dh2_got, feed_grad, ffn[0])

    dz, dz_b, sums2 = call(
        functools.partial(norm2_back_kernel, fsdp - 1),
        [shape((rows, depth), F32), shape((rows, depth), BF), shape((2, depth), F32)],
        [],
        "norm2_back",
        dh2_keep,
        *dh2_got,
        z_res,
        g_b,
        row(ln2_gain),
        smem=False,
    )
    outs = call(
        functools.partial(project_back_kernel, chips),
        [shape((CORES * rows, depth), BF)] + [shape((CORES * rows, width), BF)] * chips,
        [],
        "out_projection_back",
        place,
        dz_b,
        to_core(dz_b, seq),
        w_out,
    )
    dz2, do = outs[0], outs[1:]
    do = [do[0]] + [to_line(do[k], seq, k) for k in steps]

    block_out = z_res + ffn[0]
    for j in flips:
        block_out = block_out + to_fsdp(ffn[j], fsdp, j).astype(F32)
    block_out = block_out.astype(BF)

    outs = call(
        functools.partial(project_grad_kernel, chips, fsdp),
        [shape((chips, piece, depth), BF)] * fsdp,
        [pltpu.VMEM((chips * width, depth), F32)],
        "out_projection_gradient",
        place,
        *att,
        dz2,
    )
    o_blocks = [outs[0]] + [to_fsdp(outs[j], fsdp, j) for j in flips]
    do = after(do, outs[0])

    outs = call(
        functools.partial(backward_kernel, chips),
        [shape((length, 3 * width), BF), shape((chips, rows, depth), BF)]
        + [shape((rows, depth), BF)] * chips,
        [
            pltpu.VMEM((length, width), BF),
            pltpu.VMEM((length, width), F32),
            pltpu.VMEM((length, width), F32),
            pltpu.VMEM((length, depth), BF),
        ],
        "attention_backward",
        place,
        q,
        k_,
        v,
        lse,
        *do,
        cosines,
        sines,
        w_qkv,
        flops=LONG,
    )
    dp, dh_give, dh_keep = outs[0], outs[1], outs[2:]
    lanes = 3 * width
    per, count = small_rows(depth, lanes)
    blocks = call(
        functools.partial(qkv_grad_kernel, chips, fsdp),
        [shape((seq * piece + count, lanes), BF)] * fsdp,
        [pltpu.VMEM((depth, lanes), F32)],
        "qkv_gradient",
        place,
        h1,
        u1,
        dp,
        w_qkv,
        sums2,
        flops=FILL_LAST,
    )
    dh_got = after(to_core(dh_give, seq), blocks[0], o_blocks)
    dh_both = call(
        functools.partial(add_kernel, chips),
        [shape((rows, depth), BF)] * chips,
        [],
        "input_gradient_cores",
        dh_got,
        *dh_keep,
        smem=False,
    )
    dh1 = [dh_both[0]] + [to_line(dh_both[k], seq, k) for k in steps]
    blocks = [blocks[0]] + [to_fsdp(blocks[j], fsdp, j) for j in flips]
    blocks = call(
        functools.partial(qkv_line_kernel, chips, fsdp),
        [shape((CORES * piece + count, lanes), BF)] * chips,
        [pltpu.VMEM((seq * piece, lanes), F32)],
        "qkv_gradient_line",
        place,
        *blocks,
    )
    blocks = [blocks[0]] + [to_line(blocks[k], seq, k) for k in steps]
    tail = -(-(4 * per + chips) // 16) * 16
    keep, give = call(
        functools.partial(qkv_core_kernel, chips, piece, per),
        [shape((chips * piece + tail, lanes), BF)] * 2,
        [],
        "qkv_gradient_core",
        *blocks,
        smem=False,
    )
    qkv_grad, small, bias_grad = call(
        functools.partial(qkv_final_kernel, chips, piece, per),
        [
            shape((piece, 3 * depth), F32),
            shape((4, depth), F32),
            shape((3 * seq, width), F32),
        ],
        [pltpu.VMEM((3 * seq, piece, width), F32)],
        "qkv_gradient_final",
        place,
        keep,
        to_core(give, seq),
    )
    input_grad = call(
        functools.partial(norm1_back_kernel, chips),
        shape((rows, depth), F32),
        [],
        "norm1_back",
        *dh1,
        x_b,
        row(ln1_gain),
        dz,
        smem=False,
    )

    down_grad = feed_total[tiles * block :].reshape(depth // LANES, unit_pad, LANES)
    down_grad = down_grad[:, :unit_piece].transpose(1, 0, 2).reshape(unit_piece, depth)
    gu = feed_total[: tiles * block].astype(BF).reshape(tiles, fsdp, piece, LANES)
    gu = gu.transpose(1, 2, 0, 3).reshape(fsdp, piece, tiles * LANES)[:, :, : 2 * hidden]
    gu_got = [pick(gu, 0)] + [to_fsdp(pick(gu, j), fsdp, j) for j in flips]
    gu = jnp.stack(gu_got)
    order = jnp.arange(fsdp, dtype=jnp.int32) ^ f
    gu = jnp.take(gu, order, axis=0)
    gu = gu.reshape(fsdp, piece, 2, seq, unit_piece).transpose(1, 2, 3, 0, 4)
    gu_grad = gu.reshape(piece, 2 * seq * fsdp * unit_piece).astype(F32)


    total = o_blocks[0].astype(F32)
    for j in flips:
        total = total + o_blocks[j].astype(F32)
    total = after(total, blocks[0])
    out_w_grad = total[0]
    for k in steps:
        out_w_grad = out_w_grad + to_line(total[k].astype(BF), seq, k).astype(F32)

    return (
        block_out.reshape(1, rows, depth),
        input_grad.reshape(1, rows, depth),
        small[0],
        small[1],
        qkv_grad,
        bias_grad.reshape(3 * depth),
        out_w_grad,
        small[2],
        small[3],
        gu_grad,
        down_grad,
    )


def solution(mesh):
    seq, fsdp = mesh.shape["seq"], mesh.shape["fsdp"]
    split = P(("seq", "fsdp"), None)
    toks = P("fsdp", "seq", None)

    def step(*args):
        return on_device(seq, fsdp, *args)

    return jax.shard_map(
        step,
        mesh=mesh,
        in_specs=(toks, P(), P(), split, P(), split, P(), P(), split, split, toks),
        out_specs=(toks, toks, P(), P(), split, P(), split, P(), P(), split, split),
        check_vma=False,
    )
```

```python
import functools

import jax
import jax.numpy as jnp
from jax import lax
from jax.experimental import pallas as pl
from jax.experimental.pallas import tpu as pltpu
from jax.sharding import PartitionSpec as P

H = 16
HD = 64
ROT = 16
EPS = 1e-05
BF = jnp.bfloat16
F32 = jnp.float32
CORES = 2
LANES = 128
ATT = 10_000_000_000
FILL_SHORT = 4_000_000_000
FILL_LONG = 8_000_000_000
FILL_LAST = 10_000_000_000
PROJECT = 20_000_000_000
LONG = 78_000_000_000
MIB = 1024 * 1024


def to_core(value, seq):
    return lax.ppermute(value, "seq", [(i, i ^ 1) for i in range(seq)])


def to_line(value, seq, step):
    return lax.ppermute(value, "seq", [(i, i ^ (CORES * step)) for i in range(seq)])


def to_fsdp(value, fsdp, flip):
    return lax.ppermute(value, "fsdp", [(i, i ^ flip) for i in range(fsdp)])


def after(values, *earlier):
    flat, tree = jax.tree.flatten(values)
    held = lax.optimization_barrier((flat, earlier))[0]
    return jax.tree.unflatten(tree, held)


def call(body, out_shape, scratch, name, *args, smem=True, flops=1_000_000_000, vmem=12):
    specs = [pl.BlockSpec(memory_space=pltpu.VMEM) for _ in args]
    if smem:
        specs[0] = pl.BlockSpec(memory_space=pltpu.SMEM)
    return pl.pallas_call(
        body,
        out_shape=out_shape,
        in_specs=specs,
        scratch_shapes=scratch,
        compiler_params=pltpu.CompilerParams(vmem_limit_bytes=vmem * MIB),
        cost_estimate=pl.CostEstimate(flops=flops, transcendentals=0, bytes_accessed=1000000),
        name=name,
    )(*args)


def gate_kernel(*refs):
    pltpu.touch(refs[-1])


def gate(value, *earlier):
    whole = pl.BlockSpec(memory_space=pl.ANY)
    return pl.pallas_call(
        gate_kernel,
        out_shape=shape(value.shape, value.dtype),
        in_specs=[whole] * (1 + len(earlier)),
        out_specs=whole,
        input_output_aliases={0: 0},
        cost_estimate=pl.CostEstimate(flops=1000, transcendentals=0, bytes_accessed=1000),
        name="gate",
    )(value, *earlier)


def shape(dims, dtype):
    return jax.ShapeDtypeStruct(dims, dtype)


def row_type(step):
    return BF if step % 16 == 0 else F32


def at_rows(start, count, step):
    return pl.ds(pl.multiple_of(start, step), count)


def dot(left, right, left_dim, right_dim):
    return lax.dot_general(
        left, right, (((left_dim,), (right_dim,)), ((), ())), preferred_element_type=F32
    )


def rotary_tables(length, width):
    half = ROT // 2
    lane = jnp.arange(width, dtype=jnp.int32) % HD
    frequency = 10000.0 ** (-2.0 * (lane % half).astype(F32) / ROT)
    angles = jnp.arange(length, dtype=jnp.int32).astype(F32)[:, None] * frequency[None, :]
    rotated = (lane < ROT)[None, :]
    sines = jnp.where((lane < half)[None, :], -jnp.sin(angles), jnp.sin(angles))
    return (jnp.where(rotated, jnp.cos(angles), 1.0), jnp.where(rotated, sines, 0.0))


def lane_roll(value, shift):
    width = value.shape[1]
    if width % LANES == 0:
        return pltpu.roll(value, shift % width, 1)
    return jnp.roll(value, shift, axis=1)


def rotate(value, cosines, sines):
    half = ROT // 2
    lane = lax.broadcasted_iota(jnp.int32, value.shape, 1) % HD
    partner = jnp.where(lane < half, lane_roll(value, -half), lane_roll(value, half))
    return value * cosines + partner * sines


def head_lanes(value, head):
    lane = lax.broadcasted_iota(jnp.int32, value.shape, 1)
    return jnp.where(lane // HD == head, value, jnp.zeros_like(value))


def causal(scores, first_row):
    rows = first_row + lax.broadcasted_iota(jnp.int32, scores.shape, 0)
    cols = lax.broadcasted_iota(jnp.int32, scores.shape, 1)
    return jnp.where(rows >= cols, scores, -jnp.inf)


def norm_parts(values):
    mean = jnp.mean(values, axis=-1, keepdims=True)
    centred = values - mean
    inv = lax.rsqrt(jnp.mean(centred * centred, axis=-1, keepdims=True) + EPS)
    return (centred * inv, inv)


def norm_back(grad, gain, unit, inv):
    scaled = grad * gain
    return inv * (
        scaled
        - jnp.mean(scaled, axis=-1, keepdims=True)
        - unit * jnp.mean(scaled * unit, axis=-1, keepdims=True)
    )


def inputs_kernel(chips, fsdp, place, *refs):
    refs = list(refs)
    tok_ref, parts, refs = refs[0], refs[1 : 1 + fsdp], refs[1 + fsdp :]
    gain, bias, qb, cos_ref, sin_ref, h1_ref, u1_ref, q_ref, k_ref, v_ref, w_ref, w_rows = refs
    z, core, f = place[0], place[1], place[2]
    length, width = q_ref.shape
    rows = tok_ref.shape[1]
    piece = parts[0].shape[3]
    seq = chips * CORES
    for j in range(fsdp):
        for k in range(chips):
            for c in range(CORES):
                at = (((z ^ k) * CORES + (core ^ c)) * fsdp + (f ^ j)) * piece
                for t in range(3):
                    w_rows[at_rows(at, piece, piece), t * width : (t + 1) * width] = parts[j][
                        c, k, t
                    ].astype(w_rows.dtype)
    w_ref[...] = w_rows[...].astype(BF)

    def norm(s, carry):
        u1, _ = norm_parts(tok_ref[s].astype(F32))
        here = at_rows(s * rows, rows, rows)
        u1_ref[here, :] = u1.astype(BF)
        h1_ref[here, :] = (u1 * gain[...] + bias[...]).astype(BF)
        return carry

    lax.fori_loop(0, seq, norm, 0)
    me = z * CORES + core
    biases = [qb[pl.ds(part * seq + me, 1), :] for part in range(3)]
    block = min(256, length)

    def project(i, carry):
        here = at_rows(i * block, block, block)
        p = dot(h1_ref[here, :], w_ref[...], 1, 0)
        cosines, sines = cos_ref[here, :], sin_ref[here, :]
        q_ref[here, :] = rotate(p[:, :width] + biases[0], cosines, sines).astype(BF)
        k_ref[here, :] = rotate(p[:, width : 2 * width] + biases[1], cosines, sines).astype(BF)
        v_ref[here, :] = (p[:, 2 * width :] + biases[2]).astype(BF)
        return carry

    lax.fori_loop(0, length // block, project, 0)


def attend_kernel(chips, place, q_ref, k_ref, v_ref, lse_ref, *refs):
    att_out, att_ref = refs[:chips], refs[chips]
    z = place[0]
    length, width = q_ref.shape
    rows = length // (chips * CORES)
    block = min(256, length)
    scaling = HD ** (-0.5)
    for at in range(0, length, block):
        here, upto = pl.ds(at, block), pl.ds(0, at + block)
        q, k, v = q_ref[here, :], k_ref[upto, :], v_ref[upto, :]
        att = jnp.zeros((block, width), F32)
        totals = []
        for head in range(width // HD):
            scores = causal(dot(head_lanes(q, head), k, 1, 1) * scaling, at)
            top = jnp.max(scores, axis=-1, keepdims=True)
            exponent = jnp.exp(scores - top)
            total = jnp.sum(exponent, axis=-1, keepdims=True)
            weights = (exponent * (1.0 / total)).astype(BF)
            att = att + head_lanes(dot(weights, v, 1, 0), head)
            totals.append(jnp.broadcast_to(top + jnp.log(total), (block, HD)))
        att_ref[here, :] = att.astype(BF)
        lse_ref[here, :] = jnp.concatenate(totals, axis=1)
    for k in range(chips):
        at = (z ^ k) * (CORES * rows)
        att_out[k][...] = att_ref[at_rows(at, CORES * rows, CORES * rows), :]


def project_kernel(chips, fsdp, place, *refs):
    refs = list(refs)
    att, refs = refs[:chips], refs[chips:]
    parts, refs = refs[:fsdp], refs[fsdp:]
    keep_ref, give_ref, w_ref, w_rows, res = refs
    core, f = place[1], place[2]
    rows = keep_ref.shape[0]
    width = att[0].shape[1]
    piece = parts[0].shape[2]
    for j in range(fsdp):
        for k in range(chips):
            at = k * width + (f ^ j) * piece
            for t in range(parts[j].shape[1]):
                w_rows[at_rows(at, piece, piece), t * width : (t + 1) * width] = parts[j][
                    k, t
                ].astype(w_rows.dtype)
    w_ref[...] = w_rows[...].astype(BF)
    res[...] = dot(jnp.concatenate([a[...] for a in att], axis=1), w_ref[...], 1, 0)
    keep_ref[...] = res[at_rows(core * rows, rows, rows), :]
    give_ref[...] = res[at_rows((1 - core) * rows, rows, rows), :]


def norm2_kernel(x_ref, keep_ref, got_ref, gain, bias, z_ref, h2_ref):
    z = x_ref[...].astype(F32) + (keep_ref[...] + got_ref[...])
    z_ref[...] = z
    u2, _ = norm_parts(z)
    h2_ref[...] = (u2 * gain[...] + bias[...]).astype(BF)


def feed_kernel(seq, fsdp, hidden, unit_piece, place, *refs):
    refs = list(refs)
    h2, refs = refs[:fsdp], refs[fsdp:]
    g, refs = refs[:fsdp], refs[fsdp:]
    feed_ref, keep_ref, refs = refs[0], refs[1], refs[2:]
    sends, refs = refs[: fsdp - 1], refs[fsdp - 1 :]
    m_ref, dgu_ref, wd_ref, h2_all, g_all, gu_rows, down_rows, w_gu = refs
    f = place[2]
    rows, depth = keep_ref.shape
    tiles = gu_rows.shape[1] // LANES
    piece = depth // (seq * fsdp)
    unit_pad = down_pad(unit_piece)
    first = fsdp * tiles * piece

    def gather(s, carry):
        for j in range(fsdp):
            at = at_rows((s * fsdp + (f ^ j)) * piece, piece, piece)
            for t in range(tiles):
                tile = feed_ref[s, pl.ds((j * tiles + t) * piece, piece), :]
                gu_rows[at, t * LANES : (t + 1) * LANES] = tile.astype(gu_rows.dtype)
        return carry

    def gather_down(s, at):
        for t in range(depth // LANES):
            tile = feed_ref[s, pl.ds(first + t * unit_pad, unit_pad), :].astype(F32)
            down_rows[at, t * LANES : (t + 1) * LANES] = tile[:unit_piece, :]

    lax.fori_loop(0, seq, gather, 0)
    if unit_piece % 8 == 0:

        def gather_units(s, carry):
            gather_down(s, at_rows(s * unit_piece, unit_piece, 8))
            return carry

        lax.fori_loop(0, seq, gather_units, 0)
    else:
        for s in range(seq):
            gather_down(s, pl.ds(s * unit_piece, unit_piece))
    wd_ref[...] = down_rows[...].astype(BF)
    w_gu[...] = gu_rows[...].astype(BF)
    for j in range(fsdp):
        h2_all[j * rows : (j + 1) * rows, :] = h2[j][...]
        g_all[j * rows : (j + 1) * rows, :] = g[j][...]
    if dgu_ref.shape[1] > 2 * hidden:
        dgu_ref[...] = jnp.zeros_like(dgu_ref)
    chunks = 2

    def work(i, carry):
        here = at_rows(i * (chunks * rows), chunks * rows, chunks * rows)
        gu = dot(h2_all[here, :], w_gu[...], 1, 0)
        gate, up = gu[:, :hidden], gu[:, hidden : 2 * hidden]
        dm = dot(g_all[here, :], wd_ref[...], 1, 1)
        sig = 1.0 / (1.0 + jnp.exp(-gate))
        silu = gate * sig
        m_ref[here, :] = (silu * up).astype(BF)
        dgu_ref[here, :hidden] = (dm * up * sig * (1.0 + gate * (1.0 - sig))).astype(BF)
        dgu_ref[here, hidden : 2 * hidden] = (dm * silu).astype(BF)
        dh2 = dot(dgu_ref[here, :], w_gu[...], 1, 1)
        for j in range(fsdp):

            @pl.when(i == j // chunks)
            def _():
                part = dh2[(j % chunks) * rows : (j % chunks + 1) * rows, :]
                if j == 0:
                    keep_ref[...] = part
                else:
                    sends[j - 1][...] = part.astype(BF)

        return carry

    lax.fori_loop(0, fsdp // chunks, work, 0)


def down_kernel(fsdp, m_ref, wd_ref, keep_ref, *sends):
    rows = keep_ref.shape[0]
    for j in range(fsdp):
        part = dot(m_ref[j * rows : (j + 1) * rows, :], wd_ref[...], 1, 0)
        if j == 0:
            keep_ref[...] = part
        else:
            sends[j - 1][...] = part.astype(BF)


def down_pad(unit_piece):
    return -(-unit_piece // 16) * 16


def feed_grad_kernel(seq, hidden, unit_piece, m_ref, dgu_ref, g_all, h2_all, out_ref, gu_acc, down_acc):
    depth = g_all.shape[1]
    tiles = dgu_ref.shape[1] // LANES
    block = depth // seq
    unit_pad = down_pad(unit_piece)
    pair = max(1, 256 // block)

    def gate_up(i, carry):
        cols = pl.ds(pl.multiple_of(i * (pair * block), pair * block), pair * block)
        gu_acc[...] = dot(h2_all[:, cols], dgu_ref[...], 0, 0).astype(BF)
        for s in range(pair):
            for t in range(tiles):
                out_ref[i * pair + s, t * block : (t + 1) * block, :] = gu_acc[
                    s * block : (s + 1) * block, t * LANES : (t + 1) * LANES
                ]
        return carry

    lax.fori_loop(0, seq // pair, gate_up, 0)

    def down(i, carry):
        cols = pl.ds(pl.multiple_of(i * 256, 256), 256)
        down_acc[...] = dot(m_ref[...], g_all[:, cols], 0, 0)
        for s in range(seq):
            for t in range(2):
                tile = down_acc[
                    s * unit_piece : (s + 1) * unit_piece, t * LANES : (t + 1) * LANES
                ].astype(BF)
                if unit_pad > unit_piece:
                    tile = jnp.concatenate(
                        [tile, jnp.zeros((unit_pad - unit_piece, LANES), BF)], axis=0
                    )
                at = tiles * block + (i * 2 + t) * unit_pad
                out_ref[s, at_rows(at, unit_pad, 16), :] = tile
        return carry

    lax.fori_loop(0, depth // 256, down, 0)


def norm2_back_kernel(count, *refs):
    keep_ref, got, refs = refs[0], refs[1 : 1 + count], refs[1 + count :]
    z_ref, g_ref, gain, dz_ref, dzb_ref, sums_ref = refs
    dh2 = keep_ref[...]
    for ref in got:
        dh2 = dh2 + ref[...].astype(F32)
    u2, r2 = norm_parts(z_ref[...])
    dz = g_ref[...].astype(F32) + norm_back(dh2, gain[...], u2, r2)
    dz_ref[...] = dz
    dzb_ref[...] = dz.astype(BF)
    sums_ref[0:1, :] = jnp.sum(dh2 * u2, axis=0, keepdims=True)
    sums_ref[1:2, :] = jnp.sum(dh2, axis=0, keepdims=True)


def project_back_kernel(chips, place, mine_ref, other_ref, w_ref, dz2_ref, *outs):
    core = place[1]
    rows = mine_ref.shape[0]
    width = outs[0].shape[1]
    dz2_ref[at_rows(core * rows, rows, rows), :] = mine_ref[...]
    dz2_ref[at_rows((1 - core) * rows, rows, rows), :] = other_ref[...]
    do = dot(dz2_ref[...], w_ref[...], 1, 1)
    for k in range(chips):
        outs[k][...] = do[:, k * width : (k + 1) * width].astype(BF)


def project_grad_kernel(chips, fsdp, place, *refs):
    att, refs = refs[:chips], refs[chips:]
    dz2_ref, refs = refs[0], refs[1:]
    outs, acc = refs[:fsdp], refs[fsdp]
    f = place[2]
    width = att[0].shape[1]
    piece = width // fsdp
    acc[...] = dot(jnp.concatenate([a[...] for a in att], axis=1), dz2_ref[...], 0, 0)
    for j in range(fsdp):
        for k in range(chips):
            at = k * width + (f ^ j) * piece
            outs[j][k] = acc[at_rows(at, piece, piece), :].astype(BF)


def backward_kernel(chips, place, *refs):
    q_ref, k_ref, v_ref, lse_ref = refs[:4]
    do_in, refs = refs[4 : 4 + chips], refs[4 + chips :]
    cos_ref, sin_ref, w_ref, dp_ref, dh_ref, do_ref, dk_acc, dv_acc = refs
    z = place[0]
    length, width = q_ref.shape
    rows = length // (chips * CORES)
    for k in range(chips):
        at = (z ^ k) * (CORES * rows)
        do_ref[at_rows(at, CORES * rows, CORES * rows), :] = do_in[k][...]
    heads = width // HD
    block = min(256, length)
    scaling = HD ** (-0.5)
    dk_acc[...] = jnp.zeros_like(dk_acc)
    dv_acc[...] = jnp.zeros_like(dv_acc)
    for at in range(0, length, block):
        here, upto = pl.ds(at, block), pl.ds(0, at + block)
        q, do, k, v = q_ref[here, :], do_ref[here, :], k_ref[upto, :], v_ref[upto, :]
        dq = jnp.zeros((block, width), F32)
        for head in range(heads):
            qh, doh = head_lanes(q, head), head_lanes(do, head)
            lse = lse_ref[here, head * HD : head * HD + 1]
            scores = causal(dot(qh, k, 1, 1) * scaling, at)
            probs = jnp.exp(scores - lse)
            dprobs = dot(doh, v, 1, 1)
            delta = jnp.sum(probs * dprobs, axis=-1, keepdims=True)
            dscores = (probs * (dprobs - delta)).astype(BF)
            dq = dq + head_lanes(dot(dscores, k, 1, 0), head)
            dk_acc[upto, :] += dot(dscores, qh, 0, 0)
            dv_acc[upto, :] += dot(probs.astype(BF), doh, 0, 0)
        dq = rotate(dq * scaling, cos_ref[here, :], -sin_ref[here, :])
        dp_ref[here, :width] = dq.astype(BF)

    def finish(i, carry):
        here = at_rows(i * block, block, block)
        dk = rotate(dk_acc[here, :] * scaling, cos_ref[here, :], -sin_ref[here, :])
        dp_ref[here, width : 2 * width] = dk.astype(BF)
        dp_ref[here, 2 * width :] = dv_acc[here, :].astype(BF)
        dh_ref[here, :] = dot(dp_ref[here, :], w_ref[...], 1, 1).astype(BF)
        return carry

    lax.fori_loop(0, length // block, finish, 0)


def small_rows(depth, lanes):
    return -(-depth // lanes), -(-(4 * -(-depth // lanes) + 1) // 16) * 16


def tree_sum(values):
    values = list(values)
    while len(values) > 1:
        values = [values[i] + values[i + 1] for i in range(0, len(values), 2)]
    return values[0]


def qkv_grad_kernel(chips, fsdp, place, h1_ref, u1_ref, dp_ref, w_ref, sums2_ref, *refs):
    outs, acc = refs[:fsdp], refs[fsdp]
    f = place[2]
    seq = chips * CORES
    depth, lanes = acc.shape
    piece = depth // (seq * fsdp)
    length = dp_ref.shape[0]
    acc[...] = dot(h1_ref[...], dp_ref[...], 0, 0)
    block = min(256, length)

    def sums(i, carry):
        gains, shifts, biases = carry
        here = at_rows(i * block, block, block)
        dh1 = dot(dp_ref[here, :], w_ref[...], 1, 1)
        gains = gains + jnp.sum(dh1 * u1_ref[here, :].astype(F32), axis=0, keepdims=True)
        shifts = shifts + jnp.sum(dh1, axis=0, keepdims=True)
        biases = biases + jnp.sum(dp_ref[here, :].astype(F32), axis=0, keepdims=True)
        return (gains, shifts, biases)

    zeros = jnp.zeros((1, depth), F32)
    gains, shifts, biases = lax.fori_loop(
        0, length // block, sums, (zeros, zeros, jnp.zeros((1, lanes), F32))
    )
    per, count = small_rows(depth, lanes)
    small = []
    for v in (gains, shifts, sums2_ref[0:1, :], sums2_ref[1:2, :]):
        if per * lanes > depth:
            v = jnp.concatenate([v, jnp.zeros((1, per * lanes - depth), F32)], axis=1)
        small += [v[:, r * lanes : (r + 1) * lanes] for r in range(per)]
    small.append(biases)
    if count > len(small):
        small.append(jnp.zeros((count - len(small), lanes), F32))
    small = jnp.concatenate(small, axis=0)
    for j in range(fsdp):
        for s in range(seq):
            at = (s * fsdp + (f ^ j)) * piece
            outs[j][s * piece : (s + 1) * piece, :] = acc[at_rows(at, piece, piece), :].astype(BF)
        outs[j][seq * piece :, :] = small.astype(BF)


def qkv_line_kernel(chips, fsdp, place, *refs):
    got, refs = refs[:fsdp], refs[fsdp:]
    outs, acc = refs[:chips], refs[chips]
    z, core = place[0], place[1]
    count = outs[0].shape[0]
    total_rows = got[0].shape[0]
    small = total_rows - acc.shape[0]
    piece = acc.shape[0] // (chips * CORES)
    total = tree_sum([ref[...].astype(F32) for ref in got])
    acc[...] = total[: total_rows - small, :]
    for k in range(chips):
        for c in range(CORES):
            at = ((z ^ k) * CORES + (core ^ c)) * piece
            outs[k][c * piece : (c + 1) * piece, :] = acc[at_rows(at, piece, piece), :].astype(BF)
        outs[k][CORES * piece : count, :] = total[total_rows - small :, :].astype(BF)


def qkv_core_kernel(chips, piece, per, *refs):
    got, (keep_ref, give_ref) = refs[:chips], refs[chips:]
    lanes = keep_ref.shape[1]
    small = [ref[CORES * piece :, :].astype(F32) for ref in got]
    total = tree_sum(small)
    bias = [v[4 * per : 4 * per + 1, :] for v in small]
    rest = keep_ref.shape[0] - chips * piece - 4 * per - chips
    pad = [jnp.zeros((rest, lanes), F32)] if rest > 0 else []
    tail = jnp.concatenate([total[: 4 * per, :]] + bias + pad, axis=0)
    for c, ref in ((0, keep_ref), (1, give_ref)):
        for k in range(chips):
            ref[k * piece : (k + 1) * piece, :] = got[k][c * piece : (c + 1) * piece, :]
        ref[chips * piece :, :] = tail.astype(BF)


def qkv_final_kernel(chips, piece, per, place, keep_ref, got_ref, grad_ref, small_ref, bias_ref, acc):
    z, core = place[0], place[1]
    seq = chips * CORES
    lanes = keep_ref.shape[1]
    width = lanes // 3
    depth = small_ref.shape[1]
    at = chips * piece
    tails = [ref[at:, :].astype(F32) for ref in (keep_ref, got_ref)]
    total = tails[0] + tails[1]
    for c, ref in ((0, keep_ref), (1, got_ref)):
        for k in range(chips):
            src = (z ^ k) * CORES + (core ^ c)
            rows = ref[k * piece : (k + 1) * piece, :].astype(F32)
            bias = tails[c][4 * per + k : 4 * per + k + 1, :]
            for part in range(3):
                acc[part * seq + src] = rows[:, part * width : (part + 1) * width]
                bias_ref[pl.ds(part * seq + src, 1), :] = bias[:, part * width : (part + 1) * width]
    for i in range(3 * seq):
        grad_ref[:, i * width : (i + 1) * width] = acc[i]
    for v in range(4):
        for r in range(per):
            upto = min(lanes, depth - r * lanes)
            small_ref[v : v + 1, r * lanes : r * lanes + upto] = total[v * per + r : v * per + r + 1, :upto]


def norm1_back_kernel(dh1_ref, x_ref, gain, dz_ref, out_ref):
    u1, r1 = norm_parts(x_ref[...].astype(F32))
    out_ref[...] = dz_ref[...] + norm_back(dh1_ref[...].astype(F32), gain[...], u1, r1)


def on_device(
    seq,
    fsdp,
    tokens,
    ln1_gain,
    ln1_bias,
    qkv_weight,
    qkv_bias,
    out_weight,
    ln2_gain,
    ln2_bias,
    gate_up_weight,
    down_weight,
    out_grad,
):
    rows, depth = tokens.shape[1], tokens.shape[2]
    length = rows * seq
    chips = seq // CORES
    width = depth // seq
    piece = qkv_weight.shape[0]
    unit_piece = down_weight.shape[0]
    hidden = seq * unit_piece
    tiles = -(-2 * hidden // LANES)
    unit_pad = down_pad(unit_piece)
    me = lax.axis_index("seq")
    z, core, f = me // CORES, me % CORES, lax.axis_index("fsdp")
    place = jnp.stack([z, core, f]).astype(jnp.int32)
    steps, flips = range(1, chips), range(1, fsdp)
    by_place = jnp.arange(seq, dtype=jnp.int32) ^ me
    x_b = tokens.reshape(rows, depth)
    g_b = out_grad.reshape(rows, depth)
    row = lambda v: v.reshape(1, -1)

    tok_all = lax.all_gather(x_b, "seq", axis=0)

    w = qkv_weight.reshape(piece, 3, seq, width).transpose(2, 1, 0, 3)
    w = jnp.take(w, by_place, axis=0).reshape(chips, CORES * 3, piece, width)
    w = [w[0]] + [to_line(w[k], seq, k) for k in steps]
    cosines, sines = rotary_tables(length, width)
    give = after(jnp.stack([v[3:] for v in w]), cosines, sines)
    w = jnp.stack([jnp.stack([v[:3] for v in w]), to_core(give, seq)])
    w_parts = [w] + [to_fsdp(w, fsdp, j) for j in flips]

    gu = gate_up_weight.reshape(piece, 2, seq, fsdp, unit_piece).transpose(3, 0, 1, 2, 4)
    gu = gu.reshape(fsdp, piece, 2 * hidden)
    gu = jnp.pad(gu, ((0, 0), (0, 0), (0, tiles * LANES - 2 * hidden)))
    gu = gu.reshape(fsdp, piece, tiles, LANES).transpose(0, 2, 1, 3)
    pick = lambda v, j: lax.dynamic_index_in_dim(v, f ^ j, axis=0, keepdims=False)
    gu = after(gu, w)
    gu = [pick(gu, 0)] + [to_fsdp(pick(gu, j), fsdp, j) for j in flips]
    g_late = after(g_b, gu)
    g_parts = [g_b] + [to_fsdp(g_late, fsdp, j) for j in flips]

    o = after(out_weight, gu).reshape(piece, seq, width).transpose(1, 0, 2)
    o = [o] + [to_line(o, seq, k) for k in steps]
    down = jnp.pad(down_weight, ((0, unit_pad - unit_piece), (0, 0)))
    down = down.reshape(unit_pad, depth // LANES, LANES).transpose(1, 0, 2)
    feed = jnp.concatenate(
        [v.reshape(-1, LANES) for v in gu] + [down.reshape(-1, LANES)], axis=0
    )
    feed = lax.all_gather(feed, "seq", axis=0)

    outs = call(
        functools.partial(inputs_kernel, chips, fsdp),
        [shape((length, depth), BF)] * 2
        + [shape((length, width), BF)] * 3
        + [shape((depth, 3 * width), BF)],
        [pltpu.VMEM((depth, 3 * width), row_type(piece))],
        "attention_inputs",
        place,
        tok_all,
        *w_parts,
        row(ln1_gain),
        row(ln1_bias),
        qkv_bias.reshape(3 * seq, width),
        cosines,
        sines,
        vmem=20,
    )
    h1, u1, q, k_, v, w_qkv = outs
    o = jnp.stack(after(o, q))
    o_parts = [o] + [to_fsdp(o, fsdp, j) for j in flips]
    outs = call(
        functools.partial(attend_kernel, chips),
        [shape((length, width), F32)] + [shape((CORES * rows, width), BF)] * chips,
        [pltpu.VMEM((length, width), BF)],
        "attention_forward",
        place,
        after(q, g_parts),
        k_,
        v,
        flops=ATT,
        vmem=16,
    )
    lse, att = outs[0], outs[1:]
    att = [att[0]] + [to_line(att[k], seq, k) for k in steps]

    keep, give, w_out = call(
        functools.partial(project_kernel, chips, fsdp),
        [shape((rows, depth), F32)] * 2 + [shape((chips * width, depth), BF)],
        [
            pltpu.VMEM((chips * width, depth), row_type(piece)),
            pltpu.VMEM((CORES * rows, depth), F32),
        ],
        "out_projection",
        place,
        *att,
        *o_parts,
        flops=PROJECT,
    )
    z_res, h2 = call(
        norm2_kernel,
        [shape((rows, depth), F32), shape((rows, depth), BF)],
        [],
        "norm2",
        x_b,
        keep,
        to_core(give, seq),
        row(ln2_gain),
        row(ln2_bias),
        smem=False,
    )
    h2_parts = [h2] + [to_fsdp(h2, fsdp, j) for j in flips]

    tokens_here = fsdp * rows
    outs = call(
        functools.partial(feed_kernel, seq, fsdp, hidden, unit_piece),
        [shape((rows, depth), F32)]
        + [shape((rows, depth), BF)] * (fsdp - 1)
        + [
            shape((tokens_here, hidden), BF),
            shape((tokens_here, tiles * LANES), BF),
            shape((hidden, depth), BF),
            shape((tokens_here, depth), BF),
            shape((tokens_here, depth), BF),
        ],
        [
            pltpu.VMEM((depth, tiles * LANES), row_type(piece)),
            pltpu.VMEM((hidden, depth), F32),
            pltpu.VMEM((depth, tiles * LANES), BF),
        ],
        "feed_forward",
        place,
        *h2_parts,
        *g_parts,
        feed,
        vmem=40,
    )
    dh2_keep, dh2_send = outs[0], outs[1:fsdp]
    m, dgu, w_down, h2_all, g_all = outs[fsdp:]
    dh2_got = [to_fsdp(v, fsdp, j) for j, v in zip(flips, dh2_send)]

    block = depth // seq
    lines = tiles * block + (depth // LANES) * unit_pad
    feed_grad = call(
        functools.partial(feed_grad_kernel, seq, hidden, unit_piece),
        shape((seq, lines, LANES), BF),
        [
            pltpu.VMEM((max(block, 256), tiles * LANES), BF),
            pltpu.VMEM((hidden, 256), F32),
        ],
        "feed_gradient",
        m,
        dgu,
        g_all,
        h2_all,
        smem=False,
        flops=FILL_LONG,
        vmem=24,
    )
    feed_raw = lax.psum_scatter(feed_grad, "seq", scatter_dimension=0)
    feed_total = feed_raw.astype(F32)

    ffn = call(
        functools.partial(down_kernel, fsdp),
        [shape((rows, depth), F32)] + [shape((rows, depth), BF)] * (fsdp - 1),
        [],
        "down_projection",
        m,
        w_down,
        smem=False,
        flops=FILL_SHORT,
    )
    dh2_got = after(dh2_got, feed_grad, ffn[0])

    dz, dz_b, sums2 = call(
        functools.partial(norm2_back_kernel, fsdp - 1),
        [shape((rows, depth), F32), shape((rows, depth), BF), shape((2, depth), F32)],
        [],
        "norm2_back",
        dh2_keep,
        *dh2_got,
        z_res,
        g_b,
        row(ln2_gain),
        smem=False,
    )
    outs = call(
        functools.partial(project_back_kernel, chips),
        [shape((CORES * rows, depth), BF)] + [shape((CORES * rows, width), BF)] * chips,
        [],
        "out_projection_back",
        place,
        dz_b,
        to_core(dz_b, seq),
        w_out,
    )
    dz2, do = outs[0], outs[1:]
    do = [do[0]] + [to_line(do[k], seq, k) for k in steps]


    outs = call(
        functools.partial(project_grad_kernel, chips, fsdp),
        [shape((chips, piece, depth), BF)] * fsdp,
        [pltpu.VMEM((chips * width, depth), F32)],
        "out_projection_gradient",
        place,
        *att,
        dz2,
    )
    o_blocks = outs
    do = after(do, outs[0])

    outs = call(
        functools.partial(backward_kernel, chips),
        [shape((length, 3 * width), BF), shape((length, depth), BF)],
        [
            pltpu.VMEM((length, width), BF),
            pltpu.VMEM((length, width), F32),
            pltpu.VMEM((length, width), F32),
        ],
        "attention_backward",
        place,
        q,
        k_,
        v,
        lse,
        *do,
        cosines,
        sines,
        w_qkv,
        flops=LONG,
        vmem=20,
    )
    dp, dh1 = outs
    lanes = 3 * width
    per, count = small_rows(depth, lanes)
    blocks = call(
        functools.partial(qkv_grad_kernel, chips, fsdp),
        [shape((seq * piece + count, lanes), BF)] * fsdp,
        [pltpu.VMEM((depth, lanes), F32)],
        "qkv_gradient",
        place,
        h1,
        u1,
        dp,
        w_qkv,
        sums2,
        flops=FILL_LAST,
        vmem=20,
    )
    line_in = [blocks[0]] + [to_fsdp(blocks[j], fsdp, j) for j in flips]
    blocks = call(
        functools.partial(qkv_line_kernel, chips, fsdp),
        [shape((CORES * piece + count, lanes), BF)] * chips,
        [pltpu.VMEM((seq * piece, lanes), F32)],
        "qkv_gradient_line",
        place,
        *line_in,
    )
    o_late = after(o_blocks, line_in[0])
    total = o_blocks[0].astype(F32)
    for j in flips:
        total = total + to_fsdp(o_late[j], fsdp, j).astype(F32)
    dh1 = gate(dh1, feed_raw, blocks[0])
    ffn_late = after(ffn, blocks[0])
    block_out = z_res + ffn[0]
    for j in flips:
        block_out = block_out + to_fsdp(ffn_late[j], fsdp, j).astype(F32)
    block_out = block_out.astype(BF)
    dh1 = lax.psum_scatter(dh1, "seq", scatter_dimension=0, tiled=True)
    blocks = [blocks[0]] + [to_line(blocks[k], seq, k) for k in steps]
    tail = -(-(4 * per + chips) // 16) * 16
    keep, give = call(
        functools.partial(qkv_core_kernel, chips, piece, per),
        [shape((chips * piece + tail, lanes), BF)] * 2,
        [],
        "qkv_gradient_core",
        *blocks,
        smem=False,
    )
    qkv_grad, small, bias_grad = call(
        functools.partial(qkv_final_kernel, chips, piece, per),
        [
            shape((piece, 3 * depth), F32),
            shape((4, depth), F32),
            shape((3 * seq, width), F32),
        ],
        [pltpu.VMEM((3 * seq, piece, width), F32)],
        "qkv_gradient_final",
        place,
        keep,
        to_core(give, seq),
    )
    input_grad = call(
        norm1_back_kernel,
        shape((rows, depth), F32),
        [],
        "norm1_back",
        dh1,
        x_b,
        row(ln1_gain),
        dz,
        smem=False,
    )

    down_grad = feed_total[tiles * block :].reshape(depth // LANES, unit_pad, LANES)
    down_grad = down_grad[:, :unit_piece].transpose(1, 0, 2).reshape(unit_piece, depth)
    gu = feed_total[: tiles * block].astype(BF).reshape(tiles, fsdp, piece, LANES)
    gu = gu.transpose(1, 2, 0, 3).reshape(fsdp, piece, tiles * LANES)[:, :, : 2 * hidden]
    gu_got = [pick(gu, 0)] + [to_fsdp(pick(gu, j), fsdp, j) for j in flips]
    gu = jnp.stack(gu_got)
    order = jnp.arange(fsdp, dtype=jnp.int32) ^ f
    gu = jnp.take(gu, order, axis=0)
    gu = gu.reshape(fsdp, piece, 2, seq, unit_piece).transpose(1, 2, 3, 0, 4)
    gu_grad = gu.reshape(piece, 2 * seq * fsdp * unit_piece).astype(F32)


    out_w_grad = total[0]
    for k in steps:
        out_w_grad = out_w_grad + to_line(total[k].astype(BF), seq, k).astype(F32)

    return (
        block_out.reshape(1, rows, depth),
        input_grad.reshape(1, rows, depth),
        small[0],
        small[1],
        qkv_grad,
        bias_grad.reshape(3 * depth),
        out_w_grad,
        small[2],
        small[3],
        gu_grad,
        down_grad,
    )


def solution(mesh):
    seq, fsdp = mesh.shape["seq"], mesh.shape["fsdp"]
    split = P(("seq", "fsdp"), None)
    toks = P("fsdp", "seq", None)

    def step(*args):
        return on_device(seq, fsdp, *args)

    return jax.shard_map(
        step,
        mesh=mesh,
        in_specs=(toks, P(), P(), split, P(), split, P(), P(), split, split, toks),
        out_specs=(toks, toks, P(), P(), split, P(), split, P(), P(), split, split),
        check_vma=False,
    )
```

```python
import functools

import jax
import jax.numpy as jnp
from jax import lax
from jax.experimental import pallas as pl
from jax.experimental.pallas import tpu as pltpu
from jax.sharding import PartitionSpec as P

H = 16
HD = 64
ROT = 16
EPS = 1e-05
BF = jnp.bfloat16
F32 = jnp.float32
CORES = 2
LANES = 128
ATT = 10_000_000_000
FILL_SHORT = 4_000_000_000
FILL_LONG = 8_000_000_000
FILL_LAST = 10_000_000_000
PROJECT = 20_000_000_000
LONG = 70_000_000_000
MIB = 1024 * 1024


def to_core(value, seq):
    return lax.ppermute(value, "seq", [(i, i ^ 1) for i in range(seq)])


def to_line(value, seq, step):
    return lax.ppermute(value, "seq", [(i, i ^ (CORES * step)) for i in range(seq)])


def to_fsdp(value, fsdp, flip):
    return lax.ppermute(value, "fsdp", [(i, i ^ flip) for i in range(fsdp)])


def after(values, *earlier):
    flat, tree = jax.tree.flatten(values)
    held = lax.optimization_barrier((flat, earlier))[0]
    return jax.tree.unflatten(tree, held)


def call(body, out_shape, scratch, name, *args, smem=True, flops=1_000_000_000, vmem=8, far=(), far_out=()):
    spaces = lambda count, hbm: [
        pl.BlockSpec(memory_space=pltpu.HBM if i in hbm else pltpu.VMEM) for i in range(count)
    ]
    specs = spaces(len(args), far)
    args = [
        pltpu.with_memory_space_constraint(a, pltpu.HBM) if i in far else a
        for i, a in enumerate(args)
    ]
    alone = not isinstance(out_shape, (list, tuple))
    outs = [out_shape] if alone else list(out_shape)
    outs = [pltpu.HBM(o.shape, o.dtype) if i in far_out else o for i, o in enumerate(outs)]
    out_shape = outs[0] if alone else outs
    out_specs = spaces(1 if alone else len(out_shape), far_out)
    if smem:
        specs[0] = pl.BlockSpec(memory_space=pltpu.SMEM)
    return pl.pallas_call(
        body,
        out_shape=out_shape,
        in_specs=specs,
        out_specs=out_specs[0] if alone else out_specs,
        scratch_shapes=scratch,
        compiler_params=pltpu.CompilerParams(vmem_limit_bytes=vmem * MIB),
        cost_estimate=pl.CostEstimate(flops=flops, transcendentals=0, bytes_accessed=1000000),
        name=name,
    )(*args)


def gate_kernel(*refs):
    pltpu.touch(refs[-1])


def gate(value, *earlier):
    whole = pl.BlockSpec(memory_space=pl.ANY)
    return pl.pallas_call(
        gate_kernel,
        out_shape=shape(value.shape, value.dtype),
        in_specs=[whole] * (1 + len(earlier)),
        out_specs=whole,
        input_output_aliases={0: 0},
        cost_estimate=pl.CostEstimate(flops=1000, transcendentals=0, bytes_accessed=1000),
        name="gate",
    )(value, *earlier)


def shape(dims, dtype):
    return jax.ShapeDtypeStruct(dims, dtype)


def row_type(step):
    return BF if step % 16 == 0 else F32


def at_rows(start, count, step):
    return pl.ds(pl.multiple_of(start, step), count)


def dot(left, right, left_dim, right_dim):
    return lax.dot_general(
        left, right, (((left_dim,), (right_dim,)), ((), ())), preferred_element_type=F32
    )


def rotary_tables(length, width):
    half = ROT // 2
    lane = jnp.arange(width, dtype=jnp.int32) % HD
    frequency = 10000.0 ** (-2.0 * (lane % half).astype(F32) / ROT)
    angles = jnp.arange(length, dtype=jnp.int32).astype(F32)[:, None] * frequency[None, :]
    rotated = (lane < ROT)[None, :]
    sines = jnp.where((lane < half)[None, :], -jnp.sin(angles), jnp.sin(angles))
    return (jnp.where(rotated, jnp.cos(angles), 1.0), jnp.where(rotated, sines, 0.0))


def lane_roll(value, shift):
    width = value.shape[1]
    if width % LANES == 0:
        return pltpu.roll(value, shift % width, 1)
    return jnp.roll(value, shift, axis=1)


def rotate(value, cosines, sines):
    half = ROT // 2
    lane = lax.broadcasted_iota(jnp.int32, value.shape, 1) % HD
    partner = jnp.where(lane < half, lane_roll(value, -half), lane_roll(value, half))
    return value * cosines + partner * sines


def head_lanes(value, head):
    lane = lax.broadcasted_iota(jnp.int32, value.shape, 1)
    return jnp.where(lane // HD == head, value, jnp.zeros_like(value))


def causal(scores, first_row):
    rows = first_row + lax.broadcasted_iota(jnp.int32, scores.shape, 0)
    cols = lax.broadcasted_iota(jnp.int32, scores.shape, 1)
    return jnp.where(rows >= cols, scores, -jnp.inf)


def norm_parts(values):
    mean = jnp.mean(values, axis=-1, keepdims=True)
    centred = values - mean
    inv = lax.rsqrt(jnp.mean(centred * centred, axis=-1, keepdims=True) + EPS)
    return (centred * inv, inv)


def norm_back(grad, gain, unit, inv):
    scaled = grad * gain
    return inv * (
        scaled
        - jnp.mean(scaled, axis=-1, keepdims=True)
        - unit * jnp.mean(scaled * unit, axis=-1, keepdims=True)
    )


def inputs_kernel(chips, fsdp, place, *refs):
    refs = list(refs)
    tok_ref, parts, refs = refs[0], refs[1 : 1 + fsdp], refs[1 + fsdp :]
    gain, bias, qb, cos_ref, sin_ref, h1_ref, u1_ref, q_ref, k_ref, v_ref, w_ref = refs[:11]
    w_rows, tok_in, tok_sem = refs[11:]

    def tok_copy(s):
        return pltpu.make_async_copy(tok_ref.at[s], tok_in.at[s], tok_sem.at[s])

    for s in range(chips * CORES):
        tok_copy(s).start()
    z, core, f = place[0], place[1], place[2]
    length, width = q_ref.shape
    rows = tok_ref.shape[1]
    piece = parts[0].shape[3]
    seq = chips * CORES
    for j in range(fsdp):
        for k in range(chips):
            for c in range(CORES):
                at = (((z ^ k) * CORES + (core ^ c)) * fsdp + (f ^ j)) * piece
                for t in range(3):
                    w_rows[at_rows(at, piece, piece), t * width : (t + 1) * width] = parts[j][
                        c, k, t
                    ].astype(w_rows.dtype)
    w_ref[...] = w_rows[...].astype(BF)

    def norm(s, carry):
        tok_copy(s).wait()
        u1, _ = norm_parts(tok_in[s].astype(F32))
        here = at_rows(s * rows, rows, rows)
        u1_ref[here, :] = u1.astype(BF)
        h1_ref[here, :] = (u1 * gain[...] + bias[...]).astype(BF)
        return carry

    lax.fori_loop(0, seq, norm, 0)
    me = z * CORES + core
    biases = [qb[pl.ds(part * seq + me, 1), :] for part in range(3)]
    block = min(256, length)

    def project(i, carry):
        here = at_rows(i * block, block, block)
        p = dot(h1_ref[here, :], w_ref[...], 1, 0)
        cosines, sines = cos_ref[here, :], sin_ref[here, :]
        q_ref[here, :] = rotate(p[:, :width] + biases[0], cosines, sines).astype(BF)
        k_ref[here, :] = rotate(p[:, width : 2 * width] + biases[1], cosines, sines).astype(BF)
        v_ref[here, :] = (p[:, 2 * width :] + biases[2]).astype(BF)
        return carry

    lax.fori_loop(0, length // block, project, 0)


def attend_kernel(chips, place, q_ref, k_ref, v_ref, lse_ref, *refs):
    att_out, att_ref = refs[:chips], refs[chips]
    z = place[0]
    length, width = q_ref.shape
    rows = length // (chips * CORES)
    block = min(256, length)
    scaling = HD ** (-0.5)
    for at in range(0, length, block):
        here, upto = pl.ds(at, block), pl.ds(0, at + block)
        q, k, v = q_ref[here, :], k_ref[upto, :], v_ref[upto, :]
        att = jnp.zeros((block, width), F32)
        totals = []
        for head in range(width // HD):
            scores = causal(dot(head_lanes(q, head), k, 1, 1) * scaling, at)
            top = jnp.max(scores, axis=-1, keepdims=True)
            exponent = jnp.exp(scores - top)
            total = jnp.sum(exponent, axis=-1, keepdims=True)
            weights = (exponent * (1.0 / total)).astype(BF)
            att = att + head_lanes(dot(weights, v, 1, 0), head)
            totals.append(jnp.broadcast_to(top + jnp.log(total), (block, HD)))
        att_ref[here, :] = att.astype(BF)
        lse_ref[here, :] = jnp.concatenate(totals, axis=1)
    for k in range(chips):
        at = (z ^ k) * (CORES * rows)
        att_out[k][...] = att_ref[at_rows(at, CORES * rows, CORES * rows), :]


def project_kernel(chips, fsdp, place, *refs):
    refs = list(refs)
    att, refs = refs[:chips], refs[chips:]
    parts, refs = refs[:fsdp], refs[fsdp:]
    keep_ref, give_ref, w_ref, w_rows, res = refs
    core, f = place[1], place[2]
    rows = keep_ref.shape[0]
    width = att[0].shape[1]
    piece = parts[0].shape[2]
    for j in range(fsdp):
        for k in range(chips):
            at = k * width + (f ^ j) * piece
            for t in range(parts[j].shape[1]):
                w_rows[at_rows(at, piece, piece), t * width : (t + 1) * width] = parts[j][
                    k, t
                ].astype(w_rows.dtype)
    w_ref[...] = w_rows[...].astype(BF)
    res[...] = dot(jnp.concatenate([a[...] for a in att], axis=1), w_ref[...], 1, 0)
    keep_ref[...] = res[at_rows(core * rows, rows, rows), :]
    give_ref[...] = res[at_rows((1 - core) * rows, rows, rows), :]


def norm2_kernel(x_ref, keep_ref, got_ref, gain, bias, z_ref, h2_ref):
    z = x_ref[...].astype(F32) + (keep_ref[...] + got_ref[...])
    z_ref[...] = z
    u2, _ = norm_parts(z)
    h2_ref[...] = (u2 * gain[...] + bias[...]).astype(BF)


def feed_kernel(seq, fsdp, hidden, unit_piece, place, *refs):
    refs = list(refs)
    h2, refs = refs[:fsdp], refs[fsdp:]
    g, refs = refs[:fsdp], refs[fsdp:]
    feed_ref, keep_ref, refs = refs[0], refs[1], refs[2:]
    sends, refs = refs[: fsdp - 1], refs[fsdp - 1 :]
    m_ref, dgu_ref, wd_far, h2_all, g_all, down_rows, feed_in, feed_sem, g_sem, wd_out, wd_sem, gu_rows = refs[:12]
    w_gu = refs[12] if len(refs) > 12 else gu_rows
    f = place[2]
    rows, depth = keep_ref.shape
    copies = [
        pltpu.make_async_copy(feed_ref.at[s], feed_in.at[s], feed_sem.at[s]) for s in range(seq)
    ]
    for copy in copies:
        copy.start()
    g_copies = [
        pltpu.make_async_copy(g[j], g_all.at[pl.ds(j * rows, rows), :], g_sem.at[j])
        for j in range(fsdp)
    ]
    for copy in g_copies:
        copy.start()
    for j in range(fsdp):
        h2_all[j * rows : (j + 1) * rows, :] = h2[j][...]
    tiles = gu_rows.shape[1] // LANES
    piece = depth // (seq * fsdp)
    unit_pad = down_pad(unit_piece)
    first = fsdp * tiles * piece

    def gather(s, carry):
        pltpu.make_async_copy(feed_ref.at[s], feed_in.at[s], feed_sem.at[s]).wait()
        for j in range(fsdp):
            at = at_rows((s * fsdp + (f ^ j)) * piece, piece, piece)
            for t in range(tiles):
                tile = feed_in[s, pl.ds((j * tiles + t) * piece, piece), :]
                gu_rows[at, t * LANES : (t + 1) * LANES] = tile.astype(gu_rows.dtype)
        return carry

    def gather_down(s, at):
        for t in range(depth // LANES):
            tile = feed_in[s, pl.ds(first + t * unit_pad, unit_pad), :].astype(F32)
            down_rows[at, t * LANES : (t + 1) * LANES] = tile[:unit_piece, :]

    lax.fori_loop(0, seq, gather, 0)
    if unit_piece % 8 == 0:

        def gather_units(s, carry):
            gather_down(s, at_rows(s * unit_piece, unit_piece, 8))
            return carry

        lax.fori_loop(0, seq, gather_units, 0)
    else:
        for s in range(seq):
            gather_down(s, pl.ds(s * unit_piece, unit_piece))
    wd_ref = wd_out
    wd_ref[...] = down_rows[...].astype(BF)
    wd_copy = pltpu.make_async_copy(wd_ref, wd_far, wd_sem)
    wd_copy.start()
    if w_gu is not gu_rows:
        w_gu[...] = gu_rows[...].astype(BF)
    for copy in g_copies:
        copy.wait()
    if dgu_ref.shape[1] > 2 * hidden:
        dgu_ref[...] = jnp.zeros_like(dgu_ref)
    chunks = 2

    def work(i, carry):
        here = at_rows(i * (chunks * rows), chunks * rows, chunks * rows)
        gu = dot(h2_all[here, :], w_gu[...], 1, 0)
        gate, up = gu[:, :hidden], gu[:, hidden : 2 * hidden]
        dm = dot(g_all[here, :], wd_ref[...], 1, 1)
        sig = 1.0 / (1.0 + jnp.exp(-gate))
        silu = gate * sig
        m_ref[here, :] = (silu * up).astype(BF)
        dgu_ref[here, :hidden] = (dm * up * sig * (1.0 + gate * (1.0 - sig))).astype(BF)
        dgu_ref[here, hidden : 2 * hidden] = (dm * silu).astype(BF)
        dh2 = dot(dgu_ref[here, :], w_gu[...], 1, 1)
        for j in range(fsdp):

            @pl.when(i == j // chunks)
            def _():
                part = dh2[(j % chunks) * rows : (j % chunks + 1) * rows, :]
                if j == 0:
                    keep_ref[...] = part
                else:
                    sends[j - 1][...] = part.astype(BF)

        return carry

    lax.fori_loop(0, fsdp // chunks, work, 0)
    wd_copy.wait()


def down_kernel(fsdp, m_ref, wd_ref, keep_ref, *sends):
    rows = keep_ref.shape[0]
    for j in range(fsdp):
        part = dot(m_ref[j * rows : (j + 1) * rows, :], wd_ref[...], 1, 0)
        if j == 0:
            keep_ref[...] = part
        else:
            sends[j - 1][...] = part.astype(BF)


def down_pad(unit_piece):
    return -(-unit_piece // 16) * 16


def feed_grad_kernel(seq, hidden, unit_piece, m_ref, dgu_ref, g_all, h2_all, out_ref, *refs):
    gu_out, down_out, down_acc, gu_sem, down_sem = refs
    depth = g_all.shape[1]
    tiles = dgu_ref.shape[1] // LANES
    block = depth // seq
    unit_pad = down_pad(unit_piece)
    pair = max(1, 256 // block)

    def gu_copy(i):
        return pltpu.make_async_copy(
            gu_out.at[pl.ds(i * pair, pair)],
            out_ref.at[pl.ds(i * pair, pair), pl.ds(0, tiles * block), :],
            gu_sem.at[i],
        )

    def down_copy(i):
        at = pl.multiple_of(i * 2 * unit_pad, 16)
        return pltpu.make_async_copy(
            down_out.at[:, pl.ds(at, 2 * unit_pad), :],
            out_ref.at[:, pl.ds(tiles * block + at, 2 * unit_pad), :],
            down_sem.at[i],
        )

    def gate_up(i, carry):
        cols = pl.ds(pl.multiple_of(i * (pair * block), pair * block), pair * block)
        grad = dot(h2_all[:, cols], dgu_ref[...], 0, 0).astype(BF)
        for s in range(pair):
            for t in range(tiles):
                gu_out[i * pair + s, t * block : (t + 1) * block, :] = grad[
                    s * block : (s + 1) * block, t * LANES : (t + 1) * LANES
                ]
        gu_copy(i).start()
        return carry

    lax.fori_loop(0, seq // pair, gate_up, 0)

    def down(i, carry):
        cols = pl.ds(pl.multiple_of(i * 256, 256), 256)
        down_acc[...] = dot(m_ref[...], g_all[:, cols], 0, 0)
        for s in range(seq):
            for t in range(2):
                tile = down_acc[
                    s * unit_piece : (s + 1) * unit_piece, t * LANES : (t + 1) * LANES
                ].astype(BF)
                if unit_pad > unit_piece:
                    tile = jnp.concatenate(
                        [tile, jnp.zeros((unit_pad - unit_piece, LANES), BF)], axis=0
                    )
                down_out[s, at_rows((i * 2 + t) * unit_pad, unit_pad, 16), :] = tile
        down_copy(i).start()
        return carry

    lax.fori_loop(0, depth // 256, down, 0)

    def finish_gu(i, carry):
        gu_copy(i).wait()
        return carry

    def finish_down(i, carry):
        down_copy(i).wait()
        return carry

    lax.fori_loop(0, seq // pair, finish_gu, 0)
    lax.fori_loop(0, depth // 256, finish_down, 0)


def norm2_back_kernel(count, *refs):
    keep_ref, got, refs = refs[0], refs[1 : 1 + count], refs[1 + count :]
    z_ref, g_ref, gain, dz_ref, dzb_ref, sums_ref = refs
    dh2 = keep_ref[...]
    for ref in got:
        dh2 = dh2 + ref[...].astype(F32)
    u2, r2 = norm_parts(z_ref[...])
    dz = g_ref[...].astype(F32) + norm_back(dh2, gain[...], u2, r2)
    dz_ref[...] = dz
    dzb_ref[...] = dz.astype(BF)
    sums_ref[0:1, :] = jnp.sum(dh2 * u2, axis=0, keepdims=True)
    sums_ref[1:2, :] = jnp.sum(dh2, axis=0, keepdims=True)


def project_back_kernel(chips, place, mine_ref, other_ref, w_ref, dz2_ref, *outs):
    core = place[1]
    rows = mine_ref.shape[0]
    width = outs[0].shape[1]
    dz2_ref[at_rows(core * rows, rows, rows), :] = mine_ref[...]
    dz2_ref[at_rows((1 - core) * rows, rows, rows), :] = other_ref[...]
    do = dot(dz2_ref[...], w_ref[...], 1, 1)
    for k in range(chips):
        outs[k][...] = do[:, k * width : (k + 1) * width].astype(BF)


def project_grad_kernel(chips, fsdp, place, *refs):
    att, refs = refs[:chips], refs[chips:]
    dz2_ref, refs = refs[0], refs[1:]
    outs, acc = refs[:fsdp], refs[fsdp]
    f = place[2]
    width = att[0].shape[1]
    piece = width // fsdp
    acc[...] = dot(jnp.concatenate([a[...] for a in att], axis=1), dz2_ref[...], 0, 0)
    for j in range(fsdp):
        for k in range(chips):
            at = k * width + (f ^ j) * piece
            outs[j][k] = acc[at_rows(at, piece, piece), :].astype(BF)


def backward_kernel(chips, place, *refs):
    q_ref, k_ref, v_ref, lse_ref = refs[:4]
    do_in, refs = refs[4 : 4 + chips], refs[4 + chips :]
    cos_ref, sin_ref, w_ref, dp_ref, dh_far, do_ref, dk_acc, dv_acc, dh_ref, dh_sem = refs
    z = place[0]
    length, width = q_ref.shape
    rows = length // (chips * CORES)
    for k in range(chips):
        at = (z ^ k) * (CORES * rows)
        do_ref[at_rows(at, CORES * rows, CORES * rows), :] = do_in[k][...]
    heads = width // HD
    block = min(256, length)
    scaling = HD ** (-0.5)
    dk_acc[...] = jnp.zeros_like(dk_acc)
    dv_acc[...] = jnp.zeros_like(dv_acc)
    for at in range(0, length, block):
        here, upto = pl.ds(at, block), pl.ds(0, at + block)
        q, do, k, v = q_ref[here, :], do_ref[here, :], k_ref[upto, :], v_ref[upto, :]
        dq = jnp.zeros((block, width), F32)
        for head in range(heads):
            qh, doh = head_lanes(q, head), head_lanes(do, head)
            lse = lse_ref[here, head * HD : head * HD + 1]
            scores = causal(dot(qh, k, 1, 1) * scaling, at)
            probs = jnp.exp(scores - lse)
            dprobs = dot(doh, v, 1, 1)
            delta = jnp.sum(probs * dprobs, axis=-1, keepdims=True)
            dscores = (probs * (dprobs - delta)).astype(BF)
            dq = dq + head_lanes(dot(dscores, k, 1, 0), head)
            dk_acc[upto, :] += dot(dscores, qh, 0, 0)
            dv_acc[upto, :] += dot(probs.astype(BF), doh, 0, 0)
        dq = rotate(dq * scaling, cos_ref[here, :], -sin_ref[here, :])
        dp_ref[here, :width] = dq.astype(BF)

    def finish(i, carry):
        here = at_rows(i * block, block, block)
        dk = rotate(dk_acc[here, :] * scaling, cos_ref[here, :], -sin_ref[here, :])
        dp_ref[here, width : 2 * width] = dk.astype(BF)
        dp_ref[here, 2 * width :] = dv_acc[here, :].astype(BF)
        dh_ref[here, :] = dot(dp_ref[here, :], w_ref[...], 1, 1).astype(BF)
        dh_copy(i).start()
        return carry

    def dh_copy(i):
        here = at_rows(i * block, block, block)
        return pltpu.make_async_copy(dh_ref.at[here, :], dh_far.at[here, :], dh_sem.at[i])

    def dh_wait(i, carry):
        dh_copy(i).wait()
        return carry

    lax.fori_loop(0, length // block, finish, 0)
    lax.fori_loop(0, length // block, dh_wait, 0)


def small_rows(depth, lanes):
    return -(-depth // lanes), -(-(4 * -(-depth // lanes) + 1) // 16) * 16


def tree_sum(values):
    values = list(values)
    while len(values) > 1:
        values = [values[i] + values[i + 1] for i in range(0, len(values), 2)]
    return values[0]


def qkv_grad_kernel(chips, fsdp, place, h1_ref, u1_ref, dp_ref, w_ref, sums2_ref, *refs):
    outs, acc = refs[:fsdp], refs[fsdp]
    f = place[2]
    seq = chips * CORES
    depth, lanes = acc.shape
    piece = depth // (seq * fsdp)
    length = dp_ref.shape[0]
    acc[...] = dot(h1_ref[...], dp_ref[...], 0, 0)
    block = min(256, length)

    def sums(i, carry):
        gains, shifts, biases = carry
        here = at_rows(i * block, block, block)
        dh1 = dot(dp_ref[here, :], w_ref[...], 1, 1)
        gains = gains + jnp.sum(dh1 * u1_ref[here, :].astype(F32), axis=0, keepdims=True)
        shifts = shifts + jnp.sum(dh1, axis=0, keepdims=True)
        biases = biases + jnp.sum(dp_ref[here, :].astype(F32), axis=0, keepdims=True)
        return (gains, shifts, biases)

    zeros = jnp.zeros((1, depth), F32)
    gains, shifts, biases = lax.fori_loop(
        0, length // block, sums, (zeros, zeros, jnp.zeros((1, lanes), F32))
    )
    per, count = small_rows(depth, lanes)
    small = []
    for v in (gains, shifts, sums2_ref[0:1, :], sums2_ref[1:2, :]):
        if per * lanes > depth:
            v = jnp.concatenate([v, jnp.zeros((1, per * lanes - depth), F32)], axis=1)
        small += [v[:, r * lanes : (r + 1) * lanes] for r in range(per)]
    small.append(biases)
    if count > len(small):
        small.append(jnp.zeros((count - len(small), lanes), F32))
    small = jnp.concatenate(small, axis=0)
    for j in range(fsdp):
        for s in range(seq):
            at = (s * fsdp + (f ^ j)) * piece
            outs[j][s * piece : (s + 1) * piece, :] = acc[at_rows(at, piece, piece), :].astype(BF)
        outs[j][seq * piece :, :] = small.astype(BF)


def qkv_line_kernel(chips, fsdp, place, *refs):
    got, refs = refs[:fsdp], refs[fsdp:]
    outs, acc = refs[:chips], refs[chips]
    z, core = place[0], place[1]
    count = outs[0].shape[0]
    total_rows = got[0].shape[0]
    small = total_rows - acc.shape[0]
    piece = acc.shape[0] // (chips * CORES)
    total = tree_sum([ref[...].astype(F32) for ref in got])
    acc[...] = total[: total_rows - small, :]
    for k in range(chips):
        for c in range(CORES):
            at = ((z ^ k) * CORES + (core ^ c)) * piece
            outs[k][c * piece : (c + 1) * piece, :] = acc[at_rows(at, piece, piece), :].astype(BF)
        outs[k][CORES * piece : count, :] = total[total_rows - small :, :].astype(BF)


def qkv_core_kernel(chips, piece, per, *refs):
    got, (keep_ref, give_ref) = refs[:chips], refs[chips:]
    lanes = keep_ref.shape[1]
    small = [ref[CORES * piece :, :].astype(F32) for ref in got]
    total = tree_sum(small)
    bias = [v[4 * per : 4 * per + 1, :] for v in small]
    rest = keep_ref.shape[0] - chips * piece - 4 * per - chips
    pad = [jnp.zeros((rest, lanes), F32)] if rest > 0 else []
    tail = jnp.concatenate([total[: 4 * per, :]] + bias + pad, axis=0)
    for c, ref in ((0, keep_ref), (1, give_ref)):
        for k in range(chips):
            ref[k * piece : (k + 1) * piece, :] = got[k][c * piece : (c + 1) * piece, :]
        ref[chips * piece :, :] = tail.astype(BF)


def qkv_final_kernel(chips, piece, per, place, keep_ref, got_ref, grad_ref, small_ref, bias_ref, acc):
    z, core = place[0], place[1]
    seq = chips * CORES
    lanes = keep_ref.shape[1]
    width = lanes // 3
    depth = small_ref.shape[1]
    at = chips * piece
    tails = [ref[at:, :].astype(F32) for ref in (keep_ref, got_ref)]
    total = tails[0] + tails[1]
    for c, ref in ((0, keep_ref), (1, got_ref)):
        for k in range(chips):
            src = (z ^ k) * CORES + (core ^ c)
            rows = ref[k * piece : (k + 1) * piece, :].astype(F32)
            bias = tails[c][4 * per + k : 4 * per + k + 1, :]
            for part in range(3):
                acc[part * seq + src] = rows[:, part * width : (part + 1) * width]
                bias_ref[pl.ds(part * seq + src, 1), :] = bias[:, part * width : (part + 1) * width]
    for i in range(3 * seq):
        grad_ref[:, i * width : (i + 1) * width] = acc[i]
    for v in range(4):
        for r in range(per):
            upto = min(lanes, depth - r * lanes)
            small_ref[v : v + 1, r * lanes : r * lanes + upto] = total[v * per + r : v * per + r + 1, :upto]


def norm1_back_kernel(dh1_ref, x_ref, gain, dz_ref, out_ref):
    u1, r1 = norm_parts(x_ref[...].astype(F32))
    out_ref[...] = dz_ref[...] + norm_back(dh1_ref[...].astype(F32), gain[...], u1, r1)


def on_device(
    seq,
    fsdp,
    tokens,
    ln1_gain,
    ln1_bias,
    qkv_weight,
    qkv_bias,
    out_weight,
    ln2_gain,
    ln2_bias,
    gate_up_weight,
    down_weight,
    out_grad,
):
    rows, depth = tokens.shape[1], tokens.shape[2]
    length = rows * seq
    chips = seq // CORES
    width = depth // seq
    piece = qkv_weight.shape[0]
    unit_piece = down_weight.shape[0]
    hidden = seq * unit_piece
    tiles = -(-2 * hidden // LANES)
    unit_pad = down_pad(unit_piece)
    me = lax.axis_index("seq")
    z, core, f = me // CORES, me % CORES, lax.axis_index("fsdp")
    place = jnp.stack([z, core, f]).astype(jnp.int32)
    steps, flips = range(1, chips), range(1, fsdp)
    by_place = jnp.arange(seq, dtype=jnp.int32) ^ me
    x_b = tokens.reshape(rows, depth)
    g_b = out_grad.reshape(rows, depth)
    row = lambda v: v.reshape(1, -1)

    tok_all = lax.all_gather(x_b, "seq", axis=0)

    w = qkv_weight.reshape(piece, 3, seq, width).transpose(2, 1, 0, 3)
    w = jnp.take(w, by_place, axis=0).reshape(chips, CORES * 3, piece, width)
    w = [w[0]] + [to_line(w[k], seq, k) for k in steps]
    cosines, sines = rotary_tables(length, width)
    give = after(jnp.stack([v[3:] for v in w]), cosines, sines)
    w = jnp.stack([jnp.stack([v[:3] for v in w]), to_core(give, seq)])
    w_parts = [w] + [to_fsdp(w, fsdp, j) for j in flips]

    gu = gate_up_weight.reshape(piece, 2, seq, fsdp, unit_piece).transpose(3, 0, 1, 2, 4)
    gu = gu.reshape(fsdp, piece, 2 * hidden)
    gu = jnp.pad(gu, ((0, 0), (0, 0), (0, tiles * LANES - 2 * hidden)))
    gu = gu.reshape(fsdp, piece, tiles, LANES).transpose(0, 2, 1, 3)
    pick = lambda v, j: lax.dynamic_index_in_dim(v, f ^ j, axis=0, keepdims=False)
    gu = after(gu, w)
    gu = [pick(gu, 0)] + [to_fsdp(pick(gu, j), fsdp, j) for j in flips]
    g_late = after(g_b, gu)
    g_parts = [g_b] + [to_fsdp(g_late, fsdp, j) for j in flips]

    o = after(out_weight, gu).reshape(piece, seq, width).transpose(1, 0, 2)
    o = [o] + [to_line(o, seq, k) for k in steps]
    down = jnp.pad(down_weight, ((0, unit_pad - unit_piece), (0, 0)))
    down = down.reshape(unit_pad, depth // LANES, LANES).transpose(1, 0, 2)
    feed = jnp.concatenate(
        [v.reshape(-1, LANES) for v in gu] + [down.reshape(-1, LANES)], axis=0
    )
    feed = lax.all_gather(feed, "seq", axis=0)

    outs = call(
        functools.partial(inputs_kernel, chips, fsdp),
        [shape((length, depth), BF)] * 2
        + [shape((length, width), BF)] * 3
        + [shape((depth, 3 * width), BF)],
        [
            pltpu.VMEM((depth, 3 * width), row_type(piece)),
            pltpu.VMEM((seq, rows, depth), BF),
            pltpu.SemaphoreType.DMA((seq,)),
        ],
        "attention_inputs",
        place,
        tok_all,
        *w_parts,
        row(ln1_gain),
        row(ln1_bias),
        qkv_bias.reshape(3 * seq, width),
        cosines,
        sines,
        far=(1,),
        vmem=12,
    )
    h1, u1, q, k_, v, w_qkv = outs
    o = jnp.stack(after(o, q))
    o_parts = [o] + [to_fsdp(o, fsdp, j) for j in flips]
    outs = call(
        functools.partial(attend_kernel, chips),
        [shape((length, width), F32)] + [shape((CORES * rows, width), BF)] * chips,
        [pltpu.VMEM((length, width), BF)],
        "attention_forward",
        place,
        after(q, g_parts),
        k_,
        v,
        flops=ATT,
        vmem=12,
    )
    lse, att = outs[0], outs[1:]
    att = [att[0]] + [to_line(att[k], seq, k) for k in steps]

    keep, give, w_out = call(
        functools.partial(project_kernel, chips, fsdp),
        [shape((rows, depth), F32)] * 2 + [shape((chips * width, depth), BF)],
        [
            pltpu.VMEM((chips * width, depth), row_type(piece)),
            pltpu.VMEM((CORES * rows, depth), F32),
        ],
        "out_projection",
        place,
        *att,
        *o_parts,
        flops=PROJECT,
    )
    z_res, h2 = call(
        norm2_kernel,
        [shape((rows, depth), F32), shape((rows, depth), BF)],
        [],
        "norm2",
        x_b,
        keep,
        to_core(give, seq),
        row(ln2_gain),
        row(ln2_bias),
        smem=False,
    )
    h2_parts = [h2] + [to_fsdp(h2, fsdp, j) for j in flips]

    tokens_here = fsdp * rows
    outs = call(
        functools.partial(feed_kernel, seq, fsdp, hidden, unit_piece),
        [shape((rows, depth), F32)]
        + [shape((rows, depth), BF)] * (fsdp - 1)
        + [
            shape((tokens_here, hidden), BF),
            shape((tokens_here, tiles * LANES), BF),
            shape((hidden, depth), BF),
            shape((tokens_here, depth), BF),
            shape((tokens_here, depth), BF),
        ],
        [
            pltpu.VMEM((hidden, depth), F32),
            pltpu.VMEM(feed.shape, BF),
            pltpu.SemaphoreType.DMA((seq,)),
            pltpu.SemaphoreType.DMA((fsdp,)),
            pltpu.VMEM((hidden, depth), BF),
            pltpu.SemaphoreType.DMA(()),
            pltpu.VMEM((depth, tiles * LANES), row_type(piece)),
        ]
        + ([] if row_type(piece) == BF else [pltpu.VMEM((depth, tiles * LANES), BF)]),
        "feed_forward",
        place,
        *h2_parts,
        *g_parts,
        feed,
        far=tuple(range(1 + fsdp, 2 + 2 * fsdp)),
        far_out=(fsdp + 2,),
        vmem=20,
    )
    dh2_keep, dh2_send = outs[0], outs[1:fsdp]
    m, dgu, w_down, h2_all, g_all = outs[fsdp:]
    dh2_got = [to_fsdp(v, fsdp, j) for j, v in zip(flips, dh2_send)]

    block = depth // seq
    lines = tiles * block + (depth // LANES) * unit_pad
    feed_grad = call(
        functools.partial(feed_grad_kernel, seq, hidden, unit_piece),
        shape((seq, lines, LANES), BF),
        [
            pltpu.VMEM((seq, tiles * block, LANES), BF),
            pltpu.VMEM((seq, lines - tiles * block, LANES), BF),
            pltpu.VMEM((hidden, 256), F32),
            pltpu.SemaphoreType.DMA((seq // max(1, 256 // block),)),
            pltpu.SemaphoreType.DMA((depth // 256,)),
        ],
        "feed_gradient",
        m,
        dgu,
        g_all,
        h2_all,
        smem=False,
        flops=FILL_LONG,
        vmem=16,
        far_out=(0,),
    )
    feed_raw = lax.psum_scatter(feed_grad, "seq", scatter_dimension=0)
    feed_total = feed_raw.astype(F32)

    ffn = call(
        functools.partial(down_kernel, fsdp),
        [shape((rows, depth), F32)] + [shape((rows, depth), BF)] * (fsdp - 1),
        [],
        "down_projection",
        m,
        w_down,
        smem=False,
        flops=FILL_SHORT,
    )
    dh2_got = after(dh2_got, feed_grad, ffn[0])

    dz, dz_b, sums2 = call(
        functools.partial(norm2_back_kernel, fsdp - 1),
        [shape((rows, depth), F32), shape((rows, depth), BF), shape((2, depth), F32)],
        [],
        "norm2_back",
        dh2_keep,
        *dh2_got,
        z_res,
        g_b,
        row(ln2_gain),
        smem=False,
    )
    outs = call(
        functools.partial(project_back_kernel, chips),
        [shape((CORES * rows, depth), BF)] + [shape((CORES * rows, width), BF)] * chips,
        [],
        "out_projection_back",
        place,
        dz_b,
        to_core(dz_b, seq),
        w_out,
    )
    dz2, do = outs[0], outs[1:]
    do = [do[0]] + [to_line(do[k], seq, k) for k in steps]


    outs = call(
        functools.partial(project_grad_kernel, chips, fsdp),
        [shape((chips, piece, depth), BF)] * fsdp,
        [pltpu.VMEM((chips * width, depth), F32)],
        "out_projection_gradient",
        place,
        *att,
        dz2,
    )
    o_blocks = outs
    do = after(do, outs[0])
    ffn_late = after(ffn, do[0])
    ffn_got = [to_fsdp(ffn_late[j], fsdp, j) for j in flips]

    outs = call(
        functools.partial(backward_kernel, chips),
        [shape((length, 3 * width), BF), shape((length, depth), BF)],
        [
            pltpu.VMEM((length, width), BF),
            pltpu.VMEM((length, width), F32),
            pltpu.VMEM((length, width), F32),
            pltpu.VMEM((length, depth), BF),
            pltpu.SemaphoreType.DMA((length // min(256, length),)),
        ],
        "attention_backward",
        place,
        q,
        k_,
        v,
        lse,
        *do,
        cosines,
        sines,
        w_qkv,
        flops=LONG,
        far_out=(1,),
        vmem=12,
    )
    dp, dh1 = outs
    lanes = 3 * width
    per, count = small_rows(depth, lanes)
    blocks = call(
        functools.partial(qkv_grad_kernel, chips, fsdp),
        [shape((seq * piece + count, lanes), BF)] * fsdp,
        [pltpu.VMEM((depth, lanes), F32)],
        "qkv_gradient",
        place,
        h1,
        u1,
        after(dp, ffn_got),
        w_qkv,
        sums2,
        flops=FILL_LAST,
        vmem=12,
    )
    line_in = [blocks[0]] + [to_fsdp(blocks[j], fsdp, j) for j in flips]
    blocks = call(
        functools.partial(qkv_line_kernel, chips, fsdp),
        [shape((CORES * piece + count, lanes), BF)] * chips,
        [pltpu.VMEM((seq * piece, lanes), F32)],
        "qkv_gradient_line",
        place,
        *line_in,
    )
    o_late = after(o_blocks, blocks[0])
    total = o_blocks[0].astype(F32)
    for j in flips:
        total = total + to_fsdp(o_late[j], fsdp, j).astype(F32)
    dh1 = gate(dh1, feed_raw, blocks[0])
    block_out = z_res + ffn[0]
    for v in ffn_got:
        block_out = block_out + v.astype(F32)
    block_out = block_out.astype(BF)
    dh1 = lax.psum_scatter(dh1, "seq", scatter_dimension=0, tiled=True)
    blocks = [blocks[0]] + [to_line(blocks[k], seq, k) for k in steps]
    tail = -(-(4 * per + chips) // 16) * 16
    keep, give = call(
        functools.partial(qkv_core_kernel, chips, piece, per),
        [shape((chips * piece + tail, lanes), BF)] * 2,
        [],
        "qkv_gradient_core",
        *blocks,
        smem=False,
    )
    qkv_grad, small, bias_grad = call(
        functools.partial(qkv_final_kernel, chips, piece, per),
        [
            shape((piece, 3 * depth), F32),
            shape((4, depth), F32),
            shape((3 * seq, width), F32),
        ],
        [pltpu.VMEM((3 * seq, piece, width), F32)],
        "qkv_gradient_final",
        place,
        keep,
        to_core(give, seq),
    )
    input_grad = call(
        norm1_back_kernel,
        shape((rows, depth), F32),
        [],
        "norm1_back",
        dh1,
        x_b,
        row(ln1_gain),
        dz,
        smem=False,
    )

    down_grad = feed_total[tiles * block :].reshape(depth // LANES, unit_pad, LANES)
    down_grad = down_grad[:, :unit_piece].transpose(1, 0, 2).reshape(unit_piece, depth)
    gu = feed_total[: tiles * block].astype(BF).reshape(tiles, fsdp, piece, LANES)
    gu = gu.transpose(1, 2, 0, 3).reshape(fsdp, piece, tiles * LANES)[:, :, : 2 * hidden]
    gu_got = [pick(gu, 0)] + [to_fsdp(pick(gu, j), fsdp, j) for j in flips]
    gu = jnp.stack(gu_got)
    order = jnp.arange(fsdp, dtype=jnp.int32) ^ f
    gu = jnp.take(gu, order, axis=0)
    gu = gu.reshape(fsdp, piece, 2, seq, unit_piece).transpose(1, 2, 3, 0, 4)
    gu_grad = gu.reshape(piece, 2 * seq * fsdp * unit_piece).astype(F32)


    out_w_grad = total[0]
    for k in steps:
        out_w_grad = out_w_grad + to_line(total[k].astype(BF), seq, k).astype(F32)

    return (
        block_out.reshape(1, rows, depth),
        input_grad.reshape(1, rows, depth),
        small[0],
        small[1],
        qkv_grad,
        bias_grad.reshape(3 * depth),
        out_w_grad,
        small[2],
        small[3],
        gu_grad,
        down_grad,
    )


def solution(mesh):
    seq, fsdp = mesh.shape["seq"], mesh.shape["fsdp"]
    split = P(("seq", "fsdp"), None)
    toks = P("fsdp", "seq", None)

    def step(*args):
        return on_device(seq, fsdp, *args)

    return jax.shard_map(
        step,
        mesh=mesh,
        in_specs=(toks, P(), P(), split, P(), split, P(), P(), split, split, toks),
        out_specs=(toks, toks, P(), P(), split, P(), split, P(), P(), split, split),
        check_vma=False,
    )
```

```python
import functools

import jax
import jax.numpy as jnp
from jax import lax
from jax.experimental import pallas as pl
from jax.experimental.pallas import tpu as pltpu
from jax.sharding import PartitionSpec as P

H = 16
HD = 64
ROT = 16
EPS = 1e-05
BF = jnp.bfloat16
F32 = jnp.float32
CORES = 2
LANES = 128
ATT = 10_000_000_000
FILL_SHORT = 4_000_000_000
FILL_LONG = 8_000_000_000
FILL_LAST = 10_000_000_000
PROJECT = 20_000_000_000
LONG = 20_000_000_000
MIB = 1024 * 1024


def to_core(value, seq):
    return lax.ppermute(value, "seq", [(i, i ^ 1) for i in range(seq)])


def to_line(value, seq, step):
    return lax.ppermute(value, "seq", [(i, i ^ (CORES * step)) for i in range(seq)])


def to_fsdp(value, fsdp, flip):
    return lax.ppermute(value, "fsdp", [(i, i ^ flip) for i in range(fsdp)])


def after(values, *earlier):
    flat, tree = jax.tree.flatten(values)
    held = lax.optimization_barrier((flat, earlier))[0]
    return jax.tree.unflatten(tree, held)


def call(body, out_shape, scratch, name, *args, smem=True, flops=1_000_000_000, vmem=8, far=(), far_out=()):
    spaces = lambda count, hbm: [
        pl.BlockSpec(memory_space=pltpu.HBM if i in hbm else pltpu.VMEM) for i in range(count)
    ]
    specs = spaces(len(args), far)
    args = [
        pltpu.with_memory_space_constraint(a, pltpu.HBM) if i in far else a
        for i, a in enumerate(args)
    ]
    alone = not isinstance(out_shape, (list, tuple))
    outs = [out_shape] if alone else list(out_shape)
    outs = [pltpu.HBM(o.shape, o.dtype) if i in far_out else o for i, o in enumerate(outs)]
    out_shape = outs[0] if alone else outs
    out_specs = spaces(1 if alone else len(out_shape), far_out)
    if smem:
        specs[0] = pl.BlockSpec(memory_space=pltpu.SMEM)
    return pl.pallas_call(
        body,
        out_shape=out_shape,
        in_specs=specs,
        out_specs=out_specs[0] if alone else out_specs,
        scratch_shapes=scratch,
        compiler_params=pltpu.CompilerParams(vmem_limit_bytes=vmem * MIB),
        cost_estimate=pl.CostEstimate(flops=flops, transcendentals=0, bytes_accessed=1000000),
        name=name,
    )(*args)


def gate_kernel(*refs):
    pltpu.touch(refs[-1])


def gate(value, *earlier):
    whole = pl.BlockSpec(memory_space=pl.ANY)
    return pl.pallas_call(
        gate_kernel,
        out_shape=shape(value.shape, value.dtype),
        in_specs=[whole] * (1 + len(earlier)),
        out_specs=whole,
        input_output_aliases={0: 0},
        cost_estimate=pl.CostEstimate(flops=1000, transcendentals=0, bytes_accessed=1000),
        name="gate",
    )(value, *earlier)


def shape(dims, dtype):
    return jax.ShapeDtypeStruct(dims, dtype)


def row_type(step):
    return BF if step % 16 == 0 else F32


def at_rows(start, count, step):
    return pl.ds(pl.multiple_of(start, step), count)


def dot(left, right, left_dim, right_dim):
    return lax.dot_general(
        left, right, (((left_dim,), (right_dim,)), ((), ())), preferred_element_type=F32
    )


def rotary_tables(length, width):
    half = ROT // 2
    lane = jnp.arange(width, dtype=jnp.int32) % HD
    frequency = 10000.0 ** (-2.0 * (lane % half).astype(F32) / ROT)
    angles = jnp.arange(length, dtype=jnp.int32).astype(F32)[:, None] * frequency[None, :]
    rotated = (lane < ROT)[None, :]
    sines = jnp.where((lane < half)[None, :], -jnp.sin(angles), jnp.sin(angles))
    return (jnp.where(rotated, jnp.cos(angles), 1.0), jnp.where(rotated, sines, 0.0))


def lane_roll(value, shift):
    width = value.shape[1]
    if width % LANES == 0:
        return pltpu.roll(value, shift % width, 1)
    return jnp.roll(value, shift, axis=1)


def rotate(value, cosines, sines):
    half = ROT // 2
    lane = lax.broadcasted_iota(jnp.int32, value.shape, 1) % HD
    partner = jnp.where(lane < half, lane_roll(value, -half), lane_roll(value, half))
    return value * cosines + partner * sines


def head_lanes(value, head):
    lane = lax.broadcasted_iota(jnp.int32, value.shape, 1)
    return jnp.where(lane // HD == head, value, jnp.zeros_like(value))


def causal(scores, first_row):
    rows = first_row + lax.broadcasted_iota(jnp.int32, scores.shape, 0)
    cols = lax.broadcasted_iota(jnp.int32, scores.shape, 1)
    return jnp.where(rows >= cols, scores, -jnp.inf)


def norm_parts(values):
    mean = jnp.mean(values, axis=-1, keepdims=True)
    centred = values - mean
    inv = lax.rsqrt(jnp.mean(centred * centred, axis=-1, keepdims=True) + EPS)
    return (centred * inv, inv)


def norm_back(grad, gain, unit, inv):
    scaled = grad * gain
    return inv * (
        scaled
        - jnp.mean(scaled, axis=-1, keepdims=True)
        - unit * jnp.mean(scaled * unit, axis=-1, keepdims=True)
    )


def inputs_kernel(chips, fsdp, place, *refs):
    refs = list(refs)
    tok_ref, parts, refs = refs[0], refs[1 : 1 + fsdp], refs[1 + fsdp :]
    gain, bias, qb, cos_ref, sin_ref, h1_far, u1_far, q_ref, k_ref, v_ref, w_ref = refs[:11]
    w_rows, tok_in, tok_sem, h1_ref, u1_ref, h1_sem, u1_sem = refs[11:]

    def tok_copy(s):
        return pltpu.make_async_copy(tok_ref.at[s], tok_in.at[s], tok_sem.at[s])

    for s in range(chips * CORES):
        tok_copy(s).start()
    z, core, f = place[0], place[1], place[2]
    length, width = q_ref.shape
    rows = tok_ref.shape[1]
    piece = parts[0].shape[3]
    seq = chips * CORES
    for j in range(fsdp):
        for k in range(chips):
            for c in range(CORES):
                at = (((z ^ k) * CORES + (core ^ c)) * fsdp + (f ^ j)) * piece
                for t in range(3):
                    w_rows[at_rows(at, piece, piece), t * width : (t + 1) * width] = parts[j][
                        c, k, t
                    ].astype(w_rows.dtype)
    w_ref[...] = w_rows[...].astype(BF)

    def norm(s, carry):
        tok_copy(s).wait()
        u1, _ = norm_parts(tok_in[s].astype(F32))
        here = at_rows(s * rows, rows, rows)
        u1_ref[here, :] = u1.astype(BF)
        h1_ref[here, :] = (u1 * gain[...] + bias[...]).astype(BF)
        u1_copy(s).start()
        h1_copy(s).start()
        return carry

    def h1_copy(s):
        here = at_rows(s * rows, rows, rows)
        return pltpu.make_async_copy(h1_ref.at[here, :], h1_far.at[here, :], h1_sem.at[s])

    def u1_copy(s):
        here = at_rows(s * rows, rows, rows)
        return pltpu.make_async_copy(u1_ref.at[here, :], u1_far.at[here, :], u1_sem.at[s])

    def finish(s, carry):
        u1_copy(s).wait()
        h1_copy(s).wait()
        return carry

    lax.fori_loop(0, seq, norm, 0)
    me = z * CORES + core
    biases = [qb[pl.ds(part * seq + me, 1), :] for part in range(3)]
    block = min(256, length)

    def project(i, carry):
        here = at_rows(i * block, block, block)
        p = dot(h1_ref[here, :], w_ref[...], 1, 0)
        cosines, sines = cos_ref[here, :], sin_ref[here, :]
        q_ref[here, :] = rotate(p[:, :width] + biases[0], cosines, sines).astype(BF)
        k_ref[here, :] = rotate(p[:, width : 2 * width] + biases[1], cosines, sines).astype(BF)
        v_ref[here, :] = (p[:, 2 * width :] + biases[2]).astype(BF)
        return carry

    lax.fori_loop(0, length // block, project, 0)
    lax.fori_loop(0, seq, finish, 0)


def attend_kernel(chips, place, q_ref, k_ref, v_ref, lse_ref, *refs):
    att_out, att_ref = refs[:chips], refs[chips]
    z = place[0]
    length, width = q_ref.shape
    rows = length // (chips * CORES)
    block = min(256, length)
    scaling = HD ** (-0.5)
    for at in range(0, length, block):
        here, upto = pl.ds(at, block), pl.ds(0, at + block)
        q, k, v = q_ref[here, :], k_ref[upto, :], v_ref[upto, :]
        att = jnp.zeros((block, width), F32)
        totals = []
        for head in range(width // HD):
            scores = causal(dot(head_lanes(q, head), k, 1, 1) * scaling, at)
            top = jnp.max(scores, axis=-1, keepdims=True)
            exponent = jnp.exp(scores - top)
            total = jnp.sum(exponent, axis=-1, keepdims=True)
            weights = (exponent * (1.0 / total)).astype(BF)
            att = att + head_lanes(dot(weights, v, 1, 0), head)
            totals.append(jnp.broadcast_to(top + jnp.log(total), (block, HD)))
        att_ref[here, :] = att.astype(BF)
        lse_ref[here, :] = jnp.concatenate(totals, axis=1)
    for k in range(chips):
        at = (z ^ k) * (CORES * rows)
        att_out[k][...] = att_ref[at_rows(at, CORES * rows, CORES * rows), :]


def project_kernel(chips, fsdp, place, *refs):
    refs = list(refs)
    att, refs = refs[:chips], refs[chips:]
    parts, refs = refs[:fsdp], refs[fsdp:]
    keep_ref, give_ref, w_far, w_rows, res, w_ref, w_sem = refs
    core, f = place[1], place[2]
    rows = keep_ref.shape[0]
    width = att[0].shape[1]
    piece = parts[0].shape[2]
    for j in range(fsdp):
        for k in range(chips):
            at = k * width + (f ^ j) * piece
            for t in range(parts[j].shape[1]):
                w_rows[at_rows(at, piece, piece), t * width : (t + 1) * width] = parts[j][
                    k, t
                ].astype(w_rows.dtype)
    w_ref[...] = w_rows[...].astype(BF)
    copy = pltpu.make_async_copy(w_ref, w_far, w_sem)
    copy.start()
    res[...] = dot(jnp.concatenate([a[...] for a in att], axis=1), w_ref[...], 1, 0)
    keep_ref[...] = res[at_rows(core * rows, rows, rows), :]
    give_ref[...] = res[at_rows((1 - core) * rows, rows, rows), :]
    copy.wait()


def norm2_kernel(x_ref, keep_ref, got_ref, gain, bias, z_ref, h2_ref):
    z = x_ref[...].astype(F32) + (keep_ref[...] + got_ref[...])
    z_ref[...] = z
    u2, _ = norm_parts(z)
    h2_ref[...] = (u2 * gain[...] + bias[...]).astype(BF)


def feed_kernel(seq, fsdp, hidden, unit_piece, place, *refs):
    refs = list(refs)
    h2, refs = refs[:fsdp], refs[fsdp:]
    g, refs = refs[:fsdp], refs[fsdp:]
    feed_ref, keep_ref, refs = refs[0], refs[1], refs[2:]
    sends, refs = refs[: fsdp - 1], refs[fsdp - 1 :]
    m_ref, dgu_ref, wd_far, h2_all, g_all, down_rows, feed_in, feed_sem, g_sem, wd_out, wd_sem, gu_rows = refs[:12]
    w_gu = refs[12] if len(refs) > 12 else gu_rows
    f = place[2]
    rows, depth = keep_ref.shape
    copies = [
        pltpu.make_async_copy(feed_ref.at[s], feed_in.at[s], feed_sem.at[s]) for s in range(seq)
    ]
    for copy in copies:
        copy.start()
    g_copies = [
        pltpu.make_async_copy(g[j], g_all.at[pl.ds(j * rows, rows), :], g_sem.at[j])
        for j in range(fsdp)
    ]
    for copy in g_copies:
        copy.start()
    for j in range(fsdp):
        h2_all[j * rows : (j + 1) * rows, :] = h2[j][...]
    tiles = gu_rows.shape[1] // LANES
    piece = depth // (seq * fsdp)
    unit_pad = down_pad(unit_piece)
    first = fsdp * tiles * piece

    def gather(s, carry):
        pltpu.make_async_copy(feed_ref.at[s], feed_in.at[s], feed_sem.at[s]).wait()
        for j in range(fsdp):
            at = at_rows((s * fsdp + (f ^ j)) * piece, piece, piece)
            for t in range(tiles):
                tile = feed_in[s, pl.ds((j * tiles + t) * piece, piece), :]
                gu_rows[at, t * LANES : (t + 1) * LANES] = tile.astype(gu_rows.dtype)
        return carry

    def gather_down(s, at):
        for t in range(depth // LANES):
            tile = feed_in[s, pl.ds(first + t * unit_pad, unit_pad), :].astype(F32)
            down_rows[at, t * LANES : (t + 1) * LANES] = tile[:unit_piece, :]

    lax.fori_loop(0, seq, gather, 0)
    if unit_piece % 8 == 0:

        def gather_units(s, carry):
            gather_down(s, at_rows(s * unit_piece, unit_piece, 8))
            return carry

        lax.fori_loop(0, seq, gather_units, 0)
    else:
        for s in range(seq):
            gather_down(s, pl.ds(s * unit_piece, unit_piece))
    wd_ref = wd_out
    wd_ref[...] = down_rows[...].astype(BF)
    wd_copy = pltpu.make_async_copy(wd_ref, wd_far, wd_sem)
    wd_copy.start()
    if w_gu is not gu_rows:
        w_gu[...] = gu_rows[...].astype(BF)
    for copy in g_copies:
        copy.wait()
    if dgu_ref.shape[1] > 2 * hidden:
        dgu_ref[...] = jnp.zeros_like(dgu_ref)
    chunks = 2

    def work(i, carry):
        here = at_rows(i * (chunks * rows), chunks * rows, chunks * rows)
        gu = dot(h2_all[here, :], w_gu[...], 1, 0)
        gate, up = gu[:, :hidden], gu[:, hidden : 2 * hidden]
        dm = dot(g_all[here, :], wd_ref[...], 1, 1)
        sig = 1.0 / (1.0 + jnp.exp(-gate))
        silu = gate * sig
        m_ref[here, :] = (silu * up).astype(BF)
        dgu_ref[here, :hidden] = (dm * up * sig * (1.0 + gate * (1.0 - sig))).astype(BF)
        dgu_ref[here, hidden : 2 * hidden] = (dm * silu).astype(BF)
        dh2 = dot(dgu_ref[here, :], w_gu[...], 1, 1)
        for j in range(fsdp):

            @pl.when(i == j // chunks)
            def _():
                part = dh2[(j % chunks) * rows : (j % chunks + 1) * rows, :]
                if j == 0:
                    keep_ref[...] = part
                else:
                    sends[j - 1][...] = part.astype(BF)

        return carry

    lax.fori_loop(0, fsdp // chunks, work, 0)
    wd_copy.wait()


def down_kernel(fsdp, m_ref, wd_ref, keep_ref, *sends):
    rows = keep_ref.shape[0]
    for j in range(fsdp):
        part = dot(m_ref[j * rows : (j + 1) * rows, :], wd_ref[...], 1, 0)
        if j == 0:
            keep_ref[...] = part
        else:
            sends[j - 1][...] = part.astype(BF)


def down_pad(unit_piece):
    return -(-unit_piece // 16) * 16


def feed_grad_kernel(seq, hidden, unit_piece, m_ref, dgu_ref, g_all, h2_all, out_ref, *refs):
    gu_out, down_out, down_acc, gu_sem, down_sem = refs
    depth = g_all.shape[1]
    tiles = dgu_ref.shape[1] // LANES
    block = depth // seq
    unit_pad = down_pad(unit_piece)
    pair = max(1, 256 // block)

    def gu_copy(i):
        return pltpu.make_async_copy(
            gu_out.at[pl.ds(i * pair, pair)],
            out_ref.at[pl.ds(i * pair, pair), pl.ds(0, tiles * block), :],
            gu_sem.at[i],
        )

    def down_copy(i):
        at = pl.multiple_of(i * 2 * unit_pad, 16)
        return pltpu.make_async_copy(
            down_out.at[:, pl.ds(at, 2 * unit_pad), :],
            out_ref.at[:, pl.ds(tiles * block + at, 2 * unit_pad), :],
            down_sem.at[i],
        )

    def gate_up(i, carry):
        cols = pl.ds(pl.multiple_of(i * (pair * block), pair * block), pair * block)
        grad = dot(h2_all[:, cols], dgu_ref[...], 0, 0).astype(BF)
        for s in range(pair):
            for t in range(tiles):
                gu_out[i * pair + s, t * block : (t + 1) * block, :] = grad[
                    s * block : (s + 1) * block, t * LANES : (t + 1) * LANES
                ]
        gu_copy(i).start()
        return carry

    lax.fori_loop(0, seq // pair, gate_up, 0)

    def down(i, carry):
        cols = pl.ds(pl.multiple_of(i * 256, 256), 256)
        down_acc[...] = dot(m_ref[...], g_all[:, cols], 0, 0)
        for s in range(seq):
            for t in range(2):
                tile = down_acc[
                    s * unit_piece : (s + 1) * unit_piece, t * LANES : (t + 1) * LANES
                ].astype(BF)
                if unit_pad > unit_piece:
                    tile = jnp.concatenate(
                        [tile, jnp.zeros((unit_pad - unit_piece, LANES), BF)], axis=0
                    )
                down_out[s, at_rows((i * 2 + t) * unit_pad, unit_pad, 16), :] = tile
        down_copy(i).start()
        return carry

    lax.fori_loop(0, depth // 256, down, 0)

    def finish_gu(i, carry):
        gu_copy(i).wait()
        return carry

    def finish_down(i, carry):
        down_copy(i).wait()
        return carry

    lax.fori_loop(0, seq // pair, finish_gu, 0)
    lax.fori_loop(0, depth // 256, finish_down, 0)


def norm2_back_kernel(count, *refs):
    keep_ref, got, refs = refs[0], refs[1 : 1 + count], refs[1 + count :]
    z_ref, g_ref, gain, dz_ref, dzb_ref, sums_ref = refs
    dh2 = keep_ref[...]
    for ref in got:
        dh2 = dh2 + ref[...].astype(F32)
    u2, r2 = norm_parts(z_ref[...])
    dz = g_ref[...].astype(F32) + norm_back(dh2, gain[...], u2, r2)
    dz_ref[...] = dz
    dzb_ref[...] = dz.astype(BF)
    sums_ref[0:1, :] = jnp.sum(dh2 * u2, axis=0, keepdims=True)
    sums_ref[1:2, :] = jnp.sum(dh2, axis=0, keepdims=True)


def project_back_kernel(chips, place, mine_ref, other_ref, w_ref, dz2_ref, *outs):
    core = place[1]
    rows = mine_ref.shape[0]
    width = outs[0].shape[1]
    dz2_ref[at_rows(core * rows, rows, rows), :] = mine_ref[...]
    dz2_ref[at_rows((1 - core) * rows, rows, rows), :] = other_ref[...]
    do = dot(dz2_ref[...], w_ref[...], 1, 1)
    for k in range(chips):
        outs[k][...] = do[:, k * width : (k + 1) * width].astype(BF)


def project_grad_kernel(chips, fsdp, place, *refs):
    att, refs = refs[:chips], refs[chips:]
    dz2_ref, refs = refs[0], refs[1:]
    outs, acc = refs[:fsdp], refs[fsdp]
    f = place[2]
    width = att[0].shape[1]
    piece = width // fsdp
    acc[...] = dot(jnp.concatenate([a[...] for a in att], axis=1), dz2_ref[...], 0, 0)
    for j in range(fsdp):
        for k in range(chips):
            at = k * width + (f ^ j) * piece
            outs[j][k] = acc[at_rows(at, piece, piece), :].astype(BF)


def backward_kernel(chips, place, *refs):
    q_ref, k_ref, v_ref, lse_ref = refs[:4]
    do_in, refs = refs[4 : 4 + chips], refs[4 + chips :]
    cos_ref, sin_ref, dp_ref, do_ref, dk_acc, dv_acc = refs
    z = place[0]
    length, width = q_ref.shape
    rows = length // (chips * CORES)
    for k in range(chips):
        at = (z ^ k) * (CORES * rows)
        do_ref[at_rows(at, CORES * rows, CORES * rows), :] = do_in[k][...]
    heads = width // HD
    block = min(256, length)
    scaling = HD ** (-0.5)
    dk_acc[...] = jnp.zeros_like(dk_acc)
    dv_acc[...] = jnp.zeros_like(dv_acc)
    for at in range(0, length, block):
        here, upto = pl.ds(at, block), pl.ds(0, at + block)
        q, do, k, v = q_ref[here, :], do_ref[here, :], k_ref[upto, :], v_ref[upto, :]
        dq = jnp.zeros((block, width), F32)
        for head in range(heads):
            qh, doh = head_lanes(q, head), head_lanes(do, head)
            lse = lse_ref[here, head * HD : head * HD + 1]
            scores = causal(dot(qh, k, 1, 1) * scaling, at)
            probs = jnp.exp(scores - lse)
            dprobs = dot(doh, v, 1, 1)
            delta = jnp.sum(probs * dprobs, axis=-1, keepdims=True)
            dscores = (probs * (dprobs - delta)).astype(BF)
            dq = dq + head_lanes(dot(dscores, k, 1, 0), head)
            dk_acc[upto, :] += dot(dscores, qh, 0, 0)
            dv_acc[upto, :] += dot(probs.astype(BF), doh, 0, 0)
        dq = rotate(dq * scaling, cos_ref[here, :], -sin_ref[here, :])
        dp_ref[here, :width] = dq.astype(BF)

    def finish(i, carry):
        here = at_rows(i * block, block, block)
        dk = rotate(dk_acc[here, :] * scaling, cos_ref[here, :], -sin_ref[here, :])
        dp_ref[here, width : 2 * width] = dk.astype(BF)
        dp_ref[here, 2 * width :] = dv_acc[here, :].astype(BF)
        return carry

    lax.fori_loop(0, length // block, finish, 0)


def small_rows(depth, lanes):
    return -(-depth // lanes), -(-(4 * -(-depth // lanes) + 1) // 16) * 16


def tree_sum(values):
    values = list(values)
    while len(values) > 1:
        values = [values[i] + values[i + 1] for i in range(0, len(values), 2)]
    return values[0]


def qkv_grad_kernel(chips, fsdp, place, h1_ref, u1_ref, dp_ref, w_ref, sums2_ref, *refs):
    outs, (dh_far, acc, dh_ref, dh_sem) = refs[:fsdp], refs[fsdp:]
    f = place[2]
    seq = chips * CORES
    depth, lanes = acc.shape
    piece = depth // (seq * fsdp)
    length = dp_ref.shape[0]
    acc[...] = dot(h1_ref[...], dp_ref[...], 0, 0)
    block = min(256, length)

    def dh_copy(i):
        here = at_rows(i * block, block, block)
        return pltpu.make_async_copy(dh_ref.at[here, :], dh_far.at[here, :], dh_sem.at[i])

    def dh_wait(i, carry):
        dh_copy(i).wait()
        return carry

    def sums(i, carry):
        gains, shifts, biases = carry
        here = at_rows(i * block, block, block)
        dh1 = dot(dp_ref[here, :], w_ref[...], 1, 1)
        dh_ref[here, :] = dh1.astype(BF)
        dh_copy(i).start()
        gains = gains + jnp.sum(dh1 * u1_ref[here, :].astype(F32), axis=0, keepdims=True)
        shifts = shifts + jnp.sum(dh1, axis=0, keepdims=True)
        biases = biases + jnp.sum(dp_ref[here, :].astype(F32), axis=0, keepdims=True)
        return (gains, shifts, biases)

    zeros = jnp.zeros((1, depth), F32)
    gains, shifts, biases = lax.fori_loop(
        0, length // block, sums, (zeros, zeros, jnp.zeros((1, lanes), F32))
    )
    per, count = small_rows(depth, lanes)
    small = []
    for v in (gains, shifts, sums2_ref[0:1, :], sums2_ref[1:2, :]):
        if per * lanes > depth:
            v = jnp.concatenate([v, jnp.zeros((1, per * lanes - depth), F32)], axis=1)
        small += [v[:, r * lanes : (r + 1) * lanes] for r in range(per)]
    small.append(biases)
    if count > len(small):
        small.append(jnp.zeros((count - len(small), lanes), F32))
    small = jnp.concatenate(small, axis=0)
    for j in range(fsdp):
        for s in range(seq):
            at = (s * fsdp + (f ^ j)) * piece
            outs[j][s * piece : (s + 1) * piece, :] = acc[at_rows(at, piece, piece), :].astype(BF)
        outs[j][seq * piece :, :] = small.astype(BF)
    lax.fori_loop(0, length // block, dh_wait, 0)


def qkv_line_kernel(chips, fsdp, place, *refs):
    got, refs = refs[:fsdp], refs[fsdp:]
    outs, acc = refs[:chips], refs[chips]
    z, core = place[0], place[1]
    count = outs[0].shape[0]
    total_rows = got[0].shape[0]
    small = total_rows - acc.shape[0]
    piece = acc.shape[0] // (chips * CORES)
    total = tree_sum([ref[...].astype(F32) for ref in got])
    acc[...] = total[: total_rows - small, :]
    for k in range(chips):
        for c in range(CORES):
            at = ((z ^ k) * CORES + (core ^ c)) * piece
            outs[k][c * piece : (c + 1) * piece, :] = acc[at_rows(at, piece, piece), :].astype(BF)
        outs[k][CORES * piece : count, :] = total[total_rows - small :, :].astype(BF)


def qkv_core_kernel(chips, piece, per, *refs):
    got, (keep_ref, give_ref) = refs[:chips], refs[chips:]
    lanes = keep_ref.shape[1]
    small = [ref[CORES * piece :, :].astype(F32) for ref in got]
    total = tree_sum(small)
    bias = [v[4 * per : 4 * per + 1, :] for v in small]
    rest = keep_ref.shape[0] - chips * piece - 4 * per - chips
    pad = [jnp.zeros((rest, lanes), F32)] if rest > 0 else []
    tail = jnp.concatenate([total[: 4 * per, :]] + bias + pad, axis=0)
    for c, ref in ((0, keep_ref), (1, give_ref)):
        for k in range(chips):
            ref[k * piece : (k + 1) * piece, :] = got[k][c * piece : (c + 1) * piece, :]
        ref[chips * piece :, :] = tail.astype(BF)


def qkv_final_kernel(chips, piece, per, place, keep_ref, got_ref, grad_ref, small_ref, bias_ref, acc):
    z, core = place[0], place[1]
    seq = chips * CORES
    lanes = keep_ref.shape[1]
    width = lanes // 3
    depth = small_ref.shape[1]
    at = chips * piece
    tails = [ref[at:, :].astype(F32) for ref in (keep_ref, got_ref)]
    total = tails[0] + tails[1]
    for c, ref in ((0, keep_ref), (1, got_ref)):
        for k in range(chips):
            src = (z ^ k) * CORES + (core ^ c)
            rows = ref[k * piece : (k + 1) * piece, :].astype(F32)
            bias = tails[c][4 * per + k : 4 * per + k + 1, :]
            for part in range(3):
                acc[part * seq + src] = rows[:, part * width : (part + 1) * width]
                bias_ref[pl.ds(part * seq + src, 1), :] = bias[:, part * width : (part + 1) * width]
    for i in range(3 * seq):
        grad_ref[:, i * width : (i + 1) * width] = acc[i]
    for v in range(4):
        for r in range(per):
            upto = min(lanes, depth - r * lanes)
            small_ref[v : v + 1, r * lanes : r * lanes + upto] = total[v * per + r : v * per + r + 1, :upto]


def norm1_back_kernel(dh1_ref, x_ref, gain, dz_ref, out_ref):
    u1, r1 = norm_parts(x_ref[...].astype(F32))
    out_ref[...] = dz_ref[...] + norm_back(dh1_ref[...].astype(F32), gain[...], u1, r1)


def on_device(
    seq,
    fsdp,
    tokens,
    ln1_gain,
    ln1_bias,
    qkv_weight,
    qkv_bias,
    out_weight,
    ln2_gain,
    ln2_bias,
    gate_up_weight,
    down_weight,
    out_grad,
):
    rows, depth = tokens.shape[1], tokens.shape[2]
    length = rows * seq
    chips = seq // CORES
    width = depth // seq
    piece = qkv_weight.shape[0]
    unit_piece = down_weight.shape[0]
    hidden = seq * unit_piece
    tiles = -(-2 * hidden // LANES)
    unit_pad = down_pad(unit_piece)
    me = lax.axis_index("seq")
    z, core, f = me // CORES, me % CORES, lax.axis_index("fsdp")
    place = jnp.stack([z, core, f]).astype(jnp.int32)
    steps, flips = range(1, chips), range(1, fsdp)
    by_place = jnp.arange(seq, dtype=jnp.int32) ^ me
    x_b = tokens.reshape(rows, depth)
    g_b = out_grad.reshape(rows, depth)
    row = lambda v: v.reshape(1, -1)

    tok_all = lax.all_gather(x_b, "seq", axis=0)

    w = qkv_weight.reshape(piece, 3, seq, width).transpose(2, 1, 0, 3)
    w = jnp.take(w, by_place, axis=0).reshape(chips, CORES * 3, piece, width)
    w = [w[0]] + [to_line(w[k], seq, k) for k in steps]
    cosines, sines = rotary_tables(length, width)
    give = after(jnp.stack([v[3:] for v in w]), cosines, sines)
    w = jnp.stack([jnp.stack([v[:3] for v in w]), to_core(give, seq)])
    w_parts = [w] + [to_fsdp(w, fsdp, j) for j in flips]

    gu = gate_up_weight.reshape(piece, 2, seq, fsdp, unit_piece).transpose(3, 0, 1, 2, 4)
    gu = gu.reshape(fsdp, piece, 2 * hidden)
    gu = jnp.pad(gu, ((0, 0), (0, 0), (0, tiles * LANES - 2 * hidden)))
    gu = gu.reshape(fsdp, piece, tiles, LANES).transpose(0, 2, 1, 3)
    pick = lambda v, j: lax.dynamic_index_in_dim(v, f ^ j, axis=0, keepdims=False)
    gu = after(gu, w)
    gu = [pick(gu, 0)] + [to_fsdp(pick(gu, j), fsdp, j) for j in flips]
    g_late = after(g_b, gu)
    g_parts = [g_b] + [to_fsdp(g_late, fsdp, j) for j in flips]

    o = after(out_weight, gu).reshape(piece, seq, width).transpose(1, 0, 2)
    o = [o] + [to_line(o, seq, k) for k in steps]
    down = jnp.pad(down_weight, ((0, unit_pad - unit_piece), (0, 0)))
    down = down.reshape(unit_pad, depth // LANES, LANES).transpose(1, 0, 2)
    feed = jnp.concatenate(
        [v.reshape(-1, LANES) for v in gu] + [down.reshape(-1, LANES)], axis=0
    )
    feed = lax.all_gather(feed, "seq", axis=0)

    outs = call(
        functools.partial(inputs_kernel, chips, fsdp),
        [shape((length, depth), BF)] * 2
        + [shape((length, width), BF)] * 3
        + [shape((depth, 3 * width), BF)],
        [
            pltpu.VMEM((depth, 3 * width), row_type(piece)),
            pltpu.VMEM((seq, rows, depth), BF),
            pltpu.SemaphoreType.DMA((seq,)),
            pltpu.VMEM((length, depth), BF),
            pltpu.VMEM((length, depth), BF),
            pltpu.SemaphoreType.DMA((seq,)),
            pltpu.SemaphoreType.DMA((seq,)),
        ],
        "attention_inputs",
        place,
        tok_all,
        *w_parts,
        row(ln1_gain),
        row(ln1_bias),
        qkv_bias.reshape(3 * seq, width),
        cosines,
        sines,
        far=(1,),
        far_out=(0, 1),
        vmem=16,
    )
    h1, u1, q, k_, v, w_qkv = outs
    o = jnp.stack(after(o, q))
    o_parts = [o] + [to_fsdp(o, fsdp, j) for j in flips]
    outs = call(
        functools.partial(attend_kernel, chips),
        [shape((length, width), F32)] + [shape((CORES * rows, width), BF)] * chips,
        [pltpu.VMEM((length, width), BF)],
        "attention_forward",
        place,
        after(q, g_parts),
        k_,
        v,
        flops=ATT,
        vmem=12,
    )
    lse, att = outs[0], outs[1:]
    att = [att[0]] + [to_line(att[k], seq, k) for k in steps]

    keep, give, w_out = call(
        functools.partial(project_kernel, chips, fsdp),
        [shape((rows, depth), F32)] * 2 + [shape((chips * width, depth), BF)],
        [
            pltpu.VMEM((chips * width, depth), row_type(piece)),
            pltpu.VMEM((CORES * rows, depth), F32),
            pltpu.VMEM((chips * width, depth), BF),
            pltpu.SemaphoreType.DMA(()),
        ],
        "out_projection",
        place,
        *att,
        *o_parts,
        flops=PROJECT,
        far_out=(2,),
        vmem=10,
    )
    z_res, h2 = call(
        norm2_kernel,
        [shape((rows, depth), F32), shape((rows, depth), BF)],
        [],
        "norm2",
        x_b,
        keep,
        to_core(give, seq),
        row(ln2_gain),
        row(ln2_bias),
        smem=False,
    )
    h2_parts = [h2] + [to_fsdp(h2, fsdp, j) for j in flips]

    tokens_here = fsdp * rows
    outs = call(
        functools.partial(feed_kernel, seq, fsdp, hidden, unit_piece),
        [shape((rows, depth), F32)]
        + [shape((rows, depth), BF)] * (fsdp - 1)
        + [
            shape((tokens_here, hidden), BF),
            shape((tokens_here, tiles * LANES), BF),
            shape((hidden, depth), BF),
            shape((tokens_here, depth), BF),
            shape((tokens_here, depth), BF),
        ],
        [
            pltpu.VMEM((hidden, depth), F32),
            pltpu.VMEM(feed.shape, BF),
            pltpu.SemaphoreType.DMA((seq,)),
            pltpu.SemaphoreType.DMA((fsdp,)),
            pltpu.VMEM((hidden, depth), BF),
            pltpu.SemaphoreType.DMA(()),
            pltpu.VMEM((depth, tiles * LANES), row_type(piece)),
        ]
        + ([] if row_type(piece) == BF else [pltpu.VMEM((depth, tiles * LANES), BF)]),
        "feed_forward",
        place,
        *h2_parts,
        *g_parts,
        feed,
        far=tuple(range(1 + fsdp, 2 + 2 * fsdp)),
        far_out=(fsdp + 2,),
        vmem=20,
    )
    dh2_keep, dh2_send = outs[0], outs[1:fsdp]
    m, dgu, w_down, h2_all, g_all = outs[fsdp:]
    dh2_got = [to_fsdp(v, fsdp, j) for j, v in zip(flips, dh2_send)]

    block = depth // seq
    lines = tiles * block + (depth // LANES) * unit_pad
    feed_grad = call(
        functools.partial(feed_grad_kernel, seq, hidden, unit_piece),
        shape((seq, lines, LANES), BF),
        [
            pltpu.VMEM((seq, tiles * block, LANES), BF),
            pltpu.VMEM((seq, lines - tiles * block, LANES), BF),
            pltpu.VMEM((hidden, 256), F32),
            pltpu.SemaphoreType.DMA((seq // max(1, 256 // block),)),
            pltpu.SemaphoreType.DMA((depth // 256,)),
        ],
        "feed_gradient",
        m,
        dgu,
        g_all,
        h2_all,
        smem=False,
        flops=FILL_LONG,
        vmem=16,
        far_out=(0,),
    )
    feed_raw = lax.psum_scatter(feed_grad, "seq", scatter_dimension=0)
    feed_total = feed_raw.astype(F32)

    ffn = call(
        functools.partial(down_kernel, fsdp),
        [shape((rows, depth), F32)] + [shape((rows, depth), BF)] * (fsdp - 1),
        [],
        "down_projection",
        m,
        w_down,
        smem=False,
        flops=FILL_SHORT,
    )
    dh2_got = after(dh2_got, feed_grad, ffn[0])

    dz, dz_b, sums2 = call(
        functools.partial(norm2_back_kernel, fsdp - 1),
        [shape((rows, depth), F32), shape((rows, depth), BF), shape((2, depth), F32)],
        [],
        "norm2_back",
        dh2_keep,
        *dh2_got,
        z_res,
        g_b,
        row(ln2_gain),
        smem=False,
    )
    outs = call(
        functools.partial(project_back_kernel, chips),
        [shape((CORES * rows, depth), BF)] + [shape((CORES * rows, width), BF)] * chips,
        [],
        "out_projection_back",
        place,
        dz_b,
        to_core(dz_b, seq),
        w_out,
    )
    dz2, do = outs[0], outs[1:]
    do = [do[0]] + [to_line(do[k], seq, k) for k in steps]


    outs = call(
        functools.partial(project_grad_kernel, chips, fsdp),
        [shape((chips, piece, depth), BF)] * fsdp,
        [pltpu.VMEM((chips * width, depth), F32)],
        "out_projection_gradient",
        place,
        *att,
        dz2,
    )
    o_blocks = outs
    ffn_late = after(ffn, dz_b)
    ffn_got = [to_fsdp(ffn_late[j], fsdp, j) for j in flips]
    do = after(do, outs[0], ffn_got)

    dp = call(
        functools.partial(backward_kernel, chips),
        shape((length, 3 * width), BF),
        [
            pltpu.VMEM((length, width), BF),
            pltpu.VMEM((length, width), F32),
            pltpu.VMEM((length, width), F32),
        ],
        "attention_backward",
        place,
        q,
        k_,
        v,
        lse,
        *do,
        cosines,
        sines,
        flops=LONG,
        vmem=12,
    )
    lanes = 3 * width
    per, count = small_rows(depth, lanes)
    blocks = call(
        functools.partial(qkv_grad_kernel, chips, fsdp),
        [shape((seq * piece + count, lanes), BF)] * fsdp + [shape((length, depth), BF)],
        [
            pltpu.VMEM((depth, lanes), F32),
            pltpu.VMEM((length, depth), BF),
            pltpu.SemaphoreType.DMA((length // min(256, length),)),
        ],
        "qkv_gradient",
        place,
        h1,
        u1,
        dp,
        w_qkv,
        sums2,
        flops=FILL_LAST,
        vmem=12,
        far_out=(fsdp,),
    )
    blocks, dh1 = blocks[:fsdp], blocks[fsdp]
    line_in = [blocks[0]] + [to_fsdp(blocks[j], fsdp, j) for j in flips]
    blocks = call(
        functools.partial(qkv_line_kernel, chips, fsdp),
        [shape((CORES * piece + count, lanes), BF)] * chips,
        [pltpu.VMEM((seq * piece, lanes), F32)],
        "qkv_gradient_line",
        place,
        *line_in,
    )
    o_late = after(o_blocks, blocks[0])
    total = o_blocks[0].astype(F32)
    for j in flips:
        total = total + to_fsdp(o_late[j], fsdp, j).astype(F32)
    dh1 = gate(dh1, feed_raw, blocks[0])
    block_out = z_res + ffn[0]
    for v in ffn_got:
        block_out = block_out + v.astype(F32)
    block_out = block_out.astype(BF)
    dh1 = lax.psum_scatter(dh1, "seq", scatter_dimension=0, tiled=True)
    blocks = [blocks[0]] + [to_line(blocks[k], seq, k) for k in steps]
    tail = -(-(4 * per + chips) // 16) * 16
    keep, give = call(
        functools.partial(qkv_core_kernel, chips, piece, per),
        [shape((chips * piece + tail, lanes), BF)] * 2,
        [],
        "qkv_gradient_core",
        *blocks,
        smem=False,
    )
    qkv_grad, small, bias_grad = call(
        functools.partial(qkv_final_kernel, chips, piece, per),
        [
            shape((piece, 3 * depth), F32),
            shape((4, depth), F32),
            shape((3 * seq, width), F32),
        ],
        [pltpu.VMEM((3 * seq, piece, width), F32)],
        "qkv_gradient_final",
        place,
        keep,
        to_core(give, seq),
    )
    input_grad = call(
        norm1_back_kernel,
        shape((rows, depth), F32),
        [],
        "norm1_back",
        dh1,
        x_b,
        row(ln1_gain),
        dz,
        smem=False,
    )

    down_grad = feed_total[tiles * block :].reshape(depth // LANES, unit_pad, LANES)
    down_grad = down_grad[:, :unit_piece].transpose(1, 0, 2).reshape(unit_piece, depth)
    gu = feed_total[: tiles * block].astype(BF).reshape(tiles, fsdp, piece, LANES)
    gu = gu.transpose(1, 2, 0, 3).reshape(fsdp, piece, tiles * LANES)[:, :, : 2 * hidden]
    gu_got = [pick(gu, 0)] + [to_fsdp(pick(gu, j), fsdp, j) for j in flips]
    gu = jnp.stack(gu_got)
    order = jnp.arange(fsdp, dtype=jnp.int32) ^ f
    gu = jnp.take(gu, order, axis=0)
    gu = gu.reshape(fsdp, piece, 2, seq, unit_piece).transpose(1, 2, 3, 0, 4)
    gu_grad = gu.reshape(piece, 2 * seq * fsdp * unit_piece).astype(F32)


    out_w_grad = total[0]
    for k in steps:
        out_w_grad = out_w_grad + to_line(total[k].astype(BF), seq, k).astype(F32)

    return (
        block_out.reshape(1, rows, depth),
        input_grad.reshape(1, rows, depth),
        small[0],
        small[1],
        qkv_grad,
        bias_grad.reshape(3 * depth),
        out_w_grad,
        small[2],
        small[3],
        gu_grad,
        down_grad,
    )


def solution(mesh):
    seq, fsdp = mesh.shape["seq"], mesh.shape["fsdp"]
    split = P(("seq", "fsdp"), None)
    toks = P("fsdp", "seq", None)

    def step(*args):
        return on_device(seq, fsdp, *args)

    return jax.shard_map(
        step,
        mesh=mesh,
        in_specs=(toks, P(), P(), split, P(), split, P(), P(), split, split, toks),
        out_specs=(toks, toks, P(), P(), split, P(), split, P(), P(), split, split),
        check_vma=False,
    )
```

```python
import functools

import jax
import jax.numpy as jnp
from jax import lax
from jax.experimental import pallas as pl
from jax.experimental.pallas import tpu as pltpu
from jax.sharding import PartitionSpec as P

H = 16
HD = 64
ROT = 16
EPS = 1e-05
BF = jnp.bfloat16
F32 = jnp.float32
CORES = 2
LANES = 128
ATT = 10_000_000_000
FILL_SHORT = 4_000_000_000
FILL_LONG = 8_000_000_000
FILL_LAST = 10_000_000_000
PROJECT = 20_000_000_000
LONG = 20_000_000_000
MIB = 1024 * 1024


def to_core(value, seq):
    return lax.ppermute(value, "seq", [(i, i ^ 1) for i in range(seq)])


def to_line(value, seq, step):
    return lax.ppermute(value, "seq", [(i, i ^ (CORES * step)) for i in range(seq)])


def to_fsdp(value, fsdp, flip):
    return lax.ppermute(value, "fsdp", [(i, i ^ flip) for i in range(fsdp)])


def after(values, *earlier):
    flat, tree = jax.tree.flatten(values)
    held = lax.optimization_barrier((flat, earlier))[0]
    return jax.tree.unflatten(tree, held)


def call(body, out_shape, scratch, name, *args, smem=True, flops=1_000_000_000, vmem=8, far=(), far_out=()):
    spaces = lambda count, hbm: [
        pl.BlockSpec(memory_space=pltpu.HBM if i in hbm else pltpu.VMEM) for i in range(count)
    ]
    specs = spaces(len(args), far)
    args = [
        pltpu.with_memory_space_constraint(a, pltpu.HBM) if i in far else a
        for i, a in enumerate(args)
    ]
    alone = not isinstance(out_shape, (list, tuple))
    outs = [out_shape] if alone else list(out_shape)
    outs = [pltpu.HBM(o.shape, o.dtype) if i in far_out else o for i, o in enumerate(outs)]
    out_shape = outs[0] if alone else outs
    out_specs = spaces(1 if alone else len(out_shape), far_out)
    if smem:
        specs[0] = pl.BlockSpec(memory_space=pltpu.SMEM)
    return pl.pallas_call(
        body,
        out_shape=out_shape,
        in_specs=specs,
        out_specs=out_specs[0] if alone else out_specs,
        scratch_shapes=scratch,
        compiler_params=pltpu.CompilerParams(vmem_limit_bytes=vmem * MIB),
        cost_estimate=pl.CostEstimate(flops=flops, transcendentals=0, bytes_accessed=1000000),
        name=name,
    )(*args)


def gate_kernel(*refs):
    pltpu.touch(refs[-1])


def gate(value, *earlier):
    whole = pl.BlockSpec(memory_space=pl.ANY)
    return pl.pallas_call(
        gate_kernel,
        out_shape=shape(value.shape, value.dtype),
        in_specs=[whole] * (1 + len(earlier)),
        out_specs=whole,
        input_output_aliases={0: 0},
        cost_estimate=pl.CostEstimate(flops=1000, transcendentals=0, bytes_accessed=1000),
        name="gate",
    )(value, *earlier)


def shape(dims, dtype):
    return jax.ShapeDtypeStruct(dims, dtype)


def row_type(step):
    return BF if step % 16 == 0 else F32


def at_rows(start, count, step):
    return pl.ds(pl.multiple_of(start, step), count)


def dot(left, right, left_dim, right_dim):
    return lax.dot_general(
        left, right, (((left_dim,), (right_dim,)), ((), ())), preferred_element_type=F32
    )


def rotary_tables(length, width):
    half = ROT // 2
    lane = jnp.arange(width, dtype=jnp.int32) % HD
    frequency = 10000.0 ** (-2.0 * (lane % half).astype(F32) / ROT)
    angles = jnp.arange(length, dtype=jnp.int32).astype(F32)[:, None] * frequency[None, :]
    rotated = (lane < ROT)[None, :]
    sines = jnp.where((lane < half)[None, :], -jnp.sin(angles), jnp.sin(angles))
    return (jnp.where(rotated, jnp.cos(angles), 1.0), jnp.where(rotated, sines, 0.0))


def lane_roll(value, shift):
    width = value.shape[1]
    if width % LANES == 0:
        return pltpu.roll(value, shift % width, 1)
    return jnp.roll(value, shift, axis=1)


def rotate(value, cosines, sines):
    half = ROT // 2
    lane = lax.broadcasted_iota(jnp.int32, value.shape, 1) % HD
    partner = jnp.where(lane < half, lane_roll(value, -half), lane_roll(value, half))
    return value * cosines + partner * sines


def head_lanes(value, head):
    lane = lax.broadcasted_iota(jnp.int32, value.shape, 1)
    return jnp.where(lane // HD == head, value, jnp.zeros_like(value))


def causal(scores, first_row):
    rows = first_row + lax.broadcasted_iota(jnp.int32, scores.shape, 0)
    cols = lax.broadcasted_iota(jnp.int32, scores.shape, 1)
    return jnp.where(rows >= cols, scores, -jnp.inf)


def norm_parts(values):
    mean = jnp.mean(values, axis=-1, keepdims=True)
    centred = values - mean
    inv = lax.rsqrt(jnp.mean(centred * centred, axis=-1, keepdims=True) + EPS)
    return (centred * inv, inv)


def norm_back(grad, gain, unit, inv):
    scaled = grad * gain
    return inv * (
        scaled
        - jnp.mean(scaled, axis=-1, keepdims=True)
        - unit * jnp.mean(scaled * unit, axis=-1, keepdims=True)
    )


def inputs_kernel(chips, fsdp, place, *refs):
    refs = list(refs)
    tok_ref, parts, refs = refs[0], refs[1 : 1 + fsdp], refs[1 + fsdp :]
    gain, bias, qb, cos_ref, sin_ref, h1_far, u1_far, q_ref, k_ref, v_ref, w_ref = refs[:11]
    w_rows, tok_in, tok_sem, h1_ref, u1_ref, h1_sem, u1_sem = refs[11:]

    def tok_copy(s):
        return pltpu.make_async_copy(tok_ref.at[s], tok_in.at[s], tok_sem.at[s])

    for s in range(chips * CORES):
        tok_copy(s).start()
    z, core, f = place[0], place[1], place[2]
    length, width = q_ref.shape
    rows = tok_ref.shape[1]
    piece = parts[0].shape[3]
    seq = chips * CORES
    for j in range(fsdp):
        for k in range(chips):
            for c in range(CORES):
                at = (((z ^ k) * CORES + (core ^ c)) * fsdp + (f ^ j)) * piece
                for t in range(3):
                    w_rows[at_rows(at, piece, piece), t * width : (t + 1) * width] = parts[j][
                        c, k, t
                    ].astype(w_rows.dtype)
    w_ref[...] = w_rows[...].astype(BF)

    def norm(s, carry):
        tok_copy(s).wait()
        u1, _ = norm_parts(tok_in[s].astype(F32))
        here = at_rows(s * rows, rows, rows)
        u1_ref[here, :] = u1.astype(BF)
        h1_ref[here, :] = (u1 * gain[...] + bias[...]).astype(BF)
        u1_copy(s).start()
        h1_copy(s).start()
        return carry

    def h1_copy(s):
        here = at_rows(s * rows, rows, rows)
        return pltpu.make_async_copy(h1_ref.at[here, :], h1_far.at[here, :], h1_sem.at[s])

    def u1_copy(s):
        here = at_rows(s * rows, rows, rows)
        return pltpu.make_async_copy(u1_ref.at[here, :], u1_far.at[here, :], u1_sem.at[s])

    def finish(s, carry):
        u1_copy(s).wait()
        h1_copy(s).wait()
        return carry

    lax.fori_loop(0, seq, norm, 0)
    me = z * CORES + core
    biases = [qb[pl.ds(part * seq + me, 1), :] for part in range(3)]
    block = min(256, length)

    def project(i, carry):
        here = at_rows(i * block, block, block)
        p = dot(h1_ref[here, :], w_ref[...], 1, 0)
        cosines, sines = cos_ref[here, :], sin_ref[here, :]
        q_ref[here, :] = rotate(p[:, :width] + biases[0], cosines, sines).astype(BF)
        k_ref[here, :] = rotate(p[:, width : 2 * width] + biases[1], cosines, sines).astype(BF)
        v_ref[here, :] = (p[:, 2 * width :] + biases[2]).astype(BF)
        return carry

    lax.fori_loop(0, length // block, project, 0)
    lax.fori_loop(0, seq, finish, 0)


def attend_kernel(chips, place, q_ref, k_ref, v_ref, lse_ref, *refs):
    att_out, att_ref = refs[:chips], refs[chips]
    z = place[0]
    length, width = q_ref.shape
    rows = length // (chips * CORES)
    block = min(256, length)
    scaling = HD ** (-0.5)
    for at in range(0, length, block):
        here, upto = pl.ds(at, block), pl.ds(0, at + block)
        q, k, v = q_ref[here, :], k_ref[upto, :], v_ref[upto, :]
        att = jnp.zeros((block, width), F32)
        totals = []
        for head in range(width // HD):
            scores = causal(dot(head_lanes(q, head), k, 1, 1) * scaling, at)
            top = jnp.max(scores, axis=-1, keepdims=True)
            exponent = jnp.exp(scores - top)
            total = jnp.sum(exponent, axis=-1, keepdims=True)
            weights = (exponent * (1.0 / total)).astype(BF)
            att = att + head_lanes(dot(weights, v, 1, 0), head)
            totals.append(jnp.broadcast_to(top + jnp.log(total), (block, HD)))
        att_ref[here, :] = att.astype(BF)
        lse_ref[here, :] = jnp.concatenate(totals, axis=1)
    for k in range(chips):
        at = (z ^ k) * (CORES * rows)
        att_out[k][...] = att_ref[at_rows(at, CORES * rows, CORES * rows), :]


def project_kernel(chips, fsdp, place, *refs):
    refs = list(refs)
    att, refs = refs[:chips], refs[chips:]
    parts, refs = refs[:fsdp], refs[fsdp:]
    keep_ref, give_ref, w_far, w_rows, res, w_ref, w_sem = refs
    core, f = place[1], place[2]
    rows = keep_ref.shape[0]
    width = att[0].shape[1]
    piece = parts[0].shape[2]
    for j in range(fsdp):
        for k in range(chips):
            at = k * width + (f ^ j) * piece
            for t in range(parts[j].shape[1]):
                w_rows[at_rows(at, piece, piece), t * width : (t + 1) * width] = parts[j][
                    k, t
                ].astype(w_rows.dtype)
    w_ref[...] = w_rows[...].astype(BF)
    copy = pltpu.make_async_copy(w_ref, w_far, w_sem)
    copy.start()
    res[...] = dot(jnp.concatenate([a[...] for a in att], axis=1), w_ref[...], 1, 0)
    keep_ref[...] = res[at_rows(core * rows, rows, rows), :]
    give_ref[...] = res[at_rows((1 - core) * rows, rows, rows), :]
    copy.wait()


def norm2_kernel(x_ref, keep_ref, got_ref, gain, bias, z_ref, h2_ref):
    z = x_ref[...].astype(F32) + (keep_ref[...] + got_ref[...])
    z_ref[...] = z
    u2, _ = norm_parts(z)
    h2_ref[...] = (u2 * gain[...] + bias[...]).astype(BF)


def feed_kernel(seq, fsdp, hidden, unit_piece, place, *refs):
    refs = list(refs)
    h2, refs = refs[:fsdp], refs[fsdp:]
    g, refs = refs[:fsdp], refs[fsdp:]
    feed_ref, keep_ref, refs = refs[0], refs[1], refs[2:]
    sends, refs = refs[: fsdp - 1], refs[fsdp - 1 :]
    m_ref, dgu_ref, wd_far, h2_all, g_all, down_rows, feed_in, feed_sem, g_sem, wd_out, wd_sem, gu_rows = refs[:12]
    w_gu = refs[12] if len(refs) > 12 else gu_rows
    f = place[2]
    rows, depth = keep_ref.shape
    copies = [
        pltpu.make_async_copy(feed_ref.at[s], feed_in.at[s], feed_sem.at[s]) for s in range(seq)
    ]
    for copy in copies:
        copy.start()
    g_copies = [
        pltpu.make_async_copy(g[j], g_all.at[pl.ds(j * rows, rows), :], g_sem.at[j])
        for j in range(fsdp)
    ]
    for copy in g_copies:
        copy.start()
    for j in range(fsdp):
        h2_all[j * rows : (j + 1) * rows, :] = h2[j][...]
    tiles = gu_rows.shape[1] // LANES
    piece = depth // (seq * fsdp)
    unit_pad = down_pad(unit_piece)
    first = fsdp * tiles * piece

    def gather(s, carry):
        pltpu.make_async_copy(feed_ref.at[s], feed_in.at[s], feed_sem.at[s]).wait()
        for j in range(fsdp):
            at = at_rows((s * fsdp + (f ^ j)) * piece, piece, piece)
            for t in range(tiles):
                tile = feed_in[s, pl.ds((j * tiles + t) * piece, piece), :]
                gu_rows[at, t * LANES : (t + 1) * LANES] = tile.astype(gu_rows.dtype)
        return carry

    def gather_down(s, at):
        for t in range(0, depth // LANES, 2):
            tile = feed_in[s, pl.ds(first + t * unit_pad, 2 * unit_pad), :].astype(F32)
            for q in range(2):
                cols = slice((t + q) * LANES, (t + q + 1) * LANES)
                down_rows[at, cols] = tile[q * unit_pad : q * unit_pad + unit_piece, :]

    lax.fori_loop(0, seq, gather, 0)
    if unit_piece % 8 == 0:

        def gather_units(s, carry):
            gather_down(s, at_rows(s * unit_piece, unit_piece, 8))
            return carry

        lax.fori_loop(0, seq, gather_units, 0)
    else:
        for s in range(seq):
            gather_down(s, pl.ds(s * unit_piece, unit_piece))
    wd_ref = wd_out
    wd_ref[...] = down_rows[...].astype(BF)
    wd_copy = pltpu.make_async_copy(wd_ref, wd_far, wd_sem)
    wd_copy.start()
    if w_gu is not gu_rows:
        w_gu[...] = gu_rows[...].astype(BF)
    for copy in g_copies:
        copy.wait()
    if dgu_ref.shape[1] > 2 * hidden:
        dgu_ref[...] = jnp.zeros_like(dgu_ref)
    chunks = 2

    def work(i, carry):
        here = at_rows(i * (chunks * rows), chunks * rows, chunks * rows)
        gu = dot(h2_all[here, :], w_gu[...], 1, 0)
        gate, up = gu[:, :hidden], gu[:, hidden : 2 * hidden]
        dm = dot(g_all[here, :], wd_ref[...], 1, 1)
        sig = 1.0 / (1.0 + jnp.exp(-gate))
        silu = gate * sig
        m_ref[here, :] = (silu * up).astype(BF)
        dgu_ref[here, :hidden] = (dm * up * sig * (1.0 + gate * (1.0 - sig))).astype(BF)
        dgu_ref[here, hidden : 2 * hidden] = (dm * silu).astype(BF)
        dh2 = dot(dgu_ref[here, :], w_gu[...], 1, 1)
        for j in range(fsdp):

            @pl.when(i == j // chunks)
            def _():
                part = dh2[(j % chunks) * rows : (j % chunks + 1) * rows, :]
                if j == 0:
                    keep_ref[...] = part
                else:
                    sends[j - 1][...] = part.astype(BF)

        return carry

    lax.fori_loop(0, fsdp // chunks, work, 0)
    wd_copy.wait()


def down_kernel(fsdp, m_ref, wd_ref, keep_ref, *sends):
    rows = keep_ref.shape[0]
    for j in range(fsdp):
        part = dot(m_ref[j * rows : (j + 1) * rows, :], wd_ref[...], 1, 0)
        if j == 0:
            keep_ref[...] = part
        else:
            sends[j - 1][...] = part.astype(BF)


def down_pad(unit_piece):
    return unit_piece if unit_piece % 8 == 0 else -(-unit_piece // 16) * 16


def feed_grad_kernel(seq, hidden, unit_piece, m_ref, dgu_ref, g_all, h2_all, out_ref, *refs):
    gu_out, down_out, down_acc, gu_sem, down_sem = refs
    depth = g_all.shape[1]
    tiles = dgu_ref.shape[1] // LANES
    block = depth // seq
    unit_pad = down_pad(unit_piece)
    pair = max(1, 256 // block)

    def gu_copy(i):
        return pltpu.make_async_copy(
            gu_out.at[pl.ds(i * pair, pair)],
            out_ref.at[pl.ds(i * pair, pair), pl.ds(0, tiles * block), :],
            gu_sem.at[i],
        )

    def down_copy(i):
        at = pl.multiple_of(i * 2 * unit_pad, 16)
        return pltpu.make_async_copy(
            down_out.at[:, pl.ds(at, 2 * unit_pad), :],
            out_ref.at[:, pl.ds(tiles * block + at, 2 * unit_pad), :],
            down_sem.at[i],
        )

    def gate_up(i, carry):
        cols = pl.ds(pl.multiple_of(i * (pair * block), pair * block), pair * block)
        grad = dot(h2_all[:, cols], dgu_ref[...], 0, 0).astype(BF)
        for s in range(pair):
            for t in range(tiles):
                gu_out[i * pair + s, t * block : (t + 1) * block, :] = grad[
                    s * block : (s + 1) * block, t * LANES : (t + 1) * LANES
                ]
        gu_copy(i).start()
        return carry

    lax.fori_loop(0, seq // pair, gate_up, 0, unroll=True)

    def down(i, carry):
        cols = pl.ds(pl.multiple_of(i * 256, 256), 256)
        down_acc[...] = dot(m_ref[...], g_all[:, cols], 0, 0)
        for s in range(seq):
            both = []
            for t in range(2):
                both.append(
                    down_acc[s * unit_piece : (s + 1) * unit_piece, t * LANES : (t + 1) * LANES]
                )
                if unit_pad > unit_piece:
                    both.append(jnp.zeros((unit_pad - unit_piece, LANES), F32))
            rows = at_rows(i * (2 * unit_pad), 2 * unit_pad, 16)
            down_out[s, rows, :] = jnp.concatenate(both, axis=0).astype(BF)
        down_copy(i).start()
        return carry

    lax.fori_loop(0, depth // 256, down, 0, unroll=True)

    def finish_gu(i, carry):
        gu_copy(i).wait()
        return carry

    def finish_down(i, carry):
        down_copy(i).wait()
        return carry

    lax.fori_loop(0, seq // pair, finish_gu, 0)
    lax.fori_loop(0, depth // 256, finish_down, 0)


def norm2_back_kernel(count, *refs):
    keep_ref, got, refs = refs[0], refs[1 : 1 + count], refs[1 + count :]
    z_ref, g_ref, gain, dz_ref, dzb_ref, sums_ref = refs
    dh2 = keep_ref[...]
    for ref in got:
        dh2 = dh2 + ref[...].astype(F32)
    u2, r2 = norm_parts(z_ref[...])
    dz = g_ref[...].astype(F32) + norm_back(dh2, gain[...], u2, r2)
    dz_ref[...] = dz
    dzb_ref[...] = dz.astype(BF)
    sums_ref[0:1, :] = jnp.sum(dh2 * u2, axis=0, keepdims=True)
    sums_ref[1:2, :] = jnp.sum(dh2, axis=0, keepdims=True)


def project_back_kernel(chips, place, mine_ref, other_ref, w_ref, dz2_ref, *outs):
    core = place[1]
    rows = mine_ref.shape[0]
    width = outs[0].shape[1]
    dz2_ref[at_rows(core * rows, rows, rows), :] = mine_ref[...]
    dz2_ref[at_rows((1 - core) * rows, rows, rows), :] = other_ref[...]
    do = dot(dz2_ref[...], w_ref[...], 1, 1)
    for k in range(chips):
        outs[k][...] = do[:, k * width : (k + 1) * width].astype(BF)


def project_grad_kernel(chips, fsdp, place, *refs):
    att, refs = refs[:chips], refs[chips:]
    dz2_ref, refs = refs[0], refs[1:]
    outs, acc = refs[:fsdp], refs[fsdp]
    f = place[2]
    width = att[0].shape[1]
    piece = width // fsdp
    acc[...] = dot(jnp.concatenate([a[...] for a in att], axis=1), dz2_ref[...], 0, 0)
    for j in range(fsdp):
        for k in range(chips):
            at = k * width + (f ^ j) * piece
            outs[j][k] = acc[at_rows(at, piece, piece), :].astype(BF)


def backward_kernel(chips, place, *refs):
    q_ref, k_ref, v_ref, lse_ref = refs[:4]
    do_in, refs = refs[4 : 4 + chips], refs[4 + chips :]
    cos_ref, sin_ref, dp_ref, do_ref, dk_acc, dv_acc = refs
    z = place[0]
    length, width = q_ref.shape
    rows = length // (chips * CORES)
    for k in range(chips):
        at = (z ^ k) * (CORES * rows)
        do_ref[at_rows(at, CORES * rows, CORES * rows), :] = do_in[k][...]
    heads = width // HD
    block = min(256, length)
    scaling = HD ** (-0.5)
    dk_acc[...] = jnp.zeros_like(dk_acc)
    dv_acc[...] = jnp.zeros_like(dv_acc)
    for at in range(0, length, block):
        here, upto = pl.ds(at, block), pl.ds(0, at + block)
        q, do, k, v = q_ref[here, :], do_ref[here, :], k_ref[upto, :], v_ref[upto, :]
        dq = jnp.zeros((block, width), F32)
        for head in range(heads):
            qh, doh = head_lanes(q, head), head_lanes(do, head)
            lse = lse_ref[here, head * HD : head * HD + 1]
            scores = causal(dot(qh, k, 1, 1) * scaling, at)
            probs = jnp.exp(scores - lse)
            dprobs = dot(doh, v, 1, 1)
            delta = jnp.sum(probs * dprobs, axis=-1, keepdims=True)
            dscores = (probs * (dprobs - delta)).astype(BF)
            dq = dq + head_lanes(dot(dscores, k, 1, 0), head)
            dk_acc[upto, :] += dot(dscores, qh, 0, 0)
            dv_acc[upto, :] += dot(probs.astype(BF), doh, 0, 0)
        dq = rotate(dq * scaling, cos_ref[here, :], -sin_ref[here, :])
        dp_ref[here, :width] = dq.astype(BF)

    def finish(i, carry):
        here = at_rows(i * block, block, block)
        dk = rotate(dk_acc[here, :] * scaling, cos_ref[here, :], -sin_ref[here, :])
        dp_ref[here, width : 2 * width] = dk.astype(BF)
        dp_ref[here, 2 * width :] = dv_acc[here, :].astype(BF)
        return carry

    lax.fori_loop(0, length // block, finish, 0)


def small_rows(depth, lanes):
    return -(-depth // lanes), -(-(4 * -(-depth // lanes) + 1) // 16) * 16


def tree_sum(values):
    values = list(values)
    while len(values) > 1:
        values = [values[i] + values[i + 1] for i in range(0, len(values), 2)]
    return values[0]


def qkv_grad_kernel(chips, fsdp, place, h1_ref, u1_ref, dp_ref, w_ref, sums2_ref, *refs):
    outs, (dh_far, acc, dh_ref, dh_sem) = refs[:fsdp], refs[fsdp:]
    f = place[2]
    seq = chips * CORES
    depth, lanes = acc.shape
    piece = depth // (seq * fsdp)
    length = dp_ref.shape[0]
    acc[...] = dot(h1_ref[...], dp_ref[...], 0, 0)
    block = min(256, length)

    def dh_copy(i):
        here = at_rows(i * block, block, block)
        return pltpu.make_async_copy(dh_ref.at[here, :], dh_far.at[here, :], dh_sem.at[i])

    def dh_wait(i, carry):
        dh_copy(i).wait()
        return carry

    def sums(i, carry):
        gains, shifts, biases = carry
        here = at_rows(i * block, block, block)
        dh1 = dot(dp_ref[here, :], w_ref[...], 1, 1)
        dh_ref[here, :] = dh1.astype(BF)
        dh_copy(i).start()
        gains = gains + jnp.sum(dh1 * u1_ref[here, :].astype(F32), axis=0, keepdims=True)
        shifts = shifts + jnp.sum(dh1, axis=0, keepdims=True)
        biases = biases + jnp.sum(dp_ref[here, :].astype(F32), axis=0, keepdims=True)
        return (gains, shifts, biases)

    zeros = jnp.zeros((1, depth), F32)
    gains, shifts, biases = lax.fori_loop(
        0, length // block, sums, (zeros, zeros, jnp.zeros((1, lanes), F32))
    )
    per, count = small_rows(depth, lanes)
    small = []
    for v in (gains, shifts, sums2_ref[0:1, :], sums2_ref[1:2, :]):
        if per * lanes > depth:
            v = jnp.concatenate([v, jnp.zeros((1, per * lanes - depth), F32)], axis=1)
        small += [v[:, r * lanes : (r + 1) * lanes] for r in range(per)]
    small.append(biases)
    if count > len(small):
        small.append(jnp.zeros((count - len(small), lanes), F32))
    small = jnp.concatenate(small, axis=0)
    for j in range(fsdp):
        for s in range(seq):
            at = (s * fsdp + (f ^ j)) * piece
            outs[j][s * piece : (s + 1) * piece, :] = acc[at_rows(at, piece, piece), :].astype(BF)
        outs[j][seq * piece :, :] = small.astype(BF)
    lax.fori_loop(0, length // block, dh_wait, 0)


def qkv_line_kernel(chips, fsdp, place, *refs):
    got, refs = refs[:fsdp], refs[fsdp:]
    outs, acc = refs[:chips], refs[chips]
    z, core = place[0], place[1]
    count = outs[0].shape[0]
    total_rows = got[0].shape[0]
    small = total_rows - acc.shape[0]
    piece = acc.shape[0] // (chips * CORES)
    total = tree_sum([ref[...].astype(F32) for ref in got])
    acc[...] = total[: total_rows - small, :]
    for k in range(chips):
        for c in range(CORES):
            at = ((z ^ k) * CORES + (core ^ c)) * piece
            outs[k][c * piece : (c + 1) * piece, :] = acc[at_rows(at, piece, piece), :].astype(BF)
        outs[k][CORES * piece : count, :] = total[total_rows - small :, :].astype(BF)


def qkv_core_kernel(chips, piece, per, *refs):
    got, (keep_ref, give_ref) = refs[:chips], refs[chips:]
    lanes = keep_ref.shape[1]
    small = [ref[CORES * piece :, :].astype(F32) for ref in got]
    total = tree_sum(small)
    bias = [v[4 * per : 4 * per + 1, :] for v in small]
    rest = keep_ref.shape[0] - chips * piece - 4 * per - chips
    pad = [jnp.zeros((rest, lanes), F32)] if rest > 0 else []
    tail = jnp.concatenate([total[: 4 * per, :]] + bias + pad, axis=0)
    for c, ref in ((0, keep_ref), (1, give_ref)):
        for k in range(chips):
            ref[k * piece : (k + 1) * piece, :] = got[k][c * piece : (c + 1) * piece, :]
        ref[chips * piece :, :] = tail.astype(BF)


def qkv_final_kernel(chips, piece, per, place, keep_ref, got_ref, grad_ref, small_ref, bias_ref, acc):
    z, core = place[0], place[1]
    seq = chips * CORES
    lanes = keep_ref.shape[1]
    width = lanes // 3
    depth = small_ref.shape[1]
    at = chips * piece
    tails = [ref[at:, :].astype(F32) for ref in (keep_ref, got_ref)]
    total = tails[0] + tails[1]
    for c, ref in ((0, keep_ref), (1, got_ref)):
        for k in range(chips):
            src = (z ^ k) * CORES + (core ^ c)
            rows = ref[k * piece : (k + 1) * piece, :].astype(F32)
            bias = tails[c][4 * per + k : 4 * per + k + 1, :]
            for part in range(3):
                acc[part * seq + src] = rows[:, part * width : (part + 1) * width]
                bias_ref[pl.ds(part * seq + src, 1), :] = bias[:, part * width : (part + 1) * width]
    for i in range(3 * seq):
        grad_ref[:, i * width : (i + 1) * width] = acc[i]
    for v in range(4):
        for r in range(per):
            upto = min(lanes, depth - r * lanes)
            small_ref[v : v + 1, r * lanes : r * lanes + upto] = total[v * per + r : v * per + r + 1, :upto]


def norm1_back_kernel(dh1_ref, x_ref, gain, dz_ref, out_ref):
    u1, r1 = norm_parts(x_ref[...].astype(F32))
    out_ref[...] = dz_ref[...] + norm_back(dh1_ref[...].astype(F32), gain[...], u1, r1)


def on_device(
    seq,
    fsdp,
    tokens,
    ln1_gain,
    ln1_bias,
    qkv_weight,
    qkv_bias,
    out_weight,
    ln2_gain,
    ln2_bias,
    gate_up_weight,
    down_weight,
    out_grad,
):
    rows, depth = tokens.shape[1], tokens.shape[2]
    length = rows * seq
    chips = seq // CORES
    width = depth // seq
    piece = qkv_weight.shape[0]
    unit_piece = down_weight.shape[0]
    hidden = seq * unit_piece
    tiles = -(-2 * hidden // LANES)
    unit_pad = down_pad(unit_piece)
    me = lax.axis_index("seq")
    z, core, f = me // CORES, me % CORES, lax.axis_index("fsdp")
    place = jnp.stack([z, core, f]).astype(jnp.int32)
    steps, flips = range(1, chips), range(1, fsdp)
    by_place = jnp.arange(seq, dtype=jnp.int32) ^ me
    x_b = tokens.reshape(rows, depth)
    g_b = out_grad.reshape(rows, depth)
    row = lambda v: v.reshape(1, -1)

    tok_all = lax.all_gather(x_b, "seq", axis=0)

    w = qkv_weight.reshape(piece, 3, seq, width).transpose(2, 1, 0, 3)
    w = jnp.take(w, by_place, axis=0).reshape(chips, CORES * 3, piece, width)
    w = [w[0]] + [to_line(w[k], seq, k) for k in steps]
    cosines, sines = rotary_tables(length, width)
    give = after(jnp.stack([v[3:] for v in w]), cosines, sines)
    w = jnp.stack([jnp.stack([v[:3] for v in w]), to_core(give, seq)])
    w_parts = [w] + [to_fsdp(w, fsdp, j) for j in flips]

    gu = gate_up_weight.reshape(piece, 2, seq, fsdp, unit_piece).transpose(3, 0, 1, 2, 4)
    gu = gu.reshape(fsdp, piece, 2 * hidden)
    gu = jnp.pad(gu, ((0, 0), (0, 0), (0, tiles * LANES - 2 * hidden)))
    gu = gu.reshape(fsdp, piece, tiles, LANES).transpose(0, 2, 1, 3)
    pick = lambda v, j: lax.dynamic_index_in_dim(v, f ^ j, axis=0, keepdims=False)
    gu = after(gu, w)
    gu = [pick(gu, 0)] + [to_fsdp(pick(gu, j), fsdp, j) for j in flips]
    g_late = after(g_b, gu)
    g_parts = [g_b] + [to_fsdp(g_late, fsdp, j) for j in flips]

    o = after(out_weight, gu).reshape(piece, seq, width).transpose(1, 0, 2)
    o = [o] + [to_line(o, seq, k) for k in steps]
    down = jnp.pad(down_weight, ((0, unit_pad - unit_piece), (0, 0)))
    down = down.reshape(unit_pad, depth // LANES, LANES).transpose(1, 0, 2)
    feed = jnp.concatenate(
        [v.reshape(-1, LANES) for v in gu] + [down.reshape(-1, LANES)], axis=0
    )
    feed = lax.all_gather(feed, "seq", axis=0)

    outs = call(
        functools.partial(inputs_kernel, chips, fsdp),
        [shape((length, depth), BF)] * 2
        + [shape((length, width), BF)] * 3
        + [shape((depth, 3 * width), BF)],
        [
            pltpu.VMEM((depth, 3 * width), row_type(piece)),
            pltpu.VMEM((seq, rows, depth), BF),
            pltpu.SemaphoreType.DMA((seq,)),
            pltpu.VMEM((length, depth), BF),
            pltpu.VMEM((length, depth), BF),
            pltpu.SemaphoreType.DMA((seq,)),
            pltpu.SemaphoreType.DMA((seq,)),
        ],
        "attention_inputs",
        place,
        tok_all,
        *w_parts,
        row(ln1_gain),
        row(ln1_bias),
        qkv_bias.reshape(3 * seq, width),
        cosines,
        sines,
        far=(1,),
        far_out=(0, 1),
        vmem=16,
    )
    h1, u1, q, k_, v, w_qkv = outs
    o = jnp.stack(after(o, q))
    o_parts = [o] + [to_fsdp(o, fsdp, j) for j in flips]
    outs = call(
        functools.partial(attend_kernel, chips),
        [shape((length, width), F32)] + [shape((CORES * rows, width), BF)] * chips,
        [pltpu.VMEM((length, width), BF)],
        "attention_forward",
        place,
        after(q, g_parts),
        k_,
        v,
        flops=ATT,
        vmem=12,
    )
    lse, att = outs[0], outs[1:]
    att = [att[0]] + [to_line(att[k], seq, k) for k in steps]

    keep, give, w_out = call(
        functools.partial(project_kernel, chips, fsdp),
        [shape((rows, depth), F32)] * 2 + [shape((chips * width, depth), BF)],
        [
            pltpu.VMEM((chips * width, depth), row_type(piece)),
            pltpu.VMEM((CORES * rows, depth), F32),
            pltpu.VMEM((chips * width, depth), BF),
            pltpu.SemaphoreType.DMA(()),
        ],
        "out_projection",
        place,
        *att,
        *o_parts,
        flops=PROJECT,
        far_out=(2,),
        vmem=10,
    )
    z_res, h2 = call(
        norm2_kernel,
        [shape((rows, depth), F32), shape((rows, depth), BF)],
        [],
        "norm2",
        x_b,
        keep,
        to_core(give, seq),
        row(ln2_gain),
        row(ln2_bias),
        smem=False,
    )
    h2_parts = [h2] + [to_fsdp(h2, fsdp, j) for j in flips]

    tokens_here = fsdp * rows
    outs = call(
        functools.partial(feed_kernel, seq, fsdp, hidden, unit_piece),
        [shape((rows, depth), F32)]
        + [shape((rows, depth), BF)] * (fsdp - 1)
        + [
            shape((tokens_here, hidden), BF),
            shape((tokens_here, tiles * LANES), BF),
            shape((hidden, depth), BF),
            shape((tokens_here, depth), BF),
            shape((tokens_here, depth), BF),
        ],
        [
            pltpu.VMEM((hidden, depth), F32),
            pltpu.VMEM(feed.shape, BF),
            pltpu.SemaphoreType.DMA((seq,)),
            pltpu.SemaphoreType.DMA((fsdp,)),
            pltpu.VMEM((hidden, depth), BF),
            pltpu.SemaphoreType.DMA(()),
            pltpu.VMEM((depth, tiles * LANES), row_type(piece)),
        ]
        + ([] if row_type(piece) == BF else [pltpu.VMEM((depth, tiles * LANES), BF)]),
        "feed_forward",
        place,
        *h2_parts,
        *g_parts,
        feed,
        far=tuple(range(1 + fsdp, 2 + 2 * fsdp)),
        far_out=(fsdp + 2,),
        vmem=20,
    )
    dh2_keep, dh2_send = outs[0], outs[1:fsdp]
    m, dgu, w_down, h2_all, g_all = outs[fsdp:]
    dh2_got = [to_fsdp(v, fsdp, j) for j, v in zip(flips, dh2_send)]

    block = depth // seq
    lines = tiles * block + (depth // LANES) * unit_pad
    feed_grad = call(
        functools.partial(feed_grad_kernel, seq, hidden, unit_piece),
        shape((seq, lines, LANES), BF),
        [
            pltpu.VMEM((seq, tiles * block, LANES), BF),
            pltpu.VMEM((seq, lines - tiles * block, LANES), BF),
            pltpu.VMEM((hidden, 256), F32),
            pltpu.SemaphoreType.DMA((seq // max(1, 256 // block),)),
            pltpu.SemaphoreType.DMA((depth // 256,)),
        ],
        "feed_gradient",
        m,
        dgu,
        g_all,
        h2_all,
        smem=False,
        flops=FILL_LONG,
        vmem=16,
        far_out=(0,),
    )
    feed_raw = lax.psum_scatter(feed_grad, "seq", scatter_dimension=0)
    feed_total = feed_raw.astype(F32)

    ffn = call(
        functools.partial(down_kernel, fsdp),
        [shape((rows, depth), F32)] + [shape((rows, depth), BF)] * (fsdp - 1),
        [],
        "down_projection",
        m,
        w_down,
        smem=False,
        flops=FILL_SHORT,
    )
    dh2_got = after(dh2_got, feed_grad, ffn[0])

    dz, dz_b, sums2 = call(
        functools.partial(norm2_back_kernel, fsdp - 1),
        [shape((rows, depth), F32), shape((rows, depth), BF), shape((2, depth), F32)],
        [],
        "norm2_back",
        dh2_keep,
        *dh2_got,
        z_res,
        g_b,
        row(ln2_gain),
        smem=False,
    )
    outs = call(
        functools.partial(project_back_kernel, chips),
        [shape((CORES * rows, depth), BF)] + [shape((CORES * rows, width), BF)] * chips,
        [],
        "out_projection_back",
        place,
        dz_b,
        to_core(dz_b, seq),
        w_out,
    )
    dz2, do = outs[0], outs[1:]
    do = [do[0]] + [to_line(do[k], seq, k) for k in steps]


    outs = call(
        functools.partial(project_grad_kernel, chips, fsdp),
        [shape((chips, piece, depth), BF)] * fsdp,
        [pltpu.VMEM((chips * width, depth), F32)],
        "out_projection_gradient",
        place,
        *att,
        dz2,
    )
    o_blocks = outs
    ffn_late = after(ffn, dz_b)
    ffn_got = [to_fsdp(ffn_late[j], fsdp, j) for j in flips]
    do = after(do, outs[0], ffn_got)

    dp = call(
        functools.partial(backward_kernel, chips),
        shape((length, 3 * width), BF),
        [
            pltpu.VMEM((length, width), BF),
            pltpu.VMEM((length, width), F32),
            pltpu.VMEM((length, width), F32),
        ],
        "attention_backward",
        place,
        q,
        k_,
        v,
        lse,
        *do,
        cosines,
        sines,
        flops=LONG,
        vmem=12,
    )
    lanes = 3 * width
    per, count = small_rows(depth, lanes)
    blocks = call(
        functools.partial(qkv_grad_kernel, chips, fsdp),
        [shape((seq * piece + count, lanes), BF)] * fsdp + [shape((length, depth), BF)],
        [
            pltpu.VMEM((depth, lanes), F32),
            pltpu.VMEM((length, depth), BF),
            pltpu.SemaphoreType.DMA((length // min(256, length),)),
        ],
        "qkv_gradient",
        place,
        h1,
        u1,
        dp,
        w_qkv,
        sums2,
        flops=FILL_LAST,
        vmem=12,
        far_out=(fsdp,),
    )
    blocks, dh1 = blocks[:fsdp], blocks[fsdp]
    line_in = [blocks[0]] + [to_fsdp(blocks[j], fsdp, j) for j in flips]
    blocks = call(
        functools.partial(qkv_line_kernel, chips, fsdp),
        [shape((CORES * piece + count, lanes), BF)] * chips,
        [pltpu.VMEM((seq * piece, lanes), F32)],
        "qkv_gradient_line",
        place,
        *line_in,
    )
    o_late = after(o_blocks, blocks[0])
    total = o_blocks[0].astype(F32)
    for j in flips:
        total = total + to_fsdp(o_late[j], fsdp, j).astype(F32)
    dh1 = gate(dh1, feed_raw, blocks[0])
    block_out = z_res + ffn[0]
    for v in ffn_got:
        block_out = block_out + v.astype(F32)
    block_out = block_out.astype(BF)
    dh1 = lax.psum_scatter(dh1, "seq", scatter_dimension=0, tiled=True)
    blocks = [blocks[0]] + [to_line(blocks[k], seq, k) for k in steps]
    tail = -(-(4 * per + chips) // 16) * 16
    keep, give = call(
        functools.partial(qkv_core_kernel, chips, piece, per),
        [shape((chips * piece + tail, lanes), BF)] * 2,
        [],
        "qkv_gradient_core",
        *blocks,
        smem=False,
    )
    qkv_grad, small, bias_grad = call(
        functools.partial(qkv_final_kernel, chips, piece, per),
        [
            shape((piece, 3 * depth), F32),
            shape((4, depth), F32),
            shape((3 * seq, width), F32),
        ],
        [pltpu.VMEM((3 * seq, piece, width), F32)],
        "qkv_gradient_final",
        place,
        keep,
        to_core(give, seq),
    )
    input_grad = call(
        norm1_back_kernel,
        shape((rows, depth), F32),
        [],
        "norm1_back",
        dh1,
        x_b,
        row(ln1_gain),
        dz,
        smem=False,
    )

    down_grad = feed_total[tiles * block :].reshape(depth // LANES, unit_pad, LANES)
    down_grad = down_grad[:, :unit_piece].transpose(1, 0, 2).reshape(unit_piece, depth)
    gu = feed_total[: tiles * block].astype(BF).reshape(tiles, fsdp, piece, LANES)
    gu = gu.transpose(1, 2, 0, 3).reshape(fsdp, piece, tiles * LANES)[:, :, : 2 * hidden]
    gu_got = [pick(gu, 0)] + [to_fsdp(pick(gu, j), fsdp, j) for j in flips]
    gu = jnp.stack(gu_got)
    order = jnp.arange(fsdp, dtype=jnp.int32) ^ f
    gu = jnp.take(gu, order, axis=0)
    gu = gu.reshape(fsdp, piece, 2, seq, unit_piece).transpose(1, 2, 3, 0, 4)
    gu_grad = gu.reshape(piece, 2 * seq * fsdp * unit_piece).astype(F32)


    out_w_grad = total[0]
    for k in steps:
        out_w_grad = out_w_grad + to_line(total[k].astype(BF), seq, k).astype(F32)

    return (
        block_out.reshape(1, rows, depth),
        input_grad.reshape(1, rows, depth),
        small[0],
        small[1],
        qkv_grad,
        bias_grad.reshape(3 * depth),
        out_w_grad,
        small[2],
        small[3],
        gu_grad,
        down_grad,
    )


def solution(mesh):
    seq, fsdp = mesh.shape["seq"], mesh.shape["fsdp"]
    split = P(("seq", "fsdp"), None)
    toks = P("fsdp", "seq", None)

    def step(*args):
        return on_device(seq, fsdp, *args)

    return jax.shard_map(
        step,
        mesh=mesh,
        in_specs=(toks, P(), P(), split, P(), split, P(), P(), split, split, toks),
        out_specs=(toks, toks, P(), P(), split, P(), split, P(), P(), split, split),
        check_vma=False,
    )
```

```python
import functools

import jax
import jax.numpy as jnp
from jax import lax
from jax.experimental import pallas as pl
from jax.experimental.pallas import tpu as pltpu
from jax.sharding import PartitionSpec as P

H = 16
HD = 64
ROT = 16
EPS = 1e-05
BF = jnp.bfloat16
F32 = jnp.float32
CORES = 2
LANES = 128
ATT = 10_000_000_000
FILL_SHORT = 4_000_000_000
FILL_LONG = 8_000_000_000
FILL_LAST = 10_000_000_000
PROJECT = 20_000_000_000
LONG = 20_000_000_000
MIB = 1024 * 1024


def to_core(value, seq):
    return lax.ppermute(value, "seq", [(i, i ^ 1) for i in range(seq)])


def to_line(value, seq, step):
    return lax.ppermute(value, "seq", [(i, i ^ (CORES * step)) for i in range(seq)])


def to_fsdp(value, fsdp, flip):
    return lax.ppermute(value, "fsdp", [(i, i ^ flip) for i in range(fsdp)])


def after(values, *earlier):
    flat, tree = jax.tree.flatten(values)
    held = lax.optimization_barrier((flat, earlier))[0]
    return jax.tree.unflatten(tree, held)


def call(body, out_shape, scratch, name, *args, smem=True, flops=1_000_000_000, vmem=8, far=(), far_out=()):
    spaces = lambda count, hbm: [
        pl.BlockSpec(memory_space=pltpu.HBM if i in hbm else pltpu.VMEM) for i in range(count)
    ]
    specs = spaces(len(args), far)
    args = [
        pltpu.with_memory_space_constraint(a, pltpu.HBM) if i in far else a
        for i, a in enumerate(args)
    ]
    alone = not isinstance(out_shape, (list, tuple))
    outs = [out_shape] if alone else list(out_shape)
    outs = [pltpu.HBM(o.shape, o.dtype) if i in far_out else o for i, o in enumerate(outs)]
    out_shape = outs[0] if alone else outs
    out_specs = spaces(1 if alone else len(out_shape), far_out)
    if smem:
        specs[0] = pl.BlockSpec(memory_space=pltpu.SMEM)
    return pl.pallas_call(
        body,
        out_shape=out_shape,
        in_specs=specs,
        out_specs=out_specs[0] if alone else out_specs,
        scratch_shapes=scratch,
        compiler_params=pltpu.CompilerParams(vmem_limit_bytes=vmem * MIB),
        cost_estimate=pl.CostEstimate(flops=flops, transcendentals=0, bytes_accessed=1000000),
        name=name,
    )(*args)


def gate_kernel(*refs):
    pltpu.touch(refs[-1])


def gate(value, *earlier):
    whole = pl.BlockSpec(memory_space=pl.ANY)
    return pl.pallas_call(
        gate_kernel,
        out_shape=shape(value.shape, value.dtype),
        in_specs=[whole] * (1 + len(earlier)),
        out_specs=whole,
        input_output_aliases={0: 0},
        cost_estimate=pl.CostEstimate(flops=1000, transcendentals=0, bytes_accessed=1000),
        name="gate",
    )(value, *earlier)


def shape(dims, dtype):
    return jax.ShapeDtypeStruct(dims, dtype)


def row_type(step):
    return BF if step % 16 == 0 else F32


def at_rows(start, count, step):
    return pl.ds(pl.multiple_of(start, step), count)


def dot(left, right, left_dim, right_dim):
    return lax.dot_general(
        left, right, (((left_dim,), (right_dim,)), ((), ())), preferred_element_type=F32
    )


def rotary_tables(length, width):
    half = ROT // 2
    lane = jnp.arange(width, dtype=jnp.int32) % HD
    frequency = 10000.0 ** (-2.0 * (lane % half).astype(F32) / ROT)
    angles = jnp.arange(length, dtype=jnp.int32).astype(F32)[:, None] * frequency[None, :]
    rotated = (lane < ROT)[None, :]
    sines = jnp.where((lane < half)[None, :], -jnp.sin(angles), jnp.sin(angles))
    return (jnp.where(rotated, jnp.cos(angles), 1.0), jnp.where(rotated, sines, 0.0))


def lane_roll(value, shift):
    width = value.shape[1]
    if width % LANES == 0:
        return pltpu.roll(value, shift % width, 1)
    return jnp.roll(value, shift, axis=1)


def rotate(value, cosines, sines):
    half = ROT // 2
    lane = lax.broadcasted_iota(jnp.int32, value.shape, 1) % HD
    partner = jnp.where(lane < half, lane_roll(value, -half), lane_roll(value, half))
    return value * cosines + partner * sines


def head_lanes(value, head):
    lane = lax.broadcasted_iota(jnp.int32, value.shape, 1)
    return jnp.where(lane // HD == head, value, jnp.zeros_like(value))


def causal(scores, first_row):
    rows = first_row + lax.broadcasted_iota(jnp.int32, scores.shape, 0)
    cols = lax.broadcasted_iota(jnp.int32, scores.shape, 1)
    return jnp.where(rows >= cols, scores, -jnp.inf)


def norm_parts(values):
    mean = jnp.mean(values, axis=-1, keepdims=True)
    centred = values - mean
    inv = lax.rsqrt(jnp.mean(centred * centred, axis=-1, keepdims=True) + EPS)
    return (centred * inv, inv)


def norm_back(grad, gain, unit, inv):
    scaled = grad * gain
    return inv * (
        scaled
        - jnp.mean(scaled, axis=-1, keepdims=True)
        - unit * jnp.mean(scaled * unit, axis=-1, keepdims=True)
    )


def inputs_kernel(chips, fsdp, place, *refs):
    refs = list(refs)
    tok_ref, parts, refs = refs[0], refs[1 : 1 + fsdp], refs[1 + fsdp :]
    gain, bias, qb, cos_ref, sin_ref, h1_far, u1_far, q_ref, k_ref, v_ref, w_ref = refs[:11]
    w_rows, tok_in, tok_sem, h1_ref, u1_ref, h1_sem, u1_sem = refs[11:]

    def tok_copy(s):
        return pltpu.make_async_copy(tok_ref.at[s], tok_in.at[s], tok_sem.at[s])

    for s in range(chips * CORES):
        tok_copy(s).start()
    z, core, f = place[0], place[1], place[2]
    length, width = q_ref.shape
    rows = tok_ref.shape[1]
    piece = parts[0].shape[3]
    seq = chips * CORES
    for j in range(fsdp):
        for k in range(chips):
            for c in range(CORES):
                at = (((z ^ k) * CORES + (core ^ c)) * fsdp + (f ^ j)) * piece
                for t in range(3):
                    w_rows[at_rows(at, piece, piece), t * width : (t + 1) * width] = parts[j][
                        c, k, t
                    ].astype(w_rows.dtype)
    w_ref[...] = w_rows[...].astype(BF)

    def norm(s, carry):
        tok_copy(s).wait()
        u1, _ = norm_parts(tok_in[s].astype(F32))
        here = at_rows(s * rows, rows, rows)
        u1_ref[here, :] = u1.astype(BF)
        h1_ref[here, :] = (u1 * gain[...] + bias[...]).astype(BF)
        u1_copy(s).start()
        h1_copy(s).start()
        return carry

    def h1_copy(s):
        here = at_rows(s * rows, rows, rows)
        return pltpu.make_async_copy(h1_ref.at[here, :], h1_far.at[here, :], h1_sem.at[s])

    def u1_copy(s):
        here = at_rows(s * rows, rows, rows)
        return pltpu.make_async_copy(u1_ref.at[here, :], u1_far.at[here, :], u1_sem.at[s])

    def finish(s, carry):
        u1_copy(s).wait()
        h1_copy(s).wait()
        return carry

    lax.fori_loop(0, seq, norm, 0)
    me = z * CORES + core
    biases = [qb[pl.ds(part * seq + me, 1), :] for part in range(3)]
    block = min(256, length)

    def project(i, carry):
        here = at_rows(i * block, block, block)
        p = dot(h1_ref[here, :], w_ref[...], 1, 0)
        cosines, sines = cos_ref[here, :], sin_ref[here, :]
        q_ref[here, :] = rotate(p[:, :width] + biases[0], cosines, sines).astype(BF)
        k_ref[here, :] = rotate(p[:, width : 2 * width] + biases[1], cosines, sines).astype(BF)
        v_ref[here, :] = (p[:, 2 * width :] + biases[2]).astype(BF)
        return carry

    lax.fori_loop(0, length // block, project, 0)
    lax.fori_loop(0, seq, finish, 0)


def attend_kernel(chips, place, q_ref, k_ref, v_ref, lse_ref, *refs):
    att_out, att_ref = refs[:chips], refs[chips]
    z = place[0]
    length, width = q_ref.shape
    rows = length // (chips * CORES)
    block = min(256, length)
    scaling = HD ** (-0.5)
    for at in range(0, length, block):
        here, upto = pl.ds(at, block), pl.ds(0, at + block)
        q, k, v = q_ref[here, :], k_ref[upto, :], v_ref[upto, :]
        att = jnp.zeros((block, width), F32)
        totals = []
        for head in range(width // HD):
            scores = causal(dot(head_lanes(q, head), k, 1, 1) * scaling, at)
            top = jnp.max(scores, axis=-1, keepdims=True)
            exponent = jnp.exp(scores - top)
            total = jnp.sum(exponent, axis=-1, keepdims=True)
            weights = (exponent * (1.0 / total)).astype(BF)
            att = att + head_lanes(dot(weights, v, 1, 0), head)
            totals.append(jnp.broadcast_to(top + jnp.log(total), (block, HD)))
        att_ref[here, :] = att.astype(BF)
        lse_ref[here, :] = jnp.concatenate(totals, axis=1)
    for k in range(chips):
        at = (z ^ k) * (CORES * rows)
        att_out[k][...] = att_ref[at_rows(at, CORES * rows, CORES * rows), :]


def project_kernel(chips, fsdp, place, *refs):
    refs = list(refs)
    att, refs = refs[:chips], refs[chips:]
    parts, refs = refs[:fsdp], refs[fsdp:]
    keep_ref, give_ref, w_far, w_rows, res, w_ref, w_sem = refs
    core, f = place[1], place[2]
    rows = keep_ref.shape[0]
    width = att[0].shape[1]
    piece = parts[0].shape[2]
    for j in range(fsdp):
        for k in range(chips):
            at = k * width + (f ^ j) * piece
            for t in range(parts[j].shape[1]):
                w_rows[at_rows(at, piece, piece), t * width : (t + 1) * width] = parts[j][
                    k, t
                ].astype(w_rows.dtype)
    w_ref[...] = w_rows[...].astype(BF)
    copy = pltpu.make_async_copy(w_ref, w_far, w_sem)
    copy.start()
    res[...] = dot(jnp.concatenate([a[...] for a in att], axis=1), w_ref[...], 1, 0)
    keep_ref[...] = res[at_rows(core * rows, rows, rows), :]
    give_ref[...] = res[at_rows((1 - core) * rows, rows, rows), :]
    copy.wait()


def norm2_kernel(x_ref, keep_ref, got_ref, gain, bias, z_ref, h2_ref):
    z = x_ref[...].astype(F32) + (keep_ref[...] + got_ref[...])
    z_ref[...] = z
    u2, _ = norm_parts(z)
    h2_ref[...] = (u2 * gain[...] + bias[...]).astype(BF)


def feed_kernel(seq, fsdp, hidden, unit_piece, place, *refs):
    refs = list(refs)
    h2, refs = refs[:fsdp], refs[fsdp:]
    g, refs = refs[:fsdp], refs[fsdp:]
    feed_ref, keep_ref, refs = refs[0], refs[1], refs[2:]
    sends, refs = refs[: fsdp - 1], refs[fsdp - 1 :]
    m_ref, dgu_ref, wd_far, h2_all, g_all, down_rows, feed_in, feed_sem, g_sem, wd_out, wd_sem, send_out, send_sem, gu_rows = refs[:14]
    w_gu = refs[14] if len(refs) > 14 else gu_rows
    f = place[2]
    rows, depth = keep_ref.shape
    copies = [
        pltpu.make_async_copy(feed_ref.at[s], feed_in.at[s], feed_sem.at[s]) for s in range(seq)
    ]
    for copy in copies:
        copy.start()
    g_copies = [
        pltpu.make_async_copy(g[j], g_all.at[pl.ds(j * rows, rows), :], g_sem.at[j])
        for j in range(fsdp)
    ]
    for copy in g_copies:
        copy.start()
    for j in range(fsdp):
        h2_all[j * rows : (j + 1) * rows, :] = h2[j][...]
    tiles = gu_rows.shape[1] // LANES
    piece = depth // (seq * fsdp)
    unit_pad = down_pad(unit_piece)
    first = fsdp * tiles * piece

    def gather(s, carry):
        pltpu.make_async_copy(feed_ref.at[s], feed_in.at[s], feed_sem.at[s]).wait()
        for j in range(fsdp):
            at = at_rows((s * fsdp + (f ^ j)) * piece, piece, piece)
            for t in range(tiles):
                tile = feed_in[s, pl.ds((j * tiles + t) * piece, piece), :]
                gu_rows[at, t * LANES : (t + 1) * LANES] = tile.astype(gu_rows.dtype)
        return carry

    def gather_down(s, at):
        for t in range(0, depth // LANES, 2):
            tile = feed_in[s, pl.ds(first + t * unit_pad, 2 * unit_pad), :].astype(F32)
            for q in range(2):
                cols = slice((t + q) * LANES, (t + q + 1) * LANES)
                down_rows[at, cols] = tile[q * unit_pad : q * unit_pad + unit_piece, :]

    lax.fori_loop(0, seq, gather, 0)
    wd_ref = wd_out
    if (2 * unit_piece) % 16 == 0:

        def gather_units(p, carry):
            at = at_rows(p * (2 * unit_piece), 2 * unit_piece, 16)
            for t in range(0, depth // LANES, 2):
                rows_of = pl.ds(first + t * unit_pad, 2 * unit_pad)
                pair = [feed_in[2 * p + n, rows_of, :].astype(F32) for n in range(2)]
                for q in range(2):
                    cut = slice(q * unit_pad, q * unit_pad + unit_piece)
                    both = jnp.concatenate([v[cut, :] for v in pair], axis=0)
                    wd_ref[at, (t + q) * LANES : (t + q + 1) * LANES] = both.astype(BF)
            return carry

        lax.fori_loop(0, seq // 2, gather_units, 0)
    else:
        for s in range(seq):
            gather_down(s, pl.ds(s * unit_piece, unit_piece))
        wd_ref[...] = down_rows[...].astype(BF)
    wd_copy = pltpu.make_async_copy(wd_ref, wd_far, wd_sem)
    wd_copy.start()
    if w_gu is not gu_rows:
        w_gu[...] = gu_rows[...].astype(BF)
    for copy in g_copies:
        copy.wait()
    if dgu_ref.shape[1] > 2 * hidden:
        dgu_ref[...] = jnp.zeros_like(dgu_ref)
    chunks = 2

    def work(i, carry):
        here = at_rows(i * (chunks * rows), chunks * rows, chunks * rows)
        gu = dot(h2_all[here, :], w_gu[...], 1, 0)
        gate, up = gu[:, :hidden], gu[:, hidden : 2 * hidden]
        dm = dot(g_all[here, :], wd_ref[...], 1, 1)
        sig = 1.0 / (1.0 + jnp.exp(-gate))
        silu = gate * sig
        m_ref[here, :] = (silu * up).astype(BF)
        dgu_ref[here, :hidden] = (dm * up * sig * (1.0 + gate * (1.0 - sig))).astype(BF)
        dgu_ref[here, hidden : 2 * hidden] = (dm * silu).astype(BF)
        dh2 = dot(dgu_ref[here, :], w_gu[...], 1, 1)
        for j in range(fsdp):

            @pl.when(i == j // chunks)
            def _():
                part = dh2[(j % chunks) * rows : (j % chunks + 1) * rows, :]
                if j == 0:
                    keep_ref[...] = part
                else:
                    send_out[j - 1] = part.astype(BF)
                    send_copy(j).start()

        return carry

    def send_copy(j):
        return pltpu.make_async_copy(send_out.at[j - 1], sends[j - 1], send_sem.at[j - 1])

    lax.fori_loop(0, fsdp // chunks, work, 0)
    wd_copy.wait()
    for j in range(1, fsdp):
        send_copy(j).wait()


def down_kernel(fsdp, m_ref, wd_ref, keep_ref, *sends):
    rows = keep_ref.shape[0]
    for j in range(fsdp):
        part = dot(m_ref[j * rows : (j + 1) * rows, :], wd_ref[...], 1, 0)
        if j == 0:
            keep_ref[...] = part
        else:
            sends[j - 1][...] = part.astype(BF)


def down_pad(unit_piece):
    return unit_piece if unit_piece % 8 == 0 else -(-unit_piece // 16) * 16


def feed_grad_kernel(seq, hidden, unit_piece, m_ref, dgu_ref, g_all, h2_all, out_ref, *refs):
    gu_out, down_out, down_acc, gu_sem, down_sem = refs
    depth = g_all.shape[1]
    tiles = dgu_ref.shape[1] // LANES
    block = depth // seq
    unit_pad = down_pad(unit_piece)
    pair = max(1, 256 // block)

    def gu_copy(i):
        return pltpu.make_async_copy(
            gu_out.at[pl.ds(i * pair, pair)],
            out_ref.at[pl.ds(i * pair, pair), pl.ds(0, tiles * block), :],
            gu_sem.at[i],
        )

    def down_copy(i):
        at = pl.multiple_of(i * 2 * unit_pad, 16)
        return pltpu.make_async_copy(
            down_out.at[:, pl.ds(at, 2 * unit_pad), :],
            out_ref.at[:, pl.ds(tiles * block + at, 2 * unit_pad), :],
            down_sem.at[i],
        )

    def gate_up(i, carry):
        cols = pl.ds(pl.multiple_of(i * (pair * block), pair * block), pair * block)
        grad = dot(h2_all[:, cols], dgu_ref[...], 0, 0).astype(BF)
        for s in range(pair):
            for t in range(tiles):
                gu_out[i * pair + s, t * block : (t + 1) * block, :] = grad[
                    s * block : (s + 1) * block, t * LANES : (t + 1) * LANES
                ]
        gu_copy(i).start()
        return carry

    lax.fori_loop(0, seq // pair, gate_up, 0, unroll=True)

    def down(i, carry):
        cols = pl.ds(pl.multiple_of(i * 256, 256), 256)
        down_acc[...] = dot(m_ref[...], g_all[:, cols], 0, 0)
        for s in range(seq):
            both = []
            for t in range(2):
                both.append(
                    down_acc[s * unit_piece : (s + 1) * unit_piece, t * LANES : (t + 1) * LANES]
                )
                if unit_pad > unit_piece:
                    both.append(jnp.zeros((unit_pad - unit_piece, LANES), F32))
            rows = at_rows(i * (2 * unit_pad), 2 * unit_pad, 16)
            down_out[s, rows, :] = jnp.concatenate(both, axis=0).astype(BF)
        down_copy(i).start()
        return carry

    lax.fori_loop(0, depth // 256, down, 0, unroll=True)

    def finish_gu(i, carry):
        gu_copy(i).wait()
        return carry

    def finish_down(i, carry):
        down_copy(i).wait()
        return carry

    lax.fori_loop(0, seq // pair, finish_gu, 0)
    lax.fori_loop(0, depth // 256, finish_down, 0)


def norm2_back_kernel(count, *refs):
    keep_ref, got, refs = refs[0], refs[1 : 1 + count], refs[1 + count :]
    z_ref, g_ref, gain, dz_ref, dzb_ref, sums_ref = refs
    dh2 = keep_ref[...]
    for ref in got:
        dh2 = dh2 + ref[...].astype(F32)
    u2, r2 = norm_parts(z_ref[...])
    dz = g_ref[...].astype(F32) + norm_back(dh2, gain[...], u2, r2)
    dz_ref[...] = dz
    dzb_ref[...] = dz.astype(BF)
    sums_ref[0:1, :] = jnp.sum(dh2 * u2, axis=0, keepdims=True)
    sums_ref[1:2, :] = jnp.sum(dh2, axis=0, keepdims=True)


def project_back_kernel(chips, place, mine_ref, other_ref, w_ref, dz2_ref, *outs):
    core = place[1]
    rows = mine_ref.shape[0]
    width = outs[0].shape[1]
    dz2_ref[at_rows(core * rows, rows, rows), :] = mine_ref[...]
    dz2_ref[at_rows((1 - core) * rows, rows, rows), :] = other_ref[...]
    do = dot(dz2_ref[...], w_ref[...], 1, 1)
    for k in range(chips):
        outs[k][...] = do[:, k * width : (k + 1) * width].astype(BF)


def project_grad_kernel(chips, fsdp, place, *refs):
    att, refs = refs[:chips], refs[chips:]
    dz2_ref, refs = refs[0], refs[1:]
    outs, acc = refs[:fsdp], refs[fsdp]
    f = place[2]
    width = att[0].shape[1]
    piece = width // fsdp
    acc[...] = dot(jnp.concatenate([a[...] for a in att], axis=1), dz2_ref[...], 0, 0)
    for j in range(fsdp):
        for k in range(chips):
            at = k * width + (f ^ j) * piece
            outs[j][k] = acc[at_rows(at, piece, piece), :].astype(BF)


def backward_kernel(chips, place, *refs):
    q_ref, k_ref, v_ref, lse_ref = refs[:4]
    do_in, refs = refs[4 : 4 + chips], refs[4 + chips :]
    cos_ref, sin_ref, dp_ref, do_ref, dk_acc, dv_acc = refs
    z = place[0]
    length, width = q_ref.shape
    rows = length // (chips * CORES)
    for k in range(chips):
        at = (z ^ k) * (CORES * rows)
        do_ref[at_rows(at, CORES * rows, CORES * rows), :] = do_in[k][...]
    heads = width // HD
    block = min(256, length)
    scaling = HD ** (-0.5)
    dk_acc[...] = jnp.zeros_like(dk_acc)
    dv_acc[...] = jnp.zeros_like(dv_acc)
    for at in range(0, length, block):
        here, upto = pl.ds(at, block), pl.ds(0, at + block)
        q, do, k, v = q_ref[here, :], do_ref[here, :], k_ref[upto, :], v_ref[upto, :]
        dq = jnp.zeros((block, width), F32)
        for head in range(heads):
            qh, doh = head_lanes(q, head), head_lanes(do, head)
            lse = lse_ref[here, head * HD : head * HD + 1]
            scores = causal(dot(qh, k, 1, 1) * scaling, at)
            probs = jnp.exp(scores - lse)
            dprobs = dot(doh, v, 1, 1)
            delta = jnp.sum(probs * dprobs, axis=-1, keepdims=True)
            dscores = (probs * (dprobs - delta)).astype(BF)
            dq = dq + head_lanes(dot(dscores, k, 1, 0), head)
            dk_acc[upto, :] += dot(dscores, qh, 0, 0)
            dv_acc[upto, :] += dot(probs.astype(BF), doh, 0, 0)
        dq = rotate(dq * scaling, cos_ref[here, :], -sin_ref[here, :])
        dp_ref[here, :width] = dq.astype(BF)

    def finish(i, carry):
        here = at_rows(i * block, block, block)
        dk = rotate(dk_acc[here, :] * scaling, cos_ref[here, :], -sin_ref[here, :])
        dp_ref[here, width : 2 * width] = dk.astype(BF)
        dp_ref[here, 2 * width :] = dv_acc[here, :].astype(BF)
        return carry

    lax.fori_loop(0, length // block, finish, 0, unroll=True)


def small_rows(depth, lanes):
    return -(-depth // lanes), -(-(4 * -(-depth // lanes) + 1) // 16) * 16


def tree_sum(values):
    values = list(values)
    while len(values) > 1:
        values = [values[i] + values[i + 1] for i in range(0, len(values), 2)]
    return values[0]


def qkv_grad_kernel(chips, fsdp, place, h1_ref, u1_ref, dp_ref, w_ref, sums2_ref, *refs):
    outs, (dh_far, acc, dh_ref, dh_sem) = refs[:fsdp], refs[fsdp:]
    f = place[2]
    seq = chips * CORES
    depth, lanes = acc.shape
    piece = depth // (seq * fsdp)
    length = dp_ref.shape[0]
    acc[...] = dot(h1_ref[...], dp_ref[...], 0, 0)
    block = min(256, length)

    def dh_copy(i):
        here = at_rows(i * block, block, block)
        return pltpu.make_async_copy(dh_ref.at[here, :], dh_far.at[here, :], dh_sem.at[i])

    def dh_wait(i, carry):
        dh_copy(i).wait()
        return carry

    def sums(i, carry):
        gains, shifts, biases = carry
        here = at_rows(i * block, block, block)
        dh1 = dot(dp_ref[here, :], w_ref[...], 1, 1)
        dh_ref[here, :] = dh1.astype(BF)
        dh_copy(i).start()
        gains = gains + jnp.sum(dh1 * u1_ref[here, :].astype(F32), axis=0, keepdims=True)
        shifts = shifts + jnp.sum(dh1, axis=0, keepdims=True)
        biases = biases + jnp.sum(dp_ref[here, :].astype(F32), axis=0, keepdims=True)
        return (gains, shifts, biases)

    zeros = jnp.zeros((1, depth), F32)
    gains, shifts, biases = lax.fori_loop(
        0, length // block, sums, (zeros, zeros, jnp.zeros((1, lanes), F32)), unroll=True
    )
    per, count = small_rows(depth, lanes)
    small = []
    for v in (gains, shifts, sums2_ref[0:1, :], sums2_ref[1:2, :]):
        if per * lanes > depth:
            v = jnp.concatenate([v, jnp.zeros((1, per * lanes - depth), F32)], axis=1)
        small += [v[:, r * lanes : (r + 1) * lanes] for r in range(per)]
    small.append(biases)
    if count > len(small):
        small.append(jnp.zeros((count - len(small), lanes), F32))
    small = jnp.concatenate(small, axis=0)
    for j in range(fsdp):
        for s in range(seq):
            at = (s * fsdp + (f ^ j)) * piece
            outs[j][s * piece : (s + 1) * piece, :] = acc[at_rows(at, piece, piece), :].astype(BF)
        outs[j][seq * piece :, :] = small.astype(BF)
    lax.fori_loop(0, length // block, dh_wait, 0)


def qkv_line_kernel(chips, fsdp, place, *refs):
    got, refs = refs[:fsdp], refs[fsdp:]
    outs, acc = refs[:chips], refs[chips]
    z, core = place[0], place[1]
    count = outs[0].shape[0]
    total_rows = got[0].shape[0]
    small = total_rows - acc.shape[0]
    piece = acc.shape[0] // (chips * CORES)
    total = tree_sum([ref[...].astype(F32) for ref in got])
    acc[...] = total[: total_rows - small, :]
    for k in range(chips):
        for c in range(CORES):
            at = ((z ^ k) * CORES + (core ^ c)) * piece
            outs[k][c * piece : (c + 1) * piece, :] = acc[at_rows(at, piece, piece), :].astype(BF)
        outs[k][CORES * piece : count, :] = total[total_rows - small :, :].astype(BF)


def qkv_core_kernel(chips, piece, per, *refs):
    got, (keep_ref, give_ref) = refs[:chips], refs[chips:]
    lanes = keep_ref.shape[1]
    small = [ref[CORES * piece :, :].astype(F32) for ref in got]
    total = tree_sum(small)
    bias = [v[4 * per : 4 * per + 1, :] for v in small]
    rest = keep_ref.shape[0] - chips * piece - 4 * per - chips
    pad = [jnp.zeros((rest, lanes), F32)] if rest > 0 else []
    tail = jnp.concatenate([total[: 4 * per, :]] + bias + pad, axis=0)
    for c, ref in ((0, keep_ref), (1, give_ref)):
        for k in range(chips):
            ref[k * piece : (k + 1) * piece, :] = got[k][c * piece : (c + 1) * piece, :]
        ref[chips * piece :, :] = tail.astype(BF)


def qkv_final_kernel(chips, piece, per, place, keep_ref, got_ref, grad_ref, small_ref, bias_ref, acc):
    z, core = place[0], place[1]
    seq = chips * CORES
    lanes = keep_ref.shape[1]
    width = lanes // 3
    depth = small_ref.shape[1]
    at = chips * piece
    tails = [ref[at:, :].astype(F32) for ref in (keep_ref, got_ref)]
    total = tails[0] + tails[1]
    for c, ref in ((0, keep_ref), (1, got_ref)):
        for k in range(chips):
            src = (z ^ k) * CORES + (core ^ c)
            rows = ref[k * piece : (k + 1) * piece, :].astype(F32)
            bias = tails[c][4 * per + k : 4 * per + k + 1, :]
            for part in range(3):
                acc[part * seq + src] = rows[:, part * width : (part + 1) * width]
                bias_ref[pl.ds(part * seq + src, 1), :] = bias[:, part * width : (part + 1) * width]
    for i in range(3 * seq):
        grad_ref[:, i * width : (i + 1) * width] = acc[i]
    for v in range(4):
        for r in range(per):
            upto = min(lanes, depth - r * lanes)
            small_ref[v : v + 1, r * lanes : r * lanes + upto] = total[v * per + r : v * per + r + 1, :upto]


def norm1_back_kernel(dh1_ref, x_ref, gain, dz_ref, out_ref):
    u1, r1 = norm_parts(x_ref[...].astype(F32))
    out_ref[...] = dz_ref[...] + norm_back(dh1_ref[...].astype(F32), gain[...], u1, r1)


def on_device(
    seq,
    fsdp,
    tokens,
    ln1_gain,
    ln1_bias,
    qkv_weight,
    qkv_bias,
    out_weight,
    ln2_gain,
    ln2_bias,
    gate_up_weight,
    down_weight,
    out_grad,
):
    rows, depth = tokens.shape[1], tokens.shape[2]
    length = rows * seq
    chips = seq // CORES
    width = depth // seq
    piece = qkv_weight.shape[0]
    unit_piece = down_weight.shape[0]
    hidden = seq * unit_piece
    tiles = -(-2 * hidden // LANES)
    unit_pad = down_pad(unit_piece)
    me = lax.axis_index("seq")
    z, core, f = me // CORES, me % CORES, lax.axis_index("fsdp")
    place = jnp.stack([z, core, f]).astype(jnp.int32)
    steps, flips = range(1, chips), range(1, fsdp)
    by_place = jnp.arange(seq, dtype=jnp.int32) ^ me
    x_b = tokens.reshape(rows, depth)
    g_b = out_grad.reshape(rows, depth)
    row = lambda v: v.reshape(1, -1)

    tok_all = lax.all_gather(x_b, "seq", axis=0)

    w = qkv_weight.reshape(piece, 3, seq, width).transpose(2, 1, 0, 3)
    w = jnp.take(w, by_place, axis=0).reshape(chips, CORES * 3, piece, width)
    w = [w[0]] + [to_line(w[k], seq, k) for k in steps]
    cosines, sines = rotary_tables(length, width)
    give = after(jnp.stack([v[3:] for v in w]), cosines, sines)
    w = jnp.stack([jnp.stack([v[:3] for v in w]), to_core(give, seq)])
    w_parts = [w] + [to_fsdp(w, fsdp, j) for j in flips]

    gu = gate_up_weight.reshape(piece, 2, seq, fsdp, unit_piece).transpose(3, 0, 1, 2, 4)
    gu = gu.reshape(fsdp, piece, 2 * hidden)
    gu = jnp.pad(gu, ((0, 0), (0, 0), (0, tiles * LANES - 2 * hidden)))
    gu = gu.reshape(fsdp, piece, tiles, LANES).transpose(0, 2, 1, 3)
    pick = lambda v, j: lax.dynamic_index_in_dim(v, f ^ j, axis=0, keepdims=False)
    gu = after(gu, w)
    gu = [pick(gu, 0)] + [to_fsdp(pick(gu, j), fsdp, j) for j in flips]
    g_late = after(g_b, gu)
    g_parts = [g_b] + [to_fsdp(g_late, fsdp, j) for j in flips]

    o = after(out_weight, gu).reshape(piece, seq, width).transpose(1, 0, 2)
    o = [o] + [to_line(o, seq, k) for k in steps]
    down = jnp.pad(down_weight, ((0, unit_pad - unit_piece), (0, 0)))
    down = down.reshape(unit_pad, depth // LANES, LANES).transpose(1, 0, 2)
    feed = jnp.concatenate(
        [v.reshape(-1, LANES) for v in gu] + [down.reshape(-1, LANES)], axis=0
    )
    feed = lax.all_gather(feed, "seq", axis=0)

    outs = call(
        functools.partial(inputs_kernel, chips, fsdp),
        [shape((length, depth), BF)] * 2
        + [shape((length, width), BF)] * 3
        + [shape((depth, 3 * width), BF)],
        [
            pltpu.VMEM((depth, 3 * width), row_type(piece)),
            pltpu.VMEM((seq, rows, depth), BF),
            pltpu.SemaphoreType.DMA((seq,)),
            pltpu.VMEM((length, depth), BF),
            pltpu.VMEM((length, depth), BF),
            pltpu.SemaphoreType.DMA((seq,)),
            pltpu.SemaphoreType.DMA((seq,)),
        ],
        "attention_inputs",
        place,
        tok_all,
        *w_parts,
        row(ln1_gain),
        row(ln1_bias),
        qkv_bias.reshape(3 * seq, width),
        cosines,
        sines,
        far=(1,),
        far_out=(0, 1),
        vmem=16,
    )
    h1, u1, q, k_, v, w_qkv = outs
    o = jnp.stack(after(o, q))
    o_parts = [o] + [to_fsdp(o, fsdp, j) for j in flips]
    outs = call(
        functools.partial(attend_kernel, chips),
        [shape((length, width), F32)] + [shape((CORES * rows, width), BF)] * chips,
        [pltpu.VMEM((length, width), BF)],
        "attention_forward",
        place,
        after(q, g_parts),
        k_,
        v,
        flops=ATT,
        vmem=12,
    )
    lse, att = outs[0], outs[1:]
    att = [att[0]] + [to_line(att[k], seq, k) for k in steps]

    keep, give, w_out = call(
        functools.partial(project_kernel, chips, fsdp),
        [shape((rows, depth), F32)] * 2 + [shape((chips * width, depth), BF)],
        [
            pltpu.VMEM((chips * width, depth), row_type(piece)),
            pltpu.VMEM((CORES * rows, depth), F32),
            pltpu.VMEM((chips * width, depth), BF),
            pltpu.SemaphoreType.DMA(()),
        ],
        "out_projection",
        place,
        *att,
        *o_parts,
        flops=PROJECT,
        far_out=(2,),
        vmem=10,
    )
    z_res, h2 = call(
        norm2_kernel,
        [shape((rows, depth), F32), shape((rows, depth), BF)],
        [],
        "norm2",
        x_b,
        keep,
        to_core(give, seq),
        row(ln2_gain),
        row(ln2_bias),
        smem=False,
    )
    h2_parts = [h2] + [to_fsdp(h2, fsdp, j) for j in flips]

    tokens_here = fsdp * rows
    outs = call(
        functools.partial(feed_kernel, seq, fsdp, hidden, unit_piece),
        [shape((rows, depth), F32)]
        + [shape((rows, depth), BF)] * (fsdp - 1)
        + [
            shape((tokens_here, hidden), BF),
            shape((tokens_here, tiles * LANES), BF),
            shape((hidden, depth), BF),
            shape((tokens_here, depth), BF),
            shape((tokens_here, depth), BF),
        ],
        [
            pltpu.VMEM((hidden, depth), F32),
            pltpu.VMEM(feed.shape, BF),
            pltpu.SemaphoreType.DMA((seq,)),
            pltpu.SemaphoreType.DMA((fsdp,)),
            pltpu.VMEM((hidden, depth), BF),
            pltpu.SemaphoreType.DMA(()),
            pltpu.VMEM((fsdp - 1, rows, depth), BF),
            pltpu.SemaphoreType.DMA((fsdp - 1,)),
            pltpu.VMEM((depth, tiles * LANES), row_type(piece)),
        ]
        + ([] if row_type(piece) == BF else [pltpu.VMEM((depth, tiles * LANES), BF)]),
        "feed_forward",
        place,
        *h2_parts,
        *g_parts,
        feed,
        far=tuple(range(1 + fsdp, 2 + 2 * fsdp)),
        far_out=tuple(range(1, fsdp)) + (fsdp + 2,),
        vmem=20,
    )
    dh2_keep, dh2_send = outs[0], outs[1:fsdp]
    m, dgu, w_down, h2_all, g_all = outs[fsdp:]
    dh2_got = [to_fsdp(v, fsdp, j) for j, v in zip(flips, dh2_send)]

    block = depth // seq
    lines = tiles * block + (depth // LANES) * unit_pad
    feed_grad = call(
        functools.partial(feed_grad_kernel, seq, hidden, unit_piece),
        shape((seq, lines, LANES), BF),
        [
            pltpu.VMEM((seq, tiles * block, LANES), BF),
            pltpu.VMEM((seq, lines - tiles * block, LANES), BF),
            pltpu.VMEM((hidden, 256), F32),
            pltpu.SemaphoreType.DMA((seq // max(1, 256 // block),)),
            pltpu.SemaphoreType.DMA((depth // 256,)),
        ],
        "feed_gradient",
        m,
        dgu,
        g_all,
        h2_all,
        smem=False,
        flops=FILL_LONG,
        vmem=16,
        far_out=(0,),
    )
    feed_raw = lax.psum_scatter(feed_grad, "seq", scatter_dimension=0)
    feed_total = feed_raw.astype(F32)

    ffn = call(
        functools.partial(down_kernel, fsdp),
        [shape((rows, depth), F32)] + [shape((rows, depth), BF)] * (fsdp - 1),
        [],
        "down_projection",
        m,
        w_down,
        smem=False,
        flops=FILL_SHORT,
    )
    dh2_got = after(dh2_got, feed_grad, ffn[0])

    dz, dz_b, sums2 = call(
        functools.partial(norm2_back_kernel, fsdp - 1),
        [shape((rows, depth), F32), shape((rows, depth), BF), shape((2, depth), F32)],
        [],
        "norm2_back",
        dh2_keep,
        *dh2_got,
        z_res,
        g_b,
        row(ln2_gain),
        smem=False,
    )
    outs = call(
        functools.partial(project_back_kernel, chips),
        [shape((CORES * rows, depth), BF)] + [shape((CORES * rows, width), BF)] * chips,
        [],
        "out_projection_back",
        place,
        dz_b,
        to_core(dz_b, seq),
        w_out,
    )
    dz2, do = outs[0], outs[1:]
    do = [do[0]] + [to_line(do[k], seq, k) for k in steps]


    outs = call(
        functools.partial(project_grad_kernel, chips, fsdp),
        [shape((chips, piece, depth), BF)] * fsdp,
        [pltpu.VMEM((chips * width, depth), F32)],
        "out_projection_gradient",
        place,
        *att,
        dz2,
    )
    o_blocks = outs
    ffn_late = after(ffn, dz_b)
    ffn_got = [to_fsdp(ffn_late[j], fsdp, j) for j in flips]
    do = after(do, outs[0], ffn_got)

    dp = call(
        functools.partial(backward_kernel, chips),
        shape((length, 3 * width), BF),
        [
            pltpu.VMEM((length, width), BF),
            pltpu.VMEM((length, width), F32),
            pltpu.VMEM((length, width), F32),
        ],
        "attention_backward",
        place,
        q,
        k_,
        v,
        lse,
        *do,
        cosines,
        sines,
        flops=LONG,
        vmem=12,
    )
    lanes = 3 * width
    per, count = small_rows(depth, lanes)
    blocks = call(
        functools.partial(qkv_grad_kernel, chips, fsdp),
        [shape((seq * piece + count, lanes), BF)] * fsdp + [shape((length, depth), BF)],
        [
            pltpu.VMEM((depth, lanes), F32),
            pltpu.VMEM((length, depth), BF),
            pltpu.SemaphoreType.DMA((length // min(256, length),)),
        ],
        "qkv_gradient",
        place,
        h1,
        u1,
        dp,
        w_qkv,
        sums2,
        flops=FILL_LAST,
        vmem=12,
        far_out=(fsdp,),
    )
    blocks, dh1 = blocks[:fsdp], blocks[fsdp]
    line_in = [blocks[0]] + [to_fsdp(blocks[j], fsdp, j) for j in flips]
    blocks = call(
        functools.partial(qkv_line_kernel, chips, fsdp),
        [shape((CORES * piece + count, lanes), BF)] * chips,
        [pltpu.VMEM((seq * piece, lanes), F32)],
        "qkv_gradient_line",
        place,
        *line_in,
    )
    o_late = after(o_blocks, blocks[0])
    total = o_blocks[0].astype(F32)
    for j in flips:
        total = total + to_fsdp(o_late[j], fsdp, j).astype(F32)
    dh1 = gate(dh1, feed_raw, blocks[0])
    block_out = z_res + ffn[0]
    for v in ffn_got:
        block_out = block_out + v.astype(F32)
    block_out = block_out.astype(BF)
    dh1 = lax.psum_scatter(dh1, "seq", scatter_dimension=0, tiled=True)
    blocks = [blocks[0]] + [to_line(blocks[k], seq, k) for k in steps]
    tail = -(-(4 * per + chips) // 16) * 16
    keep, give = call(
        functools.partial(qkv_core_kernel, chips, piece, per),
        [shape((chips * piece + tail, lanes), BF)] * 2,
        [],
        "qkv_gradient_core",
        *blocks,
        smem=False,
    )
    qkv_grad, small, bias_grad = call(
        functools.partial(qkv_final_kernel, chips, piece, per),
        [
            shape((piece, 3 * depth), F32),
            shape((4, depth), F32),
            shape((3 * seq, width), F32),
        ],
        [pltpu.VMEM((3 * seq, piece, width), F32)],
        "qkv_gradient_final",
        place,
        keep,
        to_core(give, seq),
    )
    input_grad = call(
        norm1_back_kernel,
        shape((rows, depth), F32),
        [],
        "norm1_back",
        dh1,
        x_b,
        row(ln1_gain),
        dz,
        smem=False,
    )

    down_grad = feed_total[tiles * block :].reshape(depth // LANES, unit_pad, LANES)
    down_grad = down_grad[:, :unit_piece].transpose(1, 0, 2).reshape(unit_piece, depth)
    gu = feed_total[: tiles * block].astype(BF).reshape(tiles, fsdp, piece, LANES)
    gu = gu.transpose(1, 2, 0, 3).reshape(fsdp, piece, tiles * LANES)[:, :, : 2 * hidden]
    gu_got = [pick(gu, 0)] + [to_fsdp(pick(gu, j), fsdp, j) for j in flips]
    gu = jnp.stack(gu_got)
    order = jnp.arange(fsdp, dtype=jnp.int32) ^ f
    gu = jnp.take(gu, order, axis=0)
    gu = gu.reshape(fsdp, piece, 2, seq, unit_piece).transpose(1, 2, 3, 0, 4)
    gu_grad = gu.reshape(piece, 2 * seq * fsdp * unit_piece).astype(F32)


    out_w_grad = total[0]
    for k in steps:
        out_w_grad = out_w_grad + to_line(total[k].astype(BF), seq, k).astype(F32)

    return (
        block_out.reshape(1, rows, depth),
        input_grad.reshape(1, rows, depth),
        small[0],
        small[1],
        qkv_grad,
        bias_grad.reshape(3 * depth),
        out_w_grad,
        small[2],
        small[3],
        gu_grad,
        down_grad,
    )


def solution(mesh):
    seq, fsdp = mesh.shape["seq"], mesh.shape["fsdp"]
    split = P(("seq", "fsdp"), None)
    toks = P("fsdp", "seq", None)

    def step(*args):
        return on_device(seq, fsdp, *args)

    return jax.shard_map(
        step,
        mesh=mesh,
        in_specs=(toks, P(), P(), split, P(), split, P(), P(), split, split, toks),
        out_specs=(toks, toks, P(), P(), split, P(), split, P(), P(), split, split),
        check_vma=False,
    )
```

```python
import functools

import jax
import jax.numpy as jnp
from jax import lax
from jax.experimental import pallas as pl
from jax.experimental.pallas import tpu as pltpu
from jax.sharding import PartitionSpec as P

H = 16
HD = 64
ROT = 16
EPS = 1e-05
BF = jnp.bfloat16
F32 = jnp.float32
CORES = 2
LANES = 128
ATT = 10_000_000_000
FILL_SHORT = 4_000_000_000
FILL_LONG = 8_000_000_000
FILL_LAST = 10_000_000_000
PROJECT = 20_000_000_000
LONG = 20_000_000_000
MIB = 1024 * 1024


def to_core(value, seq):
    return lax.ppermute(value, "seq", [(i, i ^ 1) for i in range(seq)])


def to_line(value, seq, step):
    return lax.ppermute(value, "seq", [(i, i ^ (CORES * step)) for i in range(seq)])


def to_fsdp(value, fsdp, flip):
    return lax.ppermute(value, "fsdp", [(i, i ^ flip) for i in range(fsdp)])


def after(values, *earlier):
    flat, tree = jax.tree.flatten(values)
    held = lax.optimization_barrier((flat, earlier))[0]
    return jax.tree.unflatten(tree, held)


def call(body, out_shape, scratch, name, *args, smem=True, flops=1_000_000_000, vmem=8, far=(), far_out=()):
    spaces = lambda count, hbm: [
        pl.BlockSpec(memory_space=pltpu.HBM if i in hbm else pltpu.VMEM) for i in range(count)
    ]
    specs = spaces(len(args), far)
    args = [
        pltpu.with_memory_space_constraint(a, pltpu.HBM) if i in far else a
        for i, a in enumerate(args)
    ]
    alone = not isinstance(out_shape, (list, tuple))
    outs = [out_shape] if alone else list(out_shape)
    outs = [pltpu.HBM(o.shape, o.dtype) if i in far_out else o for i, o in enumerate(outs)]
    out_shape = outs[0] if alone else outs
    out_specs = spaces(1 if alone else len(out_shape), far_out)
    if smem:
        specs[0] = pl.BlockSpec(memory_space=pltpu.SMEM)
    return pl.pallas_call(
        body,
        out_shape=out_shape,
        in_specs=specs,
        out_specs=out_specs[0] if alone else out_specs,
        scratch_shapes=scratch,
        compiler_params=pltpu.CompilerParams(vmem_limit_bytes=vmem * MIB),
        cost_estimate=pl.CostEstimate(flops=flops, transcendentals=0, bytes_accessed=1000000),
        name=name,
    )(*args)


def gate_kernel(*refs):
    pltpu.touch(refs[-1])


def gate(value, *earlier):
    whole = pl.BlockSpec(memory_space=pl.ANY)
    return pl.pallas_call(
        gate_kernel,
        out_shape=shape(value.shape, value.dtype),
        in_specs=[whole] * (1 + len(earlier)),
        out_specs=whole,
        input_output_aliases={0: 0},
        cost_estimate=pl.CostEstimate(flops=1000, transcendentals=0, bytes_accessed=1000),
        name="gate",
    )(value, *earlier)


def shape(dims, dtype):
    return jax.ShapeDtypeStruct(dims, dtype)


def row_type(step):
    return BF if step % 16 == 0 else F32


def at_rows(start, count, step):
    return pl.ds(pl.multiple_of(start, step), count)


def dot(left, right, left_dim, right_dim):
    return lax.dot_general(
        left, right, (((left_dim,), (right_dim,)), ((), ())), preferred_element_type=F32
    )


def rotary_tables(length, width):
    half = ROT // 2
    lane = jnp.arange(width, dtype=jnp.int32) % HD
    frequency = 10000.0 ** (-2.0 * (lane % half).astype(F32) / ROT)
    angles = jnp.arange(length, dtype=jnp.int32).astype(F32)[:, None] * frequency[None, :]
    rotated = (lane < ROT)[None, :]
    sines = jnp.where((lane < half)[None, :], -jnp.sin(angles), jnp.sin(angles))
    return (jnp.where(rotated, jnp.cos(angles), 1.0), jnp.where(rotated, sines, 0.0))


def lane_roll(value, shift):
    width = value.shape[1]
    if width % LANES == 0:
        return pltpu.roll(value, shift % width, 1)
    return jnp.roll(value, shift, axis=1)


def rotate(value, cosines, sines):
    half = ROT // 2
    lane = lax.broadcasted_iota(jnp.int32, value.shape, 1) % HD
    partner = jnp.where(lane < half, lane_roll(value, -half), lane_roll(value, half))
    return value * cosines + partner * sines


def head_lanes(value, head):
    lane = lax.broadcasted_iota(jnp.int32, value.shape, 1)
    return jnp.where(lane // HD == head, value, jnp.zeros_like(value))


def causal(scores, first_row):
    rows = first_row + lax.broadcasted_iota(jnp.int32, scores.shape, 0)
    cols = lax.broadcasted_iota(jnp.int32, scores.shape, 1)
    return jnp.where(rows >= cols, scores, -jnp.inf)


def norm_parts(values):
    mean = jnp.mean(values, axis=-1, keepdims=True)
    centred = values - mean
    inv = lax.rsqrt(jnp.mean(centred * centred, axis=-1, keepdims=True) + EPS)
    return (centred * inv, inv)


def norm_back(grad, gain, unit, inv):
    scaled = grad * gain
    return inv * (
        scaled
        - jnp.mean(scaled, axis=-1, keepdims=True)
        - unit * jnp.mean(scaled * unit, axis=-1, keepdims=True)
    )


def inputs_kernel(chips, fsdp, place, *refs):
    refs = list(refs)
    tok_ref, parts, refs = refs[0], refs[1 : 1 + fsdp], refs[1 + fsdp :]
    gain, bias, qb, cos_ref, sin_ref, h1_far, u1_far, q_ref, k_ref, v_ref, w_ref = refs[:11]
    w_rows, tok_in, tok_sem, h1_ref, u1_ref, h1_sem, u1_sem = refs[11:]

    def tok_copy(s):
        return pltpu.make_async_copy(tok_ref.at[s], tok_in.at[s], tok_sem.at[s])

    for s in range(chips * CORES):
        tok_copy(s).start()
    z, core, f = place[0], place[1], place[2]
    length, width = q_ref.shape
    rows = tok_ref.shape[1]
    piece = parts[0].shape[3]
    seq = chips * CORES
    for j in range(fsdp):
        for k in range(chips):
            for c in range(CORES):
                at = (((z ^ k) * CORES + (core ^ c)) * fsdp + (f ^ j)) * piece
                for t in range(3):
                    w_rows[at_rows(at, piece, piece), t * width : (t + 1) * width] = parts[j][
                        c, k, t
                    ].astype(w_rows.dtype)
    w_ref[...] = w_rows[...].astype(BF)

    def norm(s, carry):
        tok_copy(s).wait()
        u1, _ = norm_parts(tok_in[s].astype(F32))
        here = at_rows(s * rows, rows, rows)
        u1_ref[here, :] = u1.astype(BF)
        h1_ref[here, :] = (u1 * gain[...] + bias[...]).astype(BF)
        u1_copy(s).start()
        h1_copy(s).start()
        return carry

    def h1_copy(s):
        here = at_rows(s * rows, rows, rows)
        return pltpu.make_async_copy(h1_ref.at[here, :], h1_far.at[here, :], h1_sem.at[s])

    def u1_copy(s):
        here = at_rows(s * rows, rows, rows)
        return pltpu.make_async_copy(u1_ref.at[here, :], u1_far.at[here, :], u1_sem.at[s])

    def finish(s, carry):
        u1_copy(s).wait()
        h1_copy(s).wait()
        return carry

    lax.fori_loop(0, seq, norm, 0)
    me = z * CORES + core
    biases = [qb[pl.ds(part * seq + me, 1), :] for part in range(3)]
    block = min(256, length)

    def project(i, carry):
        here = at_rows(i * block, block, block)
        p = dot(h1_ref[here, :], w_ref[...], 1, 0)
        cosines, sines = cos_ref[here, :], sin_ref[here, :]
        q_ref[here, :] = rotate(p[:, :width] + biases[0], cosines, sines).astype(BF)
        k_ref[here, :] = rotate(p[:, width : 2 * width] + biases[1], cosines, sines).astype(BF)
        v_ref[here, :] = (p[:, 2 * width :] + biases[2]).astype(BF)
        return carry

    lax.fori_loop(0, length // block, project, 0)
    lax.fori_loop(0, seq, finish, 0)


def attend_kernel(chips, place, q_ref, k_ref, v_ref, lse_ref, *refs):
    att_out, att_ref = refs[:chips], refs[chips]
    z = place[0]
    length, width = q_ref.shape
    rows = length // (chips * CORES)
    block = min(256, length)
    scaling = HD ** (-0.5)
    for at in range(0, length, block):
        here, upto = pl.ds(at, block), pl.ds(0, at + block)
        q, k, v = q_ref[here, :], k_ref[upto, :], v_ref[upto, :]
        att = jnp.zeros((block, width), F32)
        totals = []
        for head in range(width // HD):
            scores = causal(dot(head_lanes(q, head), k, 1, 1) * scaling, at)
            top = jnp.max(scores, axis=-1, keepdims=True)
            exponent = jnp.exp(scores - top)
            total = jnp.sum(exponent, axis=-1, keepdims=True)
            weights = (exponent * (1.0 / total)).astype(BF)
            att = att + head_lanes(dot(weights, v, 1, 0), head)
            totals.append(jnp.broadcast_to(top + jnp.log(total), (block, HD)))
        att_ref[here, :] = att.astype(BF)
        lse_ref[here, :] = jnp.concatenate(totals, axis=1)
    for k in range(chips):
        at = (z ^ k) * (CORES * rows)
        att_out[k][...] = att_ref[at_rows(at, CORES * rows, CORES * rows), :]


def project_kernel(chips, fsdp, place, *refs):
    refs = list(refs)
    att, refs = refs[:chips], refs[chips:]
    parts, refs = refs[:fsdp], refs[fsdp:]
    keep_ref, give_ref, w_far, w_rows, res, w_ref, w_sem = refs
    core, f = place[1], place[2]
    rows = keep_ref.shape[0]
    width = att[0].shape[1]
    piece = parts[0].shape[2]
    for j in range(fsdp):
        for k in range(chips):
            at = k * width + (f ^ j) * piece
            for t in range(parts[j].shape[1]):
                w_rows[at_rows(at, piece, piece), t * width : (t + 1) * width] = parts[j][
                    k, t
                ].astype(w_rows.dtype)
    w_ref[...] = w_rows[...].astype(BF)
    copy = pltpu.make_async_copy(w_ref, w_far, w_sem)
    copy.start()
    res[...] = dot(jnp.concatenate([a[...] for a in att], axis=1), w_ref[...], 1, 0)
    keep_ref[...] = res[at_rows(core * rows, rows, rows), :]
    give_ref[...] = res[at_rows((1 - core) * rows, rows, rows), :]
    copy.wait()


def norm2_kernel(x_ref, keep_ref, got_ref, gain, bias, z_ref, h2_ref):
    z = x_ref[...].astype(F32) + (keep_ref[...] + got_ref[...])
    z_ref[...] = z
    u2, _ = norm_parts(z)
    h2_ref[...] = (u2 * gain[...] + bias[...]).astype(BF)


def feed_kernel(seq, fsdp, hidden, unit_piece, place, *refs):
    refs = list(refs)
    h2, refs = refs[:fsdp], refs[fsdp:]
    g, refs = refs[:fsdp], refs[fsdp:]
    feed_ref, keep_ref, refs = refs[0], refs[1], refs[2:]
    sends, refs = refs[: fsdp - 1], refs[fsdp - 1 :]
    m_ref, dgu_ref, wd_far, h2_all, g_all, down_rows, feed_in, feed_sem, g_sem, wd_out, wd_sem, send_out, send_sem, gu_rows = refs[:14]
    w_gu = refs[14] if len(refs) > 14 else gu_rows
    f = place[2]
    rows, depth = keep_ref.shape
    copies = [
        pltpu.make_async_copy(feed_ref.at[s], feed_in.at[s], feed_sem.at[s]) for s in range(seq)
    ]
    for copy in copies:
        copy.start()
    g_copies = [
        pltpu.make_async_copy(g[j], g_all.at[pl.ds(j * rows, rows), :], g_sem.at[j])
        for j in range(fsdp)
    ]
    for copy in g_copies:
        copy.start()
    for j in range(fsdp):
        h2_all[j * rows : (j + 1) * rows, :] = h2[j][...]
    tiles = gu_rows.shape[1] // LANES
    piece = depth // (seq * fsdp)
    unit_pad = down_pad(unit_piece)
    first = fsdp * tiles * piece

    def gather(s, carry):
        pltpu.make_async_copy(feed_ref.at[s], feed_in.at[s], feed_sem.at[s]).wait()
        for j in range(fsdp):
            at = at_rows((s * fsdp + (f ^ j)) * piece, piece, piece)
            for t in range(tiles):
                tile = feed_in[s, pl.ds((j * tiles + t) * piece, piece), :]
                gu_rows[at, t * LANES : (t + 1) * LANES] = tile.astype(gu_rows.dtype)
        return carry

    def gather_down(s, at):
        for t in range(0, depth // LANES, 2):
            tile = feed_in[s, pl.ds(first + t * unit_pad, 2 * unit_pad), :].astype(F32)
            for q in range(2):
                cols = slice((t + q) * LANES, (t + q + 1) * LANES)
                down_rows[at, cols] = tile[q * unit_pad : q * unit_pad + unit_piece, :]

    lax.fori_loop(0, seq, gather, 0)
    wd_ref = wd_out
    if (2 * unit_piece) % 16 == 0:

        def gather_units(p, carry):
            at = at_rows(p * (2 * unit_piece), 2 * unit_piece, 16)
            for t in range(0, depth // LANES, 2):
                rows_of = pl.ds(first + t * unit_pad, 2 * unit_pad)
                pair = [feed_in[2 * p + n, rows_of, :].astype(F32) for n in range(2)]
                for q in range(2):
                    cut = slice(q * unit_pad, q * unit_pad + unit_piece)
                    both = jnp.concatenate([v[cut, :] for v in pair], axis=0)
                    wd_ref[at, (t + q) * LANES : (t + q + 1) * LANES] = both.astype(BF)
            return carry

        lax.fori_loop(0, seq // 2, gather_units, 0)
    else:
        for s in range(seq):
            gather_down(s, pl.ds(s * unit_piece, unit_piece))
        wd_ref[...] = down_rows[...].astype(BF)
    wd_copy = pltpu.make_async_copy(wd_ref, wd_far, wd_sem)
    wd_copy.start()
    if w_gu is not gu_rows:
        w_gu[...] = gu_rows[...].astype(BF)
    for copy in g_copies:
        copy.wait()
    if dgu_ref.shape[1] > 2 * hidden:
        dgu_ref[...] = jnp.zeros_like(dgu_ref)
    chunks = 2

    def work(i, carry):
        here = at_rows(i * (chunks * rows), chunks * rows, chunks * rows)
        gu = dot(h2_all[here, :], w_gu[...], 1, 0)
        gate, up = gu[:, :hidden], gu[:, hidden : 2 * hidden]
        dm = dot(g_all[here, :], wd_ref[...], 1, 1)
        sig = 1.0 / (1.0 + jnp.exp(-gate))
        silu = gate * sig
        m_ref[here, :] = (silu * up).astype(BF)
        dgu_ref[here, :hidden] = (dm * up * sig * (1.0 + gate * (1.0 - sig))).astype(BF)
        dgu_ref[here, hidden : 2 * hidden] = (dm * silu).astype(BF)
        dh2 = dot(dgu_ref[here, :], w_gu[...], 1, 1)
        for j in range(fsdp):

            @pl.when(i == j // chunks)
            def _():
                part = dh2[(j % chunks) * rows : (j % chunks + 1) * rows, :]
                if j == 0:
                    keep_ref[...] = part
                else:
                    send_out[j - 1] = part.astype(BF)
                    send_copy(j).start()

        return carry

    def send_copy(j):
        return pltpu.make_async_copy(send_out.at[j - 1], sends[j - 1], send_sem.at[j - 1])

    lax.fori_loop(0, fsdp // chunks, work, 0)
    wd_copy.wait()
    for j in range(1, fsdp):
        send_copy(j).wait()


def down_kernel(fsdp, m_ref, wd_ref, keep_ref, *sends):
    rows = keep_ref.shape[0]
    for j in range(fsdp):
        part = dot(m_ref[j * rows : (j + 1) * rows, :], wd_ref[...], 1, 0)
        if j == 0:
            keep_ref[...] = part
        else:
            sends[j - 1][...] = part.astype(BF)


def down_pad(unit_piece):
    return unit_piece if unit_piece % 8 == 0 else -(-unit_piece // 16) * 16


def feed_grad_kernel(seq, hidden, unit_piece, m_ref, dgu_ref, g_all, h2_all, out_ref, *refs):
    gu_out, down_out, down_acc, gu_sem, down_sem = refs
    depth = g_all.shape[1]
    tiles = dgu_ref.shape[1] // LANES
    block = depth // seq
    unit_pad = down_pad(unit_piece)
    pair = max(1, 256 // block)

    def gu_copy(i):
        return pltpu.make_async_copy(
            gu_out.at[pl.ds(i * pair, pair)],
            out_ref.at[pl.ds(i * pair, pair), pl.ds(0, tiles * block), :],
            gu_sem.at[i],
        )

    def down_copy(i):
        at = pl.multiple_of(i * 2 * unit_pad, 16)
        return pltpu.make_async_copy(
            down_out.at[:, pl.ds(at, 2 * unit_pad), :],
            out_ref.at[:, pl.ds(tiles * block + at, 2 * unit_pad), :],
            down_sem.at[i],
        )

    def gate_up(i, carry):
        cols = pl.ds(pl.multiple_of(i * (pair * block), pair * block), pair * block)
        grad = dot(h2_all[:, cols], dgu_ref[...], 0, 0).astype(BF)
        for s in range(pair):
            for t in range(tiles):
                gu_out[i * pair + s, t * block : (t + 1) * block, :] = grad[
                    s * block : (s + 1) * block, t * LANES : (t + 1) * LANES
                ]
        gu_copy(i).start()
        return carry

    lax.fori_loop(0, seq // pair, gate_up, 0, unroll=True)

    def down(i, carry):
        cols = pl.ds(pl.multiple_of(i * 256, 256), 256)
        down_acc[...] = dot(m_ref[...], g_all[:, cols], 0, 0)
        for s in range(seq):
            both = []
            for t in range(2):
                both.append(
                    down_acc[s * unit_piece : (s + 1) * unit_piece, t * LANES : (t + 1) * LANES]
                )
                if unit_pad > unit_piece:
                    both.append(jnp.zeros((unit_pad - unit_piece, LANES), F32))
            rows = at_rows(i * (2 * unit_pad), 2 * unit_pad, 16)
            down_out[s, rows, :] = jnp.concatenate(both, axis=0).astype(BF)
        down_copy(i).start()
        return carry

    lax.fori_loop(0, depth // 256, down, 0, unroll=True)

    def finish_gu(i, carry):
        gu_copy(i).wait()
        return carry

    def finish_down(i, carry):
        down_copy(i).wait()
        return carry

    lax.fori_loop(0, seq // pair, finish_gu, 0)
    lax.fori_loop(0, depth // 256, finish_down, 0)


def norm2_back_kernel(count, *refs):
    keep_ref, got, refs = refs[0], refs[1 : 1 + count], refs[1 + count :]
    z_ref, g_ref, gain, dz_ref, dzb_ref, sums_ref = refs
    dh2 = keep_ref[...]
    for ref in got:
        dh2 = dh2 + ref[...].astype(F32)
    u2, r2 = norm_parts(z_ref[...])
    dz = g_ref[...].astype(F32) + norm_back(dh2, gain[...], u2, r2)
    dz_ref[...] = dz
    dzb_ref[...] = dz.astype(BF)
    sums_ref[0:1, :] = jnp.sum(dh2 * u2, axis=0, keepdims=True)
    sums_ref[1:2, :] = jnp.sum(dh2, axis=0, keepdims=True)


def project_back_kernel(chips, place, mine_ref, other_ref, w_ref, dz2_ref, *outs):
    core = place[1]
    rows = mine_ref.shape[0]
    width = outs[0].shape[1]
    dz2_ref[at_rows(core * rows, rows, rows), :] = mine_ref[...]
    dz2_ref[at_rows((1 - core) * rows, rows, rows), :] = other_ref[...]
    do = dot(dz2_ref[...], w_ref[...], 1, 1)
    for k in range(chips):
        outs[k][...] = do[:, k * width : (k + 1) * width].astype(BF)


def project_grad_kernel(chips, fsdp, place, *refs):
    att, refs = refs[:chips], refs[chips:]
    dz2_ref, refs = refs[0], refs[1:]
    outs, acc = refs[:fsdp], refs[fsdp]
    f = place[2]
    width = att[0].shape[1]
    piece = width // fsdp
    acc[...] = dot(jnp.concatenate([a[...] for a in att], axis=1), dz2_ref[...], 0, 0)
    for j in range(fsdp):
        for k in range(chips):
            at = k * width + (f ^ j) * piece
            outs[j][k] = acc[at_rows(at, piece, piece), :].astype(BF)


def backward_kernel(chips, place, *refs):
    q_ref, k_ref, v_ref, lse_ref = refs[:4]
    do_in, refs = refs[4 : 4 + chips], refs[4 + chips :]
    cos_ref, sin_ref, dp_ref, do_ref, dk_acc, dv_acc = refs
    z = place[0]
    length, width = q_ref.shape
    rows = length // (chips * CORES)
    for k in range(chips):
        at = (z ^ k) * (CORES * rows)
        do_ref[at_rows(at, CORES * rows, CORES * rows), :] = do_in[k][...]
    heads = width // HD
    block = min(256, length)
    scaling = HD ** (-0.5)
    dk_acc[...] = jnp.zeros_like(dk_acc)
    dv_acc[...] = jnp.zeros_like(dv_acc)
    for at in range(0, length, block):
        here, upto = pl.ds(at, block), pl.ds(0, at + block)
        q, do, k, v = q_ref[here, :], do_ref[here, :], k_ref[upto, :], v_ref[upto, :]
        dq = jnp.zeros((block, width), F32)
        for head in range(heads):
            qh, doh = head_lanes(q, head), head_lanes(do, head)
            lse = lse_ref[here, head * HD : head * HD + 1]
            scores = causal(dot(qh, k, 1, 1) * scaling, at)
            probs = jnp.exp(scores - lse)
            dprobs = dot(doh, v, 1, 1)
            delta = jnp.sum(probs * dprobs, axis=-1, keepdims=True)
            dscores = (probs * (dprobs - delta)).astype(BF)
            dq = dq + head_lanes(dot(dscores, k, 1, 0), head)
            dk_acc[upto, :] += dot(dscores, qh, 0, 0)
            dv_acc[upto, :] += dot(probs.astype(BF), doh, 0, 0)
        dq = rotate(dq * scaling, cos_ref[here, :], -sin_ref[here, :])
        dp_ref[here, :width] = dq.astype(BF)

    def finish(i, carry):
        here = at_rows(i * block, block, block)
        dk = rotate(dk_acc[here, :] * scaling, cos_ref[here, :], -sin_ref[here, :])
        dp_ref[here, width : 2 * width] = dk.astype(BF)
        dp_ref[here, 2 * width :] = dv_acc[here, :].astype(BF)
        return carry

    lax.fori_loop(0, length // block, finish, 0, unroll=True)


def small_rows(depth, lanes):
    return -(-depth // lanes), -(-(4 * -(-depth // lanes) + 1) // 16) * 16


def tree_sum(values):
    values = list(values)
    while len(values) > 1:
        values = [values[i] + values[i + 1] for i in range(0, len(values), 2)]
    return values[0]


def qkv_grad_kernel(chips, fsdp, place, h1_ref, u1_ref, dp_ref, w_ref, sums2_ref, *refs):
    outs, (dh_far, acc, dh_ref, dh_sem) = refs[:fsdp], refs[fsdp:]
    f = place[2]
    seq = chips * CORES
    depth, lanes = acc.shape
    piece = depth // (seq * fsdp)
    length = dp_ref.shape[0]
    acc[...] = dot(h1_ref[...], dp_ref[...], 0, 0)
    block = min(256, length)

    def dh_copy(i):
        here = at_rows(i * block, block, block)
        return pltpu.make_async_copy(dh_ref.at[here, :], dh_far.at[here, :], dh_sem.at[i])

    def dh_wait(i, carry):
        dh_copy(i).wait()
        return carry

    def sums(i, carry):
        gains, shifts, biases = carry
        here = at_rows(i * block, block, block)
        dh1 = dot(dp_ref[here, :], w_ref[...], 1, 1)
        dh_ref[here, :] = dh1.astype(BF)
        dh_copy(i).start()
        gains = gains + jnp.sum(dh1 * u1_ref[here, :].astype(F32), axis=0, keepdims=True)
        shifts = shifts + jnp.sum(dh1, axis=0, keepdims=True)
        biases = biases + jnp.sum(dp_ref[here, :].astype(F32), axis=0, keepdims=True)
        return (gains, shifts, biases)

    zeros = jnp.zeros((1, depth), F32)
    gains, shifts, biases = lax.fori_loop(
        0, length // block, sums, (zeros, zeros, jnp.zeros((1, lanes), F32)), unroll=True
    )
    per, count = small_rows(depth, lanes)
    small = []
    for v in (gains, shifts, sums2_ref[0:1, :], sums2_ref[1:2, :]):
        if per * lanes > depth:
            v = jnp.concatenate([v, jnp.zeros((1, per * lanes - depth), F32)], axis=1)
        small += [v[:, r * lanes : (r + 1) * lanes] for r in range(per)]
    small.append(biases)
    if count > len(small):
        small.append(jnp.zeros((count - len(small), lanes), F32))
    small = jnp.concatenate(small, axis=0)
    for j in range(fsdp):
        for s in range(seq):
            at = (s * fsdp + (f ^ j)) * piece
            outs[j][s * piece : (s + 1) * piece, :] = acc[at_rows(at, piece, piece), :].astype(BF)
        outs[j][seq * piece :, :] = small.astype(BF)
    lax.fori_loop(0, length // block, dh_wait, 0)


def qkv_line_kernel(chips, fsdp, place, *refs):
    got, refs = refs[:fsdp], refs[fsdp:]
    outs, acc = refs[:chips], refs[chips]
    z, core = place[0], place[1]
    count = outs[0].shape[0]
    total_rows = got[0].shape[0]
    small = total_rows - acc.shape[0]
    piece = acc.shape[0] // (chips * CORES)
    total = tree_sum([ref[...].astype(F32) for ref in got])
    acc[...] = total[: total_rows - small, :]
    for k in range(chips):
        for c in range(CORES):
            at = ((z ^ k) * CORES + (core ^ c)) * piece
            outs[k][c * piece : (c + 1) * piece, :] = acc[at_rows(at, piece, piece), :].astype(BF)
        outs[k][CORES * piece : count, :] = total[total_rows - small :, :].astype(BF)


def qkv_core_kernel(chips, piece, per, *refs):
    got, (keep_ref, give_ref) = refs[:chips], refs[chips:]
    lanes = keep_ref.shape[1]
    small = [ref[CORES * piece :, :].astype(F32) for ref in got]
    total = tree_sum(small)
    bias = [v[4 * per : 4 * per + 1, :] for v in small]
    rest = keep_ref.shape[0] - chips * piece - 4 * per - chips
    pad = [jnp.zeros((rest, lanes), F32)] if rest > 0 else []
    tail = jnp.concatenate([total[: 4 * per, :]] + bias + pad, axis=0)
    for c, ref in ((0, keep_ref), (1, give_ref)):
        for k in range(chips):
            ref[k * piece : (k + 1) * piece, :] = got[k][c * piece : (c + 1) * piece, :]
        ref[chips * piece :, :] = tail.astype(BF)


def qkv_final_kernel(chips, piece, per, place, keep_ref, got_ref, grad_ref, small_ref, bias_ref, acc):
    z, core = place[0], place[1]
    seq = chips * CORES
    lanes = keep_ref.shape[1]
    width = lanes // 3
    depth = small_ref.shape[1]
    at = chips * piece
    tails = [ref[at:, :].astype(F32) for ref in (keep_ref, got_ref)]
    total = tails[0] + tails[1]
    for c, ref in ((0, keep_ref), (1, got_ref)):
        for k in range(chips):
            src = (z ^ k) * CORES + (core ^ c)
            rows = ref[k * piece : (k + 1) * piece, :].astype(F32)
            bias = tails[c][4 * per + k : 4 * per + k + 1, :]
            for part in range(3):
                acc[part * seq + src] = rows[:, part * width : (part + 1) * width]
                bias_ref[pl.ds(part * seq + src, 1), :] = bias[:, part * width : (part + 1) * width]
    for i in range(3 * seq):
        grad_ref[:, i * width : (i + 1) * width] = acc[i]
    for v in range(4):
        for r in range(per):
            upto = min(lanes, depth - r * lanes)
            small_ref[v : v + 1, r * lanes : r * lanes + upto] = total[v * per + r : v * per + r + 1, :upto]


def norm1_back_kernel(dh1_far, x_ref, gain, dz_ref, out_ref, dh1_ref, sem):
    copy = pltpu.make_async_copy(dh1_far, dh1_ref, sem)
    copy.start()
    u1, r1 = norm_parts(x_ref[...].astype(F32))
    copy.wait()
    out_ref[...] = dz_ref[...] + norm_back(dh1_ref[...].astype(F32), gain[...], u1, r1)


def on_device(
    seq,
    fsdp,
    tokens,
    ln1_gain,
    ln1_bias,
    qkv_weight,
    qkv_bias,
    out_weight,
    ln2_gain,
    ln2_bias,
    gate_up_weight,
    down_weight,
    out_grad,
):
    rows, depth = tokens.shape[1], tokens.shape[2]
    length = rows * seq
    chips = seq // CORES
    width = depth // seq
    piece = qkv_weight.shape[0]
    unit_piece = down_weight.shape[0]
    hidden = seq * unit_piece
    tiles = -(-2 * hidden // LANES)
    unit_pad = down_pad(unit_piece)
    me = lax.axis_index("seq")
    z, core, f = me // CORES, me % CORES, lax.axis_index("fsdp")
    place = jnp.stack([z, core, f]).astype(jnp.int32)
    steps, flips = range(1, chips), range(1, fsdp)
    by_place = jnp.arange(seq, dtype=jnp.int32) ^ me
    x_b = tokens.reshape(rows, depth)
    g_b = out_grad.reshape(rows, depth)
    row = lambda v: v.reshape(1, -1)

    tok_all = lax.all_gather(x_b, "seq", axis=0)

    w = qkv_weight.reshape(piece, 3, seq, width).transpose(2, 1, 0, 3)
    w = jnp.take(w, by_place, axis=0).reshape(chips, CORES * 3, piece, width)
    w = [w[0]] + [to_line(w[k], seq, k) for k in steps]
    cosines, sines = rotary_tables(length, width)
    give = after(jnp.stack([v[3:] for v in w]), cosines, sines)
    w = jnp.stack([jnp.stack([v[:3] for v in w]), to_core(give, seq)])
    w_parts = [w] + [to_fsdp(w, fsdp, j) for j in flips]

    gu = gate_up_weight.reshape(piece, 2, seq, fsdp, unit_piece).transpose(3, 0, 1, 2, 4)
    gu = gu.reshape(fsdp, piece, 2 * hidden)
    gu = jnp.pad(gu, ((0, 0), (0, 0), (0, tiles * LANES - 2 * hidden)))
    gu = gu.reshape(fsdp, piece, tiles, LANES).transpose(0, 2, 1, 3)
    pick = lambda v, j: lax.dynamic_index_in_dim(v, f ^ j, axis=0, keepdims=False)
    gu = after(gu, w)
    gu = [pick(gu, 0)] + [to_fsdp(pick(gu, j), fsdp, j) for j in flips]
    g_late = after(g_b, gu)
    g_parts = [g_b] + [to_fsdp(g_late, fsdp, j) for j in flips]

    o = after(out_weight, gu).reshape(piece, seq, width).transpose(1, 0, 2)
    o = [o] + [to_line(o, seq, k) for k in steps]
    down = jnp.pad(down_weight, ((0, unit_pad - unit_piece), (0, 0)))
    down = down.reshape(unit_pad, depth // LANES, LANES).transpose(1, 0, 2)
    feed = jnp.concatenate(
        [v.reshape(-1, LANES) for v in gu] + [down.reshape(-1, LANES)], axis=0
    )
    feed = lax.all_gather(feed, "seq", axis=0)

    outs = call(
        functools.partial(inputs_kernel, chips, fsdp),
        [shape((length, depth), BF)] * 2
        + [shape((length, width), BF)] * 3
        + [shape((depth, 3 * width), BF)],
        [
            pltpu.VMEM((depth, 3 * width), row_type(piece)),
            pltpu.VMEM((seq, rows, depth), BF),
            pltpu.SemaphoreType.DMA((seq,)),
            pltpu.VMEM((length, depth), BF),
            pltpu.VMEM((length, depth), BF),
            pltpu.SemaphoreType.DMA((seq,)),
            pltpu.SemaphoreType.DMA((seq,)),
        ],
        "attention_inputs",
        place,
        tok_all,
        *w_parts,
        row(ln1_gain),
        row(ln1_bias),
        qkv_bias.reshape(3 * seq, width),
        cosines,
        sines,
        far=(1,),
        far_out=(0, 1),
        vmem=16,
    )
    h1, u1, q, k_, v, w_qkv = outs
    o = jnp.stack(after(o, q))
    o_parts = [o] + [to_fsdp(o, fsdp, j) for j in flips]
    outs = call(
        functools.partial(attend_kernel, chips),
        [shape((length, width), F32)] + [shape((CORES * rows, width), BF)] * chips,
        [pltpu.VMEM((length, width), BF)],
        "attention_forward",
        place,
        after(q, g_parts),
        k_,
        v,
        flops=ATT,
        vmem=12,
    )
    lse, att = outs[0], outs[1:]
    att = [att[0]] + [to_line(att[k], seq, k) for k in steps]

    keep, give, w_out = call(
        functools.partial(project_kernel, chips, fsdp),
        [shape((rows, depth), F32)] * 2 + [shape((chips * width, depth), BF)],
        [
            pltpu.VMEM((chips * width, depth), row_type(piece)),
            pltpu.VMEM((CORES * rows, depth), F32),
            pltpu.VMEM((chips * width, depth), BF),
            pltpu.SemaphoreType.DMA(()),
        ],
        "out_projection",
        place,
        *att,
        *o_parts,
        flops=PROJECT,
        far_out=(2,),
        vmem=10,
    )
    z_res, h2 = call(
        norm2_kernel,
        [shape((rows, depth), F32), shape((rows, depth), BF)],
        [],
        "norm2",
        x_b,
        keep,
        to_core(give, seq),
        row(ln2_gain),
        row(ln2_bias),
        smem=False,
    )
    h2_parts = [h2] + [to_fsdp(h2, fsdp, j) for j in flips]

    tokens_here = fsdp * rows
    outs = call(
        functools.partial(feed_kernel, seq, fsdp, hidden, unit_piece),
        [shape((rows, depth), F32)]
        + [shape((rows, depth), BF)] * (fsdp - 1)
        + [
            shape((tokens_here, hidden), BF),
            shape((tokens_here, tiles * LANES), BF),
            shape((hidden, depth), BF),
            shape((tokens_here, depth), BF),
            shape((tokens_here, depth), BF),
        ],
        [
            pltpu.VMEM((hidden, depth), F32),
            pltpu.VMEM(feed.shape, BF),
            pltpu.SemaphoreType.DMA((seq,)),
            pltpu.SemaphoreType.DMA((fsdp,)),
            pltpu.VMEM((hidden, depth), BF),
            pltpu.SemaphoreType.DMA(()),
            pltpu.VMEM((fsdp - 1, rows, depth), BF),
            pltpu.SemaphoreType.DMA((fsdp - 1,)),
            pltpu.VMEM((depth, tiles * LANES), row_type(piece)),
        ]
        + ([] if row_type(piece) == BF else [pltpu.VMEM((depth, tiles * LANES), BF)]),
        "feed_forward",
        place,
        *h2_parts,
        *g_parts,
        feed,
        far=tuple(range(1 + fsdp, 2 + 2 * fsdp)),
        far_out=tuple(range(1, fsdp)) + (fsdp + 2,),
        vmem=20,
    )
    dh2_keep, dh2_send = outs[0], outs[1:fsdp]
    m, dgu, w_down, h2_all, g_all = outs[fsdp:]
    dh2_got = [to_fsdp(v, fsdp, j) for j, v in zip(flips, dh2_send)]

    block = depth // seq
    lines = tiles * block + (depth // LANES) * unit_pad
    feed_grad = call(
        functools.partial(feed_grad_kernel, seq, hidden, unit_piece),
        shape((seq, lines, LANES), BF),
        [
            pltpu.VMEM((seq, tiles * block, LANES), BF),
            pltpu.VMEM((seq, lines - tiles * block, LANES), BF),
            pltpu.VMEM((hidden, 256), F32),
            pltpu.SemaphoreType.DMA((seq // max(1, 256 // block),)),
            pltpu.SemaphoreType.DMA((depth // 256,)),
        ],
        "feed_gradient",
        m,
        dgu,
        g_all,
        h2_all,
        smem=False,
        flops=FILL_LONG,
        vmem=16,
        far_out=(0,),
    )
    feed_raw = lax.psum_scatter(feed_grad, "seq", scatter_dimension=0)
    feed_total = feed_raw.astype(F32)

    ffn = call(
        functools.partial(down_kernel, fsdp),
        [shape((rows, depth), F32)] + [shape((rows, depth), BF)] * (fsdp - 1),
        [],
        "down_projection",
        m,
        w_down,
        smem=False,
        flops=FILL_SHORT,
    )
    dh2_got = after(dh2_got, feed_grad, ffn[0])

    dz, dz_b, sums2 = call(
        functools.partial(norm2_back_kernel, fsdp - 1),
        [shape((rows, depth), F32), shape((rows, depth), BF), shape((2, depth), F32)],
        [],
        "norm2_back",
        dh2_keep,
        *dh2_got,
        z_res,
        g_b,
        row(ln2_gain),
        smem=False,
    )
    outs = call(
        functools.partial(project_back_kernel, chips),
        [shape((CORES * rows, depth), BF)] + [shape((CORES * rows, width), BF)] * chips,
        [],
        "out_projection_back",
        place,
        dz_b,
        to_core(dz_b, seq),
        w_out,
    )
    dz2, do = outs[0], outs[1:]
    do = [do[0]] + [to_line(do[k], seq, k) for k in steps]


    outs = call(
        functools.partial(project_grad_kernel, chips, fsdp),
        [shape((chips, piece, depth), BF)] * fsdp,
        [pltpu.VMEM((chips * width, depth), F32)],
        "out_projection_gradient",
        place,
        *att,
        dz2,
    )
    o_blocks = outs
    ffn_late = after(ffn, dz_b)
    ffn_got = [to_fsdp(ffn_late[j], fsdp, j) for j in flips]
    do = after(do, outs[0], ffn_got)

    dp = call(
        functools.partial(backward_kernel, chips),
        shape((length, 3 * width), BF),
        [
            pltpu.VMEM((length, width), BF),
            pltpu.VMEM((length, width), F32),
            pltpu.VMEM((length, width), F32),
        ],
        "attention_backward",
        place,
        q,
        k_,
        v,
        lse,
        *do,
        cosines,
        sines,
        flops=LONG,
        vmem=12,
    )
    lanes = 3 * width
    per, count = small_rows(depth, lanes)
    blocks = call(
        functools.partial(qkv_grad_kernel, chips, fsdp),
        [shape((seq * piece + count, lanes), BF)] * fsdp + [shape((length, depth), BF)],
        [
            pltpu.VMEM((depth, lanes), F32),
            pltpu.VMEM((length, depth), BF),
            pltpu.SemaphoreType.DMA((length // min(256, length),)),
        ],
        "qkv_gradient",
        place,
        h1,
        u1,
        dp,
        w_qkv,
        sums2,
        flops=FILL_LAST,
        vmem=12,
        far_out=(fsdp,),
    )
    blocks, dh1 = blocks[:fsdp], blocks[fsdp]
    line_in = [blocks[0]] + [to_fsdp(blocks[j], fsdp, j) for j in flips]
    blocks = call(
        functools.partial(qkv_line_kernel, chips, fsdp),
        [shape((CORES * piece + count, lanes), BF)] * chips,
        [pltpu.VMEM((seq * piece, lanes), F32)],
        "qkv_gradient_line",
        place,
        *line_in,
    )
    o_late = after(o_blocks, blocks[0])
    total = o_blocks[0].astype(F32)
    for j in flips:
        total = total + to_fsdp(o_late[j], fsdp, j).astype(F32)
    dh1 = gate(dh1, feed_raw, blocks[0])
    block_out = z_res + ffn[0]
    for v in ffn_got:
        block_out = block_out + v.astype(F32)
    block_out = block_out.astype(BF)
    dh1 = lax.psum_scatter(dh1, "seq", scatter_dimension=0, tiled=True)
    blocks = [blocks[0]] + [to_line(blocks[k], seq, k) for k in steps]
    tail = -(-(4 * per + chips) // 16) * 16
    keep, give = call(
        functools.partial(qkv_core_kernel, chips, piece, per),
        [shape((chips * piece + tail, lanes), BF)] * 2,
        [],
        "qkv_gradient_core",
        *blocks,
        smem=False,
    )
    qkv_grad, small, bias_grad = call(
        functools.partial(qkv_final_kernel, chips, piece, per),
        [
            shape((piece, 3 * depth), F32),
            shape((4, depth), F32),
            shape((3 * seq, width), F32),
        ],
        [pltpu.VMEM((3 * seq, piece, width), F32)],
        "qkv_gradient_final",
        place,
        keep,
        to_core(give, seq),
    )
    input_grad = call(
        norm1_back_kernel,
        shape((rows, depth), F32),
        [pltpu.VMEM((rows, depth), BF), pltpu.SemaphoreType.DMA(())],
        "norm1_back",
        dh1,
        x_b,
        row(ln1_gain),
        dz,
        smem=False,
        far=(0,),
    )

    down_grad = feed_total[tiles * block :].reshape(depth // LANES, unit_pad, LANES)
    down_grad = down_grad[:, :unit_piece].transpose(1, 0, 2).reshape(unit_piece, depth)
    gu = feed_total[: tiles * block].astype(BF).reshape(tiles, fsdp, piece, LANES)
    gu = gu.transpose(1, 2, 0, 3).reshape(fsdp, piece, tiles * LANES)[:, :, : 2 * hidden]
    gu_got = [pick(gu, 0)] + [to_fsdp(pick(gu, j), fsdp, j) for j in flips]
    gu = jnp.stack(gu_got)
    order = jnp.arange(fsdp, dtype=jnp.int32) ^ f
    gu = jnp.take(gu, order, axis=0)
    gu = gu.reshape(fsdp, piece, 2, seq, unit_piece).transpose(1, 2, 3, 0, 4)
    gu_grad = gu.reshape(piece, 2 * seq * fsdp * unit_piece).astype(F32)


    out_w_grad = total[0]
    for k in steps:
        out_w_grad = out_w_grad + to_line(total[k].astype(BF), seq, k).astype(F32)

    return (
        block_out.reshape(1, rows, depth),
        input_grad.reshape(1, rows, depth),
        small[0],
        small[1],
        qkv_grad,
        bias_grad.reshape(3 * depth),
        out_w_grad,
        small[2],
        small[3],
        gu_grad,
        down_grad,
    )


def solution(mesh):
    seq, fsdp = mesh.shape["seq"], mesh.shape["fsdp"]
    split = P(("seq", "fsdp"), None)
    toks = P("fsdp", "seq", None)

    def step(*args):
        return on_device(seq, fsdp, *args)

    return jax.shard_map(
        step,
        mesh=mesh,
        in_specs=(toks, P(), P(), split, P(), split, P(), P(), split, split, toks),
        out_specs=(toks, toks, P(), P(), split, P(), split, P(), P(), split, split),
        check_vma=False,
    )
```
